512 devices in a mesh: gx: 64 (over z, x, core), gz: 8 (over y).
Axes of the slice: x: 4, y: 8, z: 8, core: 2. Of those that a mesh axis runs over, the one named last changes fastest.
Arguments:
- right_side: float32 [3, 24, 512, 1024], P(None, 'gz', 'gx'), may hold values from -48 to 48
- density: float32 [24, 512, 1024], P('gz', 'gx'), may hold values from 0.5 to 4
Outputs:
- solution_field: float32 [3, 24, 512, 1024], P(None, 'gz', 'gx')
The draws below stay inside these ranges and needn't reach their ends.
All inputs are finite; a program needn't handle non-finite values.
Results may differ from the reference program's by a relative error of at most 0.0001.
Values sent between devices are 32-bit elements; how exact they have to be, the bound alone decides.
No kernel may reach another device: no remote copies, remote signals or barrier semaphores. Data moves between devices by JAX's collectives and lax.ppermute only.
A program may use at most 128 MiB of HBM per device.

```python
import math
import jax
import jax.numpy as jnp
from jax import lax

COMPONENTS = 3
NY = 1024
LEVELS = 4
PRE = 2
POST = 2
COARSE_SWEEPS = 3
CYCLES = 2
NX = 512
NZ = 24


def draw_right_side(key, part):
    first_key = jax.random.fold_in(key, 0)
    shape = (COMPONENTS, NZ, NX, NY)
    return jnp.clip(8.0 * jax.random.normal(first_key, shape, jnp.float32), -48.0, 48.0)


def level_of(own_key, shape, pieces, low, high):
    gain = 1.0
    for dim, parts in pieces:
        heights = jax.random.uniform(jax.random.fold_in(jax.random.fold_in(own_key, 6), dim), (parts,), jnp.float32, low / len(pieces), high / len(pieces))
        gain = gain * jnp.repeat(jnp.exp(heights), shape[dim] // parts).reshape((-1,) + (1,) * (len(shape) - 1 - dim))
    return gain


def setup_inputs(seed: int = 0) -> dict:
    arg_keys = jax.random.split(jax.random.key(seed), 3)
    right_side = draw_right_side(jax.random.fold_in(arg_keys[2], 71), 0)
    density = jnp.clip(jnp.exp(math.log(4.0) - 2.0794415 * jax.random.uniform(arg_keys[1], (NZ, NX, NY), jnp.float32) ** level_of(arg_keys[1], (NZ, NX, NY), ((0, 8), (1, 64)), -0.2, 0.2)), 0.5, 4.0)
    return dict(right_side=right_side, density=density)


relaxation = 0.8
plane_coupling = 16.0
depth_coupling = 1.0


def apply_operator(field, density_level, coupling):
    diagonal = density_level + 4.0 * coupling + 2.0 * depth_coupling
    padded = jnp.pad(field, ((0, 0), (1, 1), (1, 1)))
    lateral = padded[:, 2:, 1:-1] + padded[:, :-2, 1:-1] + padded[:, 1:-1, 2:] + padded[:, 1:-1, :-2]
    vertical = jnp.roll(field, 1, axis=0) + jnp.roll(field, -1, axis=0)
    return diagonal * field - coupling * lateral - depth_coupling * vertical, diagonal


def relax_once(field, source, density_level, coupling):
    image, diagonal = apply_operator(field, density_level, coupling)
    return field + relaxation * (source - image) / diagonal


def restrict(values):
    rows_z, rows_x, rows_y = values.shape
    return values.reshape(rows_z, rows_x // 2, 2, rows_y // 2, 2).mean(axis=(2, 4))


def prolong(values):
    return jnp.repeat(jnp.repeat(values, 2, axis=1), 2, axis=2)


def vcycle(field, source, density_levels, level_index):
    coupling = plane_coupling / 4.0 ** level_index
    density_level = density_levels[level_index]
    if level_index == LEVELS - 1:
        for sweep_index in range(COARSE_SWEEPS):
            field = relax_once(field, source, density_level, coupling)
        return field
    for sweep_index in range(PRE):
        field = relax_once(field, source, density_level, coupling)
    image, diagonal = apply_operator(field, density_level, coupling)
    coarse_source = restrict(source - image)
    correction = vcycle(jnp.zeros_like(coarse_source), coarse_source, density_levels, level_index + 1)
    field = field + prolong(correction)
    for sweep_index in range(POST):
        field = relax_once(field, source, density_level, coupling)
    return field


def reference(right_side, density):
    density_levels = [density]
    for level_index in range(1, LEVELS):
        density_levels.append(restrict(density_levels[-1]))

    def solve_component(source):
        field = jnp.zeros_like(source)
        for cycle_index in range(CYCLES):
            field = vcycle(field, source, density_levels, 0)
        return field

    return lax.map(solve_component, right_side)
```

```python
import jax
import jax.numpy as jnp
from jax import lax
from jax.experimental import pallas as pl
from jax.experimental.pallas import tpu as pltpu
from jax.sharding import PartitionSpec as P

relaxation = 0.8
plane_coupling = 16.0
depth_coupling = 1.0
C = 3
NZ = 24
HALO = 6
LANES = 128
PARAMS = pltpu.CompilerParams(vmem_limit_bytes=28 << 20)


def coupling_of(level):
    return plane_coupling / 4.0**level


def base_of(level):
    return 4.0 * coupling_of(level) + 2.0 * depth_coupling


class Row:
    def __init__(self, base, shift):
        self.base, self.shift = base, shift

    def __add__(self, n):
        return Row(self.base, self.shift + n)

    def __sub__(self, n):
        return self + -n

    def double(self):
        return Row(2 * self.base, 2 * self.shift)


def index(field, r):
    return r.base + (r.shift - field[1]) if isinstance(r, Row) else r - field[1]


def row(field, c, r):
    return field[0][c, index(field, r)]


def shared(field, r):
    return field[0][index(field, r)]


def neighbours(field, c, r, level):
    mid = row(field, c, r)
    width = mid.shape[1]
    lateral = row(field, c, r - 1) + row(field, c, r + 1) + pltpu.roll(mid, 1, 1) + pltpu.roll(mid, width - 1, 1)
    vertical = pltpu.roll(mid, 1, 0) + pltpu.roll(mid, NZ - 1, 0)
    return mid, coupling_of(level) * lateral + depth_coupling * vertical


def each_row(low, high, body):
    def step(n, carry):
        body(Row(n, low))
        return carry

    lax.fori_loop(0, high - low, step, 0)


def sweep(target, field, source, factor, level, low, high):
    def body(r):
        f = shared(factor, r)
        for c in range(C):
            mid, around = neighbours(field, c, r, level)
            target[0][c, index(target, r)] = (1.0 - relaxation) * mid + f * (row(source, c, r) + around)

    each_row(low, high, body)


def first_sweep(target, source, factor, low, high):
    def body(r):
        f = shared(factor, r)
        for c in range(C):
            target[0][c, index(target, r)] = f * row(source, c, r)

    each_row(low, high, body)


def lane_index():
    return lax.broadcasted_iota(jnp.int32, (NZ, LANES), 1)


def take(values, index):
    return jnp.take_along_axis(values, index, axis=1, mode="promise_in_bounds")


def pair_sum(values, period):
    lane = lane_index()
    if values.shape[1] == 2 * LANES:
        even = (2 * lane) % LANES
        halves = [take(h + pltpu.roll(h, LANES - 1, 1), even) for h in (values[:, :LANES], values[:, LANES:])]
        return jnp.where(lane < LANES // 2, halves[0], halves[1])
    return take(values + pltpu.roll(values, LANES - 1, 1), (2 * lane) % period)


def spread(values, period):
    lane = lane_index()
    if period == 2 * LANES:
        return jnp.concatenate([take(values, lane // 2), take(values, LANES // 2 + lane // 2)], axis=1)
    return take(values, (lane % period) // 2)


def coarse_source(target, field, source, density, level, period, low, high):
    def body(q):
        for c in range(C):
            total = None
            for r in (q.double(), q.double() + 1):
                mid, around = neighbours(field, c, r, level)
                residual = row(source, c, r) + around - (shared(density, r) + base_of(level)) * mid
                total = residual if total is None else total + residual
            target[0][c, index(target, q)] = 0.25 * pair_sum(total, period)

    each_row(low, high, body)


def coarse_density(target, density, period, low, high):
    def body(q):
        total = shared(density, q.double()) + shared(density, q.double() + 1)
        target[0][index(target, q)] = 0.25 * pair_sum(total, period)

    each_row(low, high, body)


def factors(target, density, level, period, rows, position, low, high):
    i, j, count_x, count_y = position[0], position[1], position[2], position[3]
    width = target[0].shape[-1]
    lane = lax.broadcasted_iota(jnp.int32, (NZ, width), 1) % period
    inside_y = ((lane < 3 * period // 4) | (j > 0)) & ((lane < period // 2) | (lane >= 3 * period // 4) | (j < count_y - 1))

    def body(r):
        at = i * rows + r.base
        inside = inside_y & ((at >= -r.shift) & (at < count_x * rows - r.shift))
        target[0][index(target, r)] = jnp.where(inside, relaxation / (shared(density, r) + base_of(level)), 0.0)

    each_row(low, high, body)


def level_one_down(g1, v1, scratch, d1, f1, packed):
    first_sweep(scratch, g1, f1, -2, 6)
    sweep(v1, scratch, g1, f1, 1, -1, 5)
    lane = lane_index()
    for c in range(C + 1):
        pair = []
        for q in (0, 1):
            total = None
            for r in (2 * q, 2 * q + 1):
                if c == C:
                    part = shared(d1, r)
                else:
                    mid, around = neighbours(v1, c, r, 1)
                    part = row(g1, c, r) + around - (shared(d1, r) + base_of(1)) * mid
                total = part if total is None else total + part
            pair.append(0.25 * pair_sum(total, LANES))
        packed[c] = jnp.where(lane < LANES // 2, pair[0], pair[1])


def pack_kernel(source, density, out):
    blocks = out.shape[0]
    for ref, at, n in ((source, 0, source.shape[0]), (density, source.shape[0], density.shape[0])):
        for m in range(n):
            for b in range(blocks):
                out[b, at + m, :, :LANES] = ref[m, :, b * LANES : (b + 1) * LANES]
                zero = jnp.zeros((ref.shape[1], LANES), jnp.float32)
                after = ref[m, :, (b + 1) * LANES : (b + 2) * LANES] if b + 1 < blocks else zero
                before = ref[m, :, (b - 1) * LANES : b * LANES] if b else zero
                lane = lax.broadcasted_iota(jnp.int32, zero.shape, 1)
                out[b, at + m, :, LANES:] = jnp.where(lane < LANES // 2, after, before)


def unpack_kernel(taken, own, low, high, scratch):
    blocks, _, rows, _ = taken.shape
    depth = NZ // blocks
    for c in range(C + 1):
        for b in range(blocks):
            for z in range(depth):
                at = (b * depth + z) * rows
                for h in range(2):
                    scratch[c, h, at : at + rows] = taken[b, c * depth + z, :, h * LANES : (h + 1) * LANES]
    for c in range(C + 1):
        for r in range(rows):
            for h in range(2):
                part = scratch[c, h, pl.ds(r, NZ, stride=rows), :]
                lanes = slice(h * LANES, (h + 1) * LANES)
                own[c, r, :, lanes] = part
                if r < HALO:
                    low[c, r, :, lanes] = part
                if r >= rows - HALO:
                    high[c, r - rows + HALO, :, lanes] = part


def first_down_kernel(position, own, left, right, g0, d0, f0, v0, g1, d1, f1, v1, packed, field, field1):
    rows = own.shape[1]
    for c in range(C + 1):
        for piece, at, n in ((left, 0, HALO), (own, HALO, rows), (right, HALO + rows, HALO)):
            for r in range(n):
                if c < C:
                    g0[c, at + r] = piece[c, r]
                else:
                    d0[at + r] = piece[c, r]
    g, d, f, a, b = (g0, -HALO), (d0, -HALO), (f0, -HALO), (field, -HALO), (v0, -HALO)
    factors(f, d, 0, 2 * LANES, rows, position, -HALO, rows + HALO)
    coarse_density((d1, -3), d, 2 * LANES, -3, rows // 2 + 3)
    factors((f1, -3), (d1, -3), 1, LANES, rows // 2, position, -3, rows // 2 + 3)
    first_sweep(a, g, f, -6, rows + 6)
    sweep(b, a, g, f, 0, -5, rows + 5)
    coarse_source((g1, -2), b, g, d, 0, 2 * LANES, -2, rows // 2 + 2)
    level_one_down((g1, -2), (v1, -2), (field1, -2), (d1, -3), (f1, -3), packed)


def side_kernel(own, left, right, to_left, to_right):
    rows, halo = own.shape[1], left.shape[1]
    half = (rows + 2 * halo) // 2
    lane = lane_index()

    def at(c, r):
        if r < halo:
            return left[c, r]
        return own[c, r - halo] if r < halo + rows else right[c, r - halo - rows]

    for c in range(C):
        for r in range(half):
            one, two = at(c, r), pltpu.roll(at(c, r + half), LANES // 2, 1)
            to_left[c, r] = jnp.where(lane < LANES // 2, one, two)
            to_right[c, r] = jnp.where(lane < LANES // 2, two, one)


def second_down_kernel(own, left, right, after, before, g0, d0, f0, d1, f1, v0, g1, v1, packed, wide, field, field1):
    rows, halo = own.shape[1], left.shape[1]
    half = (rows + 2 * halo) // 2
    lane = lane_index()
    for c in range(C):
        for piece, at, n in ((left, 0, halo), (own, halo, rows), (right, halo + rows, halo)):
            for r in range(n):
                wide[c, at + r, :, :LANES] = piece[c, r]
        for r in range(half):
            wide[c, r, :, LANES:] = jnp.where(lane < LANES // 2, after[c, r], before[c, r])
            two = jnp.where(lane < LANES // 2, before[c, r], after[c, r])
            wide[c, r + half, :, LANES:] = pltpu.roll(two, LANES // 2, 1)
    g, d, f, a, b = (g0, -HALO), (d0, -HALO), (f0, -HALO), (field, -HALO), (v0, -HALO)
    sweep(a, (wide, -halo), g, f, 0, -6, rows + 6)
    sweep(b, a, g, f, 0, -5, rows + 5)
    coarse_source((g1, -2), b, g, d, 0, 2 * LANES, -2, rows // 2 + 2)
    level_one_down((g1, -2), (v1, -2), (field1, -2), (d1, -3), (f1, -3), packed)


def coarse_kernel(position, blocks, v1, out, g2, d2, f2, g3, d3, f3, a, b, a3, b3):
    lane = lane_index()
    count = blocks.shape[0]
    reach = count // 2 * 2
    for n in range(count):
        for c in range(C + 1):
            both = blocks[n, c]
            other = pltpu.roll(both, LANES // 2, 1)
            for q, value in ((0, jnp.where(lane < LANES // 2, both, other)), (1, jnp.where(lane < LANES // 2, other, both))):
                if c < C:
                    g2[c, 2 * n + q] = value
                else:
                    d2[2 * n + q] = value
    g, d, f, u, w = (g2, -reach), (d2, -reach), (f2, -reach), (a, -reach), (b, -reach)
    h, e, k, s, t = (g3, -reach // 2), (d3, -reach // 2), (f3, -reach // 2), (a3, -reach // 2), (b3, -reach // 2)
    factors(f, d, 2, LANES // 2, 2, position, -8, 10)
    coarse_density(e, d, LANES // 2, -3, 4)
    factors(k, e, 3, LANES // 4, 1, position, -3, 4)
    first_sweep(u, g, f, -8, 10)
    sweep(w, u, g, f, 2, -7, 9)
    coarse_source(h, w, g, d, 2, LANES // 2, -3, 4)
    first_sweep(s, h, k, -3, 4)
    sweep(t, s, h, k, 3, -2, 3)
    sweep(s, t, h, k, 3, -1, 2)

    def correct(q):
        for c in range(C):
            fine = spread(row(s, c, q), LANES // 2)
            for r in (q.double(), q.double() + 1):
                b[c, index(w, r)] = row(w, c, r) + fine

    each_row(-1, 2, correct)
    sweep(u, w, g, f, 2, -1, 3)
    sweep(w, u, g, f, 2, 0, 2)
    for c in range(C):
        for q in (0, 1):
            fine = spread(row(w, c, q), LANES)
            for r in (2 * q, 2 * q + 1):
                out[c, r] = v1[c, r + 2] + fine


def climb(own, left, right, g0, f0, v0, g1, f1, wide, u, w, field, emit):
    rows1, halo = own.shape[1], left.shape[1]
    for c in range(C):
        for piece, at, n in ((left, 0, halo), (own, halo, rows1), (right, halo + rows1, halo)):
            for r in range(n):
                wide[c, at + r] = piece[c, r]
    sweep((u, -3), (wide, -halo), (g1, -2), (f1, -3), 1, -2, rows1 + 2)
    sweep((w, -3), (u, -3), (g1, -2), (f1, -3), 1, -1, rows1 + 1)

    def correct(q):
        for c in range(C):
            fine = spread(row((w, -3), c, q), 2 * LANES)
            for r in (q.double(), q.double() + 1):
                field[c, index((field, -HALO), r)] = row((v0, -HALO), c, r) + fine

    each_row(-1, rows1 + 1, correct)
    rows = 2 * rows1
    sweep((emit, -HALO), (field, -HALO), (g0, -HALO), (f0, -HALO), 0, -1, rows + 1)
    sweep((field, -HALO), (emit, -HALO), (g0, -HALO), (f0, -HALO), 0, 0, rows)


def first_up_kernel(own, left, right, g0, f0, v0, g1, f1, out, low, high, wide, u, w, field, other):
    climb(own, left, right, g0, f0, v0, g1, f1, wide, u, w, field, other)
    rows, halo = out.shape[1], low.shape[1]
    for c in range(C):
        for r in range(rows):
            value = field[c, r + HALO, :, :LANES]
            out[c, r] = value
            if r < halo:
                low[c, r] = value
            if r >= rows - halo:
                high[c, r - rows + halo] = value


def last_up_kernel(own, left, right, g0, f0, v0, g1, f1, out, wide, u, w, field, other, scratch):
    climb(own, left, right, g0, f0, v0, g1, f1, wide, u, w, field, other)
    blocks, _, rows, _ = out.shape
    depth = NZ // blocks
    for c in range(C):
        for r in range(rows):
            scratch[c, pl.ds(r, NZ, stride=rows), :] = field[c, r + HALO, :, :LANES]
    for c in range(C):
        for z in range(NZ):
            out[z // depth, c * depth + z % depth] = scratch[c, z * rows : (z + 1) * rows]


def join_kernel(taken, out):
    for b in range(taken.shape[0]):
        out[:, :, b * LANES : (b + 1) * LANES] = taken[b]


def call(kernel, outs, scratch, *args, scalars=0):
    shape = lambda s: jax.ShapeDtypeStruct(s, jnp.float32)
    specs = [pl.BlockSpec(memory_space=pltpu.SMEM)] * scalars + [pl.BlockSpec(memory_space=pltpu.VMEM)] * (len(args) - scalars)
    out = pl.pallas_call(
        kernel,
        out_shape=[shape(s) for s in outs],
        in_specs=specs,
        out_specs=[pl.BlockSpec(memory_space=pltpu.VMEM)] * len(outs),
        scratch_shapes=[pltpu.VMEM(s, jnp.float32) for s in scratch],
        compiler_params=PARAMS,
        name=kernel.__name__,
    )(*args)
    return out


def onward(values, axis, distance, closed=False):
    count = lax.axis_size(axis)
    pairs = [(i, (i + distance) % count) for i in range(count) if closed or 0 <= i + distance < count]
    return lax.ppermute(values, axis, pairs)


def shards(right_side, density):
    blocks = lax.axis_size("gz")
    depth, rows, columns = density.shape
    position = jnp.stack([lax.axis_index("gx"), lax.axis_index("gz"), lax.axis_size("gx"), blocks]).astype(jnp.int32)
    W, R0, R1 = 2 * LANES, rows + 2 * HALO, rows // 2

    (sent,) = call(pack_kernel, [(blocks, (C + 1) * depth, rows, W)], [], right_side.reshape(C * depth, rows, columns), density)
    taken = lax.all_to_all(sent, "gz", 0, 0)
    own, low, high = call(
        unpack_kernel,
        [(C + 1, rows, NZ, W), (C + 1, HALO, NZ, W), (C + 1, HALO, NZ, W)],
        [(C + 1, 2, NZ * rows, LANES)],
        taken,
    )
    fine, mid = (C, R0, NZ, W), (C, R1 + 4, NZ, LANES)
    g0, d0, f0, v0, g1, d1, f1, v1, packed = call(
        first_down_kernel,
        [fine, fine[1:], fine[1:], fine, mid, (R1 + 6, NZ, LANES), (R1 + 6, NZ, LANES), mid, (C + 1, NZ, LANES)],
        [fine, mid],
        position,
        own,
        onward(high, "gx", 1),
        onward(low, "gx", -1),
        scalars=1,
    )

    def coarse(packed, v1):
        near = jnp.stack([onward(packed, "gx", 1, True), packed, onward(packed, "gx", -1, True)])
        nine = jnp.concatenate([onward(near, "gx", 3, True), near, onward(near, "gx", -3, True)])
        two, three = (C, 18, NZ, LANES), (C, 9, NZ, LANES)
        (out,) = call(
            coarse_kernel,
            [(C, R1, NZ, LANES)],
            [two, two[1:], two[1:], three, three[1:], three[1:], two, two, three, three],
            position,
            nine,
            v1,
            scalars=1,
        )
        return out, onward(out[:, 1:], "gx", 1), onward(out[:, :-1], "gx", -1)

    middle = (C, R1 + 6, NZ, LANES)
    reach = HALO + 1
    field, low, high = call(
        first_up_kernel,
        [(C, rows, NZ, LANES), (C, reach, NZ, LANES), (C, reach, NZ, LANES)],
        [middle, middle, middle, fine, fine],
        *coarse(packed, v1),
        g0,
        f0,
        v0,
        g1,
        f1,
    )
    left, right = onward(high, "gx", 1), onward(low, "gx", -1)
    half = (rows + 2 * reach) // 2
    to_left, to_right = call(side_kernel, [(C, half, NZ, LANES)] * 2, [], field, left, right)
    v0, g1, v1, packed = call(
        second_down_kernel,
        [fine, mid, mid, (C + 1, NZ, LANES)],
        [(C, rows + 2 * reach, NZ, W), fine, mid],
        field,
        left,
        right,
        onward(to_left, "gz", -1),
        onward(to_right, "gz", 1),
        g0,
        d0,
        f0,
        d1,
        f1,
    )
    (sent,) = call(
        last_up_kernel,
        [(blocks, C * depth, rows, LANES)],
        [middle, middle, middle, fine, fine, (C, NZ * rows, LANES)],
        *coarse(packed, v1),
        g0,
        f0,
        v0,
        g1,
        f1,
    )
    (out,) = call(join_kernel, [(C * depth, rows, columns)], [], lax.all_to_all(sent, "gz", 0, 0))
    return out.reshape(right_side.shape)


def solution(mesh):
    return jax.shard_map(
        shards,
        mesh=mesh,
        in_specs=(P(None, "gz", "gx", None), P("gz", "gx", None)),
        out_specs=P(None, "gz", "gx", None),
        check_vma=False,
    )
```

```python
import jax
import jax.numpy as jnp
from jax import lax
from jax.experimental import pallas as pl
from jax.experimental.pallas import tpu as pltpu
from jax.sharding import PartitionSpec as P

relaxation = 0.8
plane_coupling = 16.0
depth_coupling = 1.0
C = 3
NZ = 24
HALO = 6
LANES = 128
UNROLL = (2, 4, 8, 8)
PARAMS = pltpu.CompilerParams(vmem_limit_bytes=28 << 20)


def coupling_of(level):
    return plane_coupling / 4.0**level


def base_of(level):
    return 4.0 * coupling_of(level) + 2.0 * depth_coupling


class Row:
    def __init__(self, base, shift):
        self.base, self.shift = base, shift

    def __add__(self, n):
        return Row(self.base, self.shift + n)

    def __sub__(self, n):
        return self + -n

    def double(self):
        return Row(2 * self.base, 2 * self.shift)


def index(field, r):
    return r.base + (r.shift - field[1]) if isinstance(r, Row) else r - field[1]


def row(field, c, r):
    return field[0][c, index(field, r)]


def shared(field, r):
    return field[0][index(field, r)]


def neighbours(field, c, r, level):
    mid = row(field, c, r)
    width = mid.shape[1]
    lateral = row(field, c, r - 1) + row(field, c, r + 1) + pltpu.roll(mid, 1, 1) + pltpu.roll(mid, width - 1, 1)
    vertical = pltpu.roll(mid, 1, 0) + pltpu.roll(mid, NZ - 1, 0)
    return mid, coupling_of(level) * lateral + depth_coupling * vertical


def each_row(low, high, body, unroll):
    steps = (high - low) // unroll

    def step(n, carry):
        for k in range(unroll):
            body(Row(unroll * n, low + k))
        return carry

    if steps > 1:
        lax.fori_loop(0, steps, step, 0)
        low += steps * unroll
    for r in range(low, high):
        body(Row(0, r))


def sweep(target, field, source, factor, level, low, high):
    def body(r):
        f = shared(factor, r)
        for c in range(C):
            mid, around = neighbours(field, c, r, level)
            target[0][c, index(target, r)] = (1.0 - relaxation) * mid + f * (row(source, c, r) + around)

    each_row(low, high, body, UNROLL[level])


def lane_index():
    return lax.broadcasted_iota(jnp.int32, (NZ, LANES), 1)


def take(values, index):
    return jnp.take_along_axis(values, index, axis=1, mode="promise_in_bounds")


def pair_sum(values, period):
    lane = lane_index()
    if values.shape[1] == 2 * LANES:
        even = (2 * lane) % LANES
        halves = [take(h + pltpu.roll(h, LANES - 1, 1), even) for h in (values[:, :LANES], values[:, LANES:])]
        return jnp.where(lane < LANES // 2, halves[0], halves[1])
    return take(values + pltpu.roll(values, LANES - 1, 1), (2 * lane) % period)


def spread(values, period):
    lane = lane_index()
    if period == 2 * LANES:
        return jnp.concatenate([take(values, lane // 2), take(values, LANES // 2 + lane // 2)], axis=1)
    return take(values, (lane % period) // 2)


def coarse_source(target, field, source, density, level, period, low, high):
    def body(q):
        for c in range(C):
            total = None
            for r in (q.double(), q.double() + 1):
                mid, around = neighbours(field, c, r, level)
                residual = row(source, c, r) + around - (shared(density, r) + base_of(level)) * mid
                total = residual if total is None else total + residual
            target[0][c, index(target, q)] = 0.25 * pair_sum(total, period)

    each_row(low, high, body, max(1, UNROLL[level] // 2))


def from_zero(target, source, density, factor, level, period, rows, position, low, high, finer=None, reach=0):
    i, j, count_x, count_y = position[0], position[1], position[2], position[3]
    width = factor[0].shape[-1]
    lane = lax.broadcasted_iota(jnp.int32, (NZ, width), 1) % period
    inside_y = ((lane < 3 * period // 4) | (j > 0)) & ((lane < period // 2) | (lane >= 3 * period // 4) | (j < count_y - 1))

    def body(r):
        if finer is None:
            own = shared(density, r)
        else:
            own = 0.25 * pair_sum(shared(finer, r.double()) + shared(finer, r.double() + 1), 2 * period)
            density[0][index(density, r)] = own
        at = i * rows + r.base
        inside = inside_y & ((at >= -r.shift) & (at < count_x * rows - r.shift))
        f = jnp.where(inside, relaxation / (own + base_of(level)), 0.0)
        factor[0][index(factor, r)] = f
        return f

    def whole(r):
        f = body(r)
        for c in range(C):
            target[0][c, index(target, r)] = f * row(source, c, r)

    for r in [*range(low - reach, low), *range(high, high + reach)]:
        body(Row(0, r))
    each_row(low, high, whole, UNROLL[level])


def first_sweep(target, source, factor, level, low, high):
    def body(r):
        f = shared(factor, r)
        for c in range(C):
            target[0][c, index(target, r)] = f * row(source, c, r)

    each_row(low, high, body, UNROLL[level])


def level_one_down(g1, v1, scratch, d1, f1, packed):
    sweep(v1, scratch, g1, f1, 1, -1, 5)
    lane = lane_index()
    for c in range(C + 1):
        pair = []
        for q in (0, 1):
            total = None
            for r in (2 * q, 2 * q + 1):
                if c == C:
                    part = shared(d1, r)
                else:
                    mid, around = neighbours(v1, c, r, 1)
                    part = row(g1, c, r) + around - (shared(d1, r) + base_of(1)) * mid
                total = part if total is None else total + part
            pair.append(0.25 * pair_sum(total, LANES))
        packed[c] = jnp.where(lane < LANES // 2, pair[0], pair[1])


def pack_kernel(source, density, out):
    blocks = out.shape[0]
    for ref, at, n in ((source, 0, source.shape[0]), (density, source.shape[0], density.shape[0])):
        for m in range(n):
            for b in range(blocks):
                out[b, at + m, :, :LANES] = ref[m, :, b * LANES : (b + 1) * LANES]
                zero = jnp.zeros((ref.shape[1], LANES), jnp.float32)
                after = ref[m, :, (b + 1) * LANES : (b + 2) * LANES] if b + 1 < blocks else zero
                before = ref[m, :, (b - 1) * LANES : b * LANES] if b else zero
                lane = lax.broadcasted_iota(jnp.int32, zero.shape, 1)
                out[b, at + m, :, LANES:] = jnp.where(lane < LANES // 2, after, before)


def unpack_kernel(taken, own, low, high, scratch):
    blocks, _, rows, _ = taken.shape
    depth = NZ // blocks
    for c in range(C + 1):
        for b in range(blocks):
            for z in range(depth):
                at = (b * depth + z) * rows
                for h in range(2):
                    scratch[c, h, at : at + rows] = taken[b, c * depth + z, :, h * LANES : (h + 1) * LANES]
    for c in range(C + 1):
        for r in range(rows):
            for h in range(2):
                part = scratch[c, h, pl.ds(r, NZ, stride=rows), :]
                lanes = slice(h * LANES, (h + 1) * LANES)
                own[c, r, :, lanes] = part
                if r < HALO:
                    low[c, r, :, lanes] = part
                if r >= rows - HALO:
                    high[c, r - rows + HALO, :, lanes] = part


def first_down_kernel(position, own, left, right, g0, d0, f0, v0, g1, d1, f1, v1, packed, field, field1):
    rows = own.shape[1]
    for c in range(C + 1):
        for piece, at, n in ((left, 0, HALO), (own, HALO, rows), (right, HALO + rows, HALO)):
            for r in range(n):
                if c < C:
                    g0[c, at + r] = piece[c, r]
                else:
                    d0[at + r] = piece[c, r]
    g, d, f, a, b = (g0, -HALO), (d0, -HALO), (f0, -HALO), (field, -HALO), (v0, -HALO)
    from_zero(a, g, d, f, 0, 2 * LANES, rows, position, -HALO, rows + HALO)
    sweep(b, a, g, f, 0, -5, rows + 5)
    coarse_source((g1, -2), b, g, d, 0, 2 * LANES, -2, rows // 2 + 2)
    from_zero((field1, -2), (g1, -2), (d1, -3), (f1, -3), 1, LANES, rows // 2, position, -2, rows // 2 + 2, d, 1)
    level_one_down((g1, -2), (v1, -2), (field1, -2), (d1, -3), (f1, -3), packed)


def side_kernel(own, left, right, to_left, to_right):
    rows, halo = own.shape[1], left.shape[1]
    half = (rows + 2 * halo) // 2
    lane = lane_index()

    def at(c, r):
        if r < halo:
            return left[c, r]
        return own[c, r - halo] if r < halo + rows else right[c, r - halo - rows]

    for c in range(C):
        for r in range(half):
            one, two = at(c, r), pltpu.roll(at(c, r + half), LANES // 2, 1)
            to_left[c, r] = jnp.where(lane < LANES // 2, one, two)
            to_right[c, r] = jnp.where(lane < LANES // 2, two, one)


def second_down_kernel(own, left, right, after, before, g0, d0, f0, d1, f1, v0, g1, v1, packed, wide, field, field1):
    rows, halo = own.shape[1], left.shape[1]
    half = (rows + 2 * halo) // 2
    lane = lane_index()
    for c in range(C):
        for piece, at, n in ((left, 0, halo), (own, halo, rows), (right, halo + rows, halo)):
            for r in range(n):
                wide[c, at + r, :, :LANES] = piece[c, r]
        for r in range(half):
            wide[c, r, :, LANES:] = jnp.where(lane < LANES // 2, after[c, r], before[c, r])
            two = jnp.where(lane < LANES // 2, before[c, r], after[c, r])
            wide[c, r + half, :, LANES:] = pltpu.roll(two, LANES // 2, 1)
    g, d, f, a, b = (g0, -HALO), (d0, -HALO), (f0, -HALO), (field, -HALO), (v0, -HALO)
    sweep(a, (wide, -halo), g, f, 0, -6, rows + 6)
    sweep(b, a, g, f, 0, -5, rows + 5)
    coarse_source((g1, -2), b, g, d, 0, 2 * LANES, -2, rows // 2 + 2)
    first_sweep((field1, -2), (g1, -2), (f1, -3), 1, -2, rows // 2 + 2)
    level_one_down((g1, -2), (v1, -2), (field1, -2), (d1, -3), (f1, -3), packed)


def coarse_kernel(position, left, near, right, end, v1, out, g2, d2, f2, g3, d3, f3, a, b, a3, b3):
    lane = lane_index()
    side = near.shape[0]
    count = 3 * side
    reach = count // 2 * 2

    def place(n, block):
        for c in range(C + 1):
            both = block[c]
            other = pltpu.roll(both, LANES // 2, 1)
            for q, value in ((0, jnp.where(lane < LANES // 2, both, other)), (1, jnp.where(lane < LANES // 2, other, both))):
                if c < C:
                    g2[c, 2 * n + q] = value
                else:
                    d2[2 * n + q] = value

    for at, blocks in ((0, left), (side, near), (2 * side, right)):
        for n in range(side):
            place(at + n, blocks.at[n])
    pl.when(position[0] == side - 1)(lambda: place(count // 2 - side + 1, end))
    pl.when(position[0] == position[2] - side)(lambda: place(count // 2 + side - 1, end))
    g, d, f, u, w = (g2, -reach), (d2, -reach), (f2, -reach), (a, -reach), (b, -reach)
    h, e, k, s, t = (g3, -reach // 2), (d3, -reach // 2), (f3, -reach // 2), (a3, -reach // 2), (b3, -reach // 2)
    from_zero(u, g, d, f, 2, LANES // 2, 2, position, -8, 10)
    sweep(w, u, g, f, 2, -7, 9)
    coarse_source(h, w, g, d, 2, LANES // 2, -3, 4)
    from_zero(s, h, e, k, 3, LANES // 4, 1, position, -3, 4, d)
    sweep(t, s, h, k, 3, -2, 3)
    sweep(s, t, h, k, 3, -1, 2)

    def correct(q):
        for c in range(C):
            fine = spread(row(s, c, q), LANES // 2)
            for r in (q.double(), q.double() + 1):
                b[c, index(w, r)] = row(w, c, r) + fine

    each_row(-1, 2, correct, 3)
    sweep(u, w, g, f, 2, -1, 3)
    sweep(w, u, g, f, 2, 0, 2)
    for c in range(C):
        for q in (0, 1):
            fine = spread(row(w, c, q), LANES)
            for r in (2 * q, 2 * q + 1):
                out[c, r] = v1[c, r + 2] + fine


def climb(own, left, right, g0, f0, v0, g1, f1, wide, u, w, field, emit):
    rows1, halo = own.shape[1], left.shape[1]
    for c in range(C):
        for piece, at, n in ((left, 0, halo), (own, halo, rows1), (right, halo + rows1, halo)):
            for r in range(n):
                wide[c, at + r] = piece[c, r]
    sweep((u, -3), (wide, -halo), (g1, -2), (f1, -3), 1, -2, rows1 + 2)
    sweep((w, -3), (u, -3), (g1, -2), (f1, -3), 1, -1, rows1 + 1)

    def correct(q):
        for c in range(C):
            fine = spread(row((w, -3), c, q), 2 * LANES)
            for r in (q.double(), q.double() + 1):
                field[c, index((field, -HALO), r)] = row((v0, -HALO), c, r) + fine

    each_row(-1, rows1 + 1, correct, 2)
    rows = 2 * rows1
    sweep((emit, -HALO), (field, -HALO), (g0, -HALO), (f0, -HALO), 0, -1, rows + 1)
    sweep((field, -HALO), (emit, -HALO), (g0, -HALO), (f0, -HALO), 0, 0, rows)


def first_up_kernel(own, left, right, g0, f0, v0, g1, f1, out, low, high, wide, u, w, field, other):
    climb(own, left, right, g0, f0, v0, g1, f1, wide, u, w, field, other)
    rows, halo = out.shape[1], low.shape[1]
    for c in range(C):
        for r in range(rows):
            value = field[c, r + HALO, :, :LANES]
            out[c, r] = value
            if r < halo:
                low[c, r] = value
            if r >= rows - halo:
                high[c, r - rows + halo] = value


def last_up_kernel(own, left, right, g0, f0, v0, g1, f1, out, wide, u, w, field, other, scratch):
    climb(own, left, right, g0, f0, v0, g1, f1, wide, u, w, field, other)
    blocks, _, rows, _ = out.shape
    depth = NZ // blocks
    for c in range(C):
        for r in range(rows):
            scratch[c, pl.ds(r, NZ, stride=rows), :] = field[c, r + HALO, :, :LANES]
    for c in range(C):
        for z in range(NZ):
            out[z // depth, c * depth + z % depth] = scratch[c, z * rows : (z + 1) * rows]


def join_kernel(taken, out):
    for b in range(taken.shape[0]):
        out[:, :, b * LANES : (b + 1) * LANES] = taken[b]


def call(kernel, outs, scratch, *args, scalars=0):
    shape = lambda s: jax.ShapeDtypeStruct(s, jnp.float32)
    specs = [pl.BlockSpec(memory_space=pltpu.SMEM)] * scalars + [pl.BlockSpec(memory_space=pltpu.VMEM)] * (len(args) - scalars)
    out = pl.pallas_call(
        kernel,
        out_shape=[shape(s) for s in outs],
        in_specs=specs,
        out_specs=[pl.BlockSpec(memory_space=pltpu.VMEM)] * len(outs),
        scratch_shapes=[pltpu.VMEM(s, jnp.float32) for s in scratch],
        compiler_params=PARAMS,
        name=kernel.__name__,
    )(*args)
    return out


def onward(values, axis, distance):
    count = lax.axis_size(axis)
    pairs = [(i, i + distance) for i in range(count) if 0 <= i + distance < count]
    return lax.ppermute(values, axis, pairs)


def shards(right_side, density):
    blocks = lax.axis_size("gz")
    depth, rows, columns = density.shape
    position = jnp.stack([lax.axis_index("gx"), lax.axis_index("gz"), lax.axis_size("gx"), blocks]).astype(jnp.int32)
    W, R0, R1 = 2 * LANES, rows + 2 * HALO, rows // 2

    (sent,) = call(pack_kernel, [(blocks, (C + 1) * depth, rows, W)], [], right_side.reshape(C * depth, rows, columns), density)
    taken = lax.all_to_all(sent, "gz", 0, 0)
    own, low, high = call(
        unpack_kernel,
        [(C + 1, rows, NZ, W), (C + 1, HALO, NZ, W), (C + 1, HALO, NZ, W)],
        [(C + 1, 2, NZ * rows, LANES)],
        taken,
    )
    fine, mid = (C, R0, NZ, W), (C, R1 + 4, NZ, LANES)
    g0, d0, f0, v0, g1, d1, f1, v1, packed = call(
        first_down_kernel,
        [fine, fine[1:], fine[1:], fine, mid, (R1 + 6, NZ, LANES), (R1 + 6, NZ, LANES), mid, (C + 1, NZ, LANES)],
        [fine, mid],
        position,
        own,
        onward(high, "gx", 1),
        onward(low, "gx", -1),
        scalars=1,
    )

    def coarse(packed, v1):
        near = jnp.stack([onward(packed, "gx", 1), packed, onward(packed, "gx", -1)])
        last = lax.axis_size("gx") - 1
        end = lax.ppermute(packed, "gx", [(0, 2), (last, last - 2)])
        two, three = (C, 18, NZ, LANES), (C, 9, NZ, LANES)
        (out,) = call(
            coarse_kernel,
            [(C, R1, NZ, LANES)],
            [two, two[1:], two[1:], three, three[1:], three[1:], two, two, three, three],
            position,
            onward(near, "gx", 3),
            near,
            onward(near, "gx", -3),
            end,
            v1,
            scalars=1,
        )
        return out, onward(out[:, 1:], "gx", 1), onward(out[:, :-1], "gx", -1)

    middle = (C, R1 + 6, NZ, LANES)
    reach = HALO + 1
    field, low, high = call(
        first_up_kernel,
        [(C, rows, NZ, LANES), (C, reach, NZ, LANES), (C, reach, NZ, LANES)],
        [middle, middle, middle, fine, fine],
        *coarse(packed, v1),
        g0,
        f0,
        v0,
        g1,
        f1,
    )
    left, right = onward(high, "gx", 1), onward(low, "gx", -1)
    half = (rows + 2 * reach) // 2
    to_left, to_right = call(side_kernel, [(C, half, NZ, LANES)] * 2, [], field, left, right)
    v0, g1, v1, packed = call(
        second_down_kernel,
        [fine, mid, mid, (C + 1, NZ, LANES)],
        [(C, rows + 2 * reach, NZ, W), fine, mid],
        field,
        left,
        right,
        onward(to_left, "gz", -1),
        onward(to_right, "gz", 1),
        g0,
        d0,
        f0,
        d1,
        f1,
    )
    (sent,) = call(
        last_up_kernel,
        [(blocks, C * depth, rows, LANES)],
        [middle, middle, middle, fine, fine, (C, NZ * rows, LANES)],
        *coarse(packed, v1),
        g0,
        f0,
        v0,
        g1,
        f1,
    )
    (out,) = call(join_kernel, [(C * depth, rows, columns)], [], lax.all_to_all(sent, "gz", 0, 0))
    return out.reshape(right_side.shape)


def solution(mesh):
    return jax.shard_map(
        shards,
        mesh=mesh,
        in_specs=(P(None, "gz", "gx", None), P("gz", "gx", None)),
        out_specs=P(None, "gz", "gx", None),
        check_vma=False,
    )
```

```python
import jax
import jax.numpy as jnp
from jax import lax
from jax.experimental import pallas as pl
from jax.experimental.pallas import tpu as pltpu
from jax.sharding import PartitionSpec as P

relaxation = 0.8
plane_coupling = 16.0
depth_coupling = 1.0
C = 3
NZ = 24
HALO = 6
LANES = 128
UNROLL = (2, 4, 8, 8)
PARAMS = pltpu.CompilerParams(vmem_limit_bytes=28 << 20)


def coupling_of(level):
    return plane_coupling / 4.0**level


def base_of(level):
    return 4.0 * coupling_of(level) + 2.0 * depth_coupling


class Row:
    def __init__(self, base, shift):
        self.base, self.shift = base, shift

    def __add__(self, n):
        return Row(self.base, self.shift + n)

    def __sub__(self, n):
        return self + -n

    def double(self):
        return Row(2 * self.base, 2 * self.shift)


def index(field, r):
    return r.base + (r.shift - field[1]) if isinstance(r, Row) else r - field[1]


def row(field, c, r):
    return field[0][c, index(field, r)]


def shared(field, r):
    return field[0][index(field, r)]


def neighbours(field, c, r, level):
    mid = row(field, c, r)
    width = mid.shape[1]
    lateral = row(field, c, r - 1) + row(field, c, r + 1) + pltpu.roll(mid, 1, 1) + pltpu.roll(mid, width - 1, 1)
    vertical = pltpu.roll(mid, 1, 0) + pltpu.roll(mid, NZ - 1, 0)
    return mid, coupling_of(level) * lateral + depth_coupling * vertical


def each_row(low, high, body, unroll):
    steps = (high - low) // unroll

    def step(n, carry):
        for k in range(unroll):
            body(Row(unroll * n, low + k))
        return carry

    if steps > 1:
        lax.fori_loop(0, steps, step, 0)
        low += steps * unroll
    for r in range(low, high):
        body(Row(0, r))


def sweep(target, field, source, factor, level, low, high):
    def body(r):
        f = shared(factor, r)
        for c in range(C):
            mid, around = neighbours(field, c, r, level)
            target[0][c, index(target, r)] = (1.0 - relaxation) * mid + f * (row(source, c, r) + around)

    each_row(low, high, body, UNROLL[level])


def lane_index():
    return lax.broadcasted_iota(jnp.int32, (NZ, LANES), 1)


def take(values, index):
    return jnp.take_along_axis(values, index, axis=1, mode="promise_in_bounds")


def pair_sum(values, period):
    lane = lane_index()
    if values.shape[1] == 2 * LANES:
        even = (2 * lane) % LANES
        halves = [take(h + pltpu.roll(h, LANES - 1, 1), even) for h in (values[:, :LANES], values[:, LANES:])]
        return jnp.where(lane < LANES // 2, halves[0], halves[1])
    return take(values + pltpu.roll(values, LANES - 1, 1), (2 * lane) % period)


def spread(values, period):
    lane = lane_index()
    if period == 2 * LANES:
        return jnp.concatenate([take(values, lane // 2), take(values, LANES // 2 + lane // 2)], axis=1)
    return take(values, (lane % period) // 2)


def coarse_source(target, field, source, density, level, period, low, high):
    def body(q):
        for c in range(C):
            total = None
            for r in (q.double(), q.double() + 1):
                mid, around = neighbours(field, c, r, level)
                residual = row(source, c, r) + around - (shared(density, r) + base_of(level)) * mid
                total = residual if total is None else total + residual
            target[0][c, index(target, q)] = 0.25 * pair_sum(total, period)

    each_row(low, high, body, max(1, UNROLL[level] // 2))


def from_zero(target, source, density, factor, level, period, rows, position, low, high, finer=None, reach=0):
    i, j, count_x, count_y = position[0], position[1], position[2], position[3]
    width = factor[0].shape[-1]
    lane = lax.broadcasted_iota(jnp.int32, (NZ, width), 1) % period
    inside_y = ((lane < 3 * period // 4) | (j > 0)) & ((lane < period // 2) | (lane >= 3 * period // 4) | (j < count_y - 1))

    def body(r):
        if finer is None:
            own = shared(density, r)
        else:
            own = 0.25 * pair_sum(shared(finer, r.double()) + shared(finer, r.double() + 1), 2 * period)
            density[0][index(density, r)] = own
        at = i * rows + r.base
        inside = inside_y & ((at >= -r.shift) & (at < count_x * rows - r.shift))
        f = jnp.where(inside, relaxation / (own + base_of(level)), 0.0)
        factor[0][index(factor, r)] = f
        return f

    def whole(r):
        f = body(r)
        for c in range(C):
            target[0][c, index(target, r)] = f * row(source, c, r)

    for r in [*range(low - reach, low), *range(high, high + reach)]:
        body(Row(0, r))
    each_row(low, high, whole, UNROLL[level])


def first_sweep(target, source, factor, level, low, high):
    def body(r):
        f = shared(factor, r)
        for c in range(C):
            target[0][c, index(target, r)] = f * row(source, c, r)

    each_row(low, high, body, UNROLL[level])


def level_one_down(g1, v1, scratch, d1, f1, packed):
    sweep(v1, scratch, g1, f1, 1, -1, 5)
    lane = lane_index()
    for c in range(C + 1):
        pair = []
        for q in (0, 1):
            total = None
            for r in (2 * q, 2 * q + 1):
                if c == C:
                    part = shared(d1, r)
                else:
                    mid, around = neighbours(v1, c, r, 1)
                    part = row(g1, c, r) + around - (shared(d1, r) + base_of(1)) * mid
                total = part if total is None else total + part
            pair.append(0.25 * pair_sum(total, LANES))
        packed[c] = jnp.where(lane < LANES // 2, pair[0], pair[1])


def rows_to_send(position, own, first, second):
    odd, spare = position[4], own.shape[1] - first.shape[1]
    for c in range(own.shape[0]):
        for r in range(first.shape[1]):
            first[c, r] = own[c, (1 - odd) * spare + r]
            second[c, r] = own[c, odd * spare + r]


def with_halo(position, own, first, second, store):
    odd, rows, halo = position[4], own.shape[1], first.shape[1]
    for c in range(own.shape[0]):
        for piece, at in ((first, (1 - odd) * (halo + rows)), (own, halo), (second, odd * (halo + rows))):
            for r in range(piece.shape[1]):
                store(c, at + r, piece[c, r])


def pack_kernel(source, density, out):
    blocks = out.shape[0]
    for ref, at, n in ((source, 0, source.shape[0]), (density, source.shape[0], density.shape[0])):
        for m in range(n):
            for b in range(blocks):
                out[b, at + m, :, :LANES] = ref[m, :, b * LANES : (b + 1) * LANES]
                zero = jnp.zeros((ref.shape[1], LANES), jnp.float32)
                after = ref[m, :, (b + 1) * LANES : (b + 2) * LANES] if b + 1 < blocks else zero
                before = ref[m, :, (b - 1) * LANES : b * LANES] if b else zero
                lane = lax.broadcasted_iota(jnp.int32, zero.shape, 1)
                out[b, at + m, :, LANES:] = jnp.where(lane < LANES // 2, after, before)


def unpack_kernel(position, taken, own, first, second, scratch):
    blocks, _, rows, _ = taken.shape
    depth = NZ // blocks
    for c in range(C + 1):
        for b in range(blocks):
            for z in range(depth):
                at = (b * depth + z) * rows
                for h in range(2):
                    scratch[c, h, at : at + rows] = taken[b, c * depth + z, :, h * LANES : (h + 1) * LANES]
    for c in range(C + 1):
        for r in range(rows):
            for h in range(2):
                part = scratch[c, h, pl.ds(r, NZ, stride=rows), :]
                lanes = slice(h * LANES, (h + 1) * LANES)
                own[c, r, :, lanes] = part
    rows_to_send(position, own, first, second)


def first_down_kernel(position, own, first, second, g0, d0, f0, v0, g1, d1, f1, v1, packed, field, field1):
    rows = own.shape[1]

    def store(c, at, value):
        if c < C:
            g0[c, at] = value
        else:
            d0[at] = value

    with_halo(position, own, first, second, store)
    g, d, f, a, b = (g0, -HALO), (d0, -HALO), (f0, -HALO), (field, -HALO), (v0, -HALO)
    from_zero(a, g, d, f, 0, 2 * LANES, rows, position, -HALO, rows + HALO)
    sweep(b, a, g, f, 0, -5, rows + 5)
    coarse_source((g1, -2), b, g, d, 0, 2 * LANES, -2, rows // 2 + 2)
    from_zero((field1, -2), (g1, -2), (d1, -3), (f1, -3), 1, LANES, rows // 2, position, -2, rows // 2 + 2, d, 1)
    level_one_down((g1, -2), (v1, -2), (field1, -2), (d1, -3), (f1, -3), packed)


def side_kernel(position, own, first, second, tall, to_first, to_second):
    half = tall.shape[1] // 2
    low = (lane_index() < LANES // 2) == (position[5] == 1)

    def store(c, at, value):
        tall[c, at] = value

    with_halo(position, own, first, second, store)
    for c in range(C):
        for r in range(half):
            one, two = tall[c, r], pltpu.roll(tall[c, r + half], LANES // 2, 1)
            to_first[c, r] = jnp.where(low, one, two)
            to_second[c, r] = jnp.where(low, two, one)


def second_down_kernel(position, tall, first, second, g0, d0, f0, d1, f1, v0, g1, v1, packed, wide, field, field1):
    half = tall.shape[1] // 2
    halo = half - v0.shape[1] // 2 + HALO
    rows = 2 * (half - halo)
    low = (lane_index() < LANES // 2) == (position[5] == 0)
    for c in range(C):
        for r in range(2 * half):
            wide[c, r, :, :LANES] = tall[c, r]
        for r in range(half):
            wide[c, r, :, LANES:] = jnp.where(low, first[c, r], second[c, r])
            wide[c, r + half, :, LANES:] = pltpu.roll(jnp.where(low, second[c, r], first[c, r]), LANES // 2, 1)
    g, d, f, a, b = (g0, -HALO), (d0, -HALO), (f0, -HALO), (field, -HALO), (v0, -HALO)
    sweep(a, (wide, -halo), g, f, 0, -6, rows + 6)
    sweep(b, a, g, f, 0, -5, rows + 5)
    coarse_source((g1, -2), b, g, d, 0, 2 * LANES, -2, rows // 2 + 2)
    first_sweep((field1, -2), (g1, -2), (f1, -3), 1, -2, rows // 2 + 2)
    level_one_down((g1, -2), (v1, -2), (field1, -2), (d1, -3), (f1, -3), packed)


def coarse_kernel(position, pair, near1, near2, far1, far2, v1, out, first, second, g2, d2, f2, g3, d3, f3, a, b, a3, b3):
    lane = lane_index()
    reach = 10
    odd, step = position[4], 1 - 2 * position[6]

    def place(block, n):
        for c in range(C + 1):
            both = block[c]
            other = pltpu.roll(both, LANES // 2, 1)
            for q, value in ((0, jnp.where(lane < LANES // 2, both, other)), (1, jnp.where(lane < LANES // 2, other, both))):
                if c < C:
                    g2[c, 2 * n + q] = value
                else:
                    d2[2 * n + q] = value

    for blocks, away in ((pair, 0), (near1, step), (near2, -step), (far1, 2 * step), (far2, -2 * step)):
        for core in range(2):
            place(blocks.at[core], 2 * away + (reach // 2 + core - odd))
    g, d, f, u, w = (g2, -reach), (d2, -reach), (f2, -reach), (a, -reach), (b, -reach)
    h, e, k, s, t = (g3, -reach // 2), (d3, -reach // 2), (f3, -reach // 2), (a3, -reach // 2), (b3, -reach // 2)
    from_zero(u, g, d, f, 2, LANES // 2, 2, position, -8, 10)
    sweep(w, u, g, f, 2, -7, 9)
    coarse_source(h, w, g, d, 2, LANES // 2, -3, 4)
    from_zero(s, h, e, k, 3, LANES // 4, 1, position, -3, 4, d)
    sweep(t, s, h, k, 3, -2, 3)
    sweep(s, t, h, k, 3, -1, 2)

    def correct(q):
        for c in range(C):
            fine = spread(row(s, c, q), LANES // 2)
            for r in (q.double(), q.double() + 1):
                b[c, index(w, r)] = row(w, c, r) + fine

    each_row(-1, 2, correct, 3)
    sweep(u, w, g, f, 2, -1, 3)
    sweep(w, u, g, f, 2, 0, 2)
    for c in range(C):
        for q in (0, 1):
            fine = spread(row(w, c, q), LANES)
            for r in (2 * q, 2 * q + 1):
                out[c, r] = v1[c, r + 2] + fine
    rows_to_send(position, out, first, second)


def climb(position, own, first, second, g0, f0, v0, g1, f1, wide, u, w, field, emit):
    rows1, halo = own.shape[1], first.shape[1]

    def store(c, at, value):
        wide[c, at] = value

    with_halo(position, own, first, second, store)
    sweep((u, -3), (wide, -halo), (g1, -2), (f1, -3), 1, -2, rows1 + 2)
    sweep((w, -3), (u, -3), (g1, -2), (f1, -3), 1, -1, rows1 + 1)

    def correct(q):
        for c in range(C):
            fine = spread(row((w, -3), c, q), 2 * LANES)
            for r in (q.double(), q.double() + 1):
                field[c, index((field, -HALO), r)] = row((v0, -HALO), c, r) + fine

    each_row(-1, rows1 + 1, correct, 2)
    rows = 2 * rows1
    sweep((emit, -HALO), (field, -HALO), (g0, -HALO), (f0, -HALO), 0, -1, rows + 1)
    sweep((field, -HALO), (emit, -HALO), (g0, -HALO), (f0, -HALO), 0, 0, rows)


def first_up_kernel(position, own, left, right, g0, f0, v0, g1, f1, out, first, second, wide, u, w, field, other):
    climb(position, own, left, right, g0, f0, v0, g1, f1, wide, u, w, field, other)
    for c in range(C):
        for r in range(out.shape[1]):
            out[c, r] = field[c, r + HALO, :, :LANES]
    rows_to_send(position, out, first, second)


def last_up_kernel(position, own, left, right, g0, f0, v0, g1, f1, out, wide, u, w, field, other, scratch):
    climb(position, own, left, right, g0, f0, v0, g1, f1, wide, u, w, field, other)
    blocks, _, rows, _ = out.shape
    depth = NZ // blocks
    for c in range(C):
        for r in range(rows):
            scratch[c, pl.ds(r, NZ, stride=rows), :] = field[c, r + HALO, :, :LANES]
    for c in range(C):
        for z in range(NZ):
            out[z // depth, c * depth + z % depth] = scratch[c, z * rows : (z + 1) * rows]


def join_kernel(taken, out):
    for b in range(taken.shape[0]):
        out[:, :, b * LANES : (b + 1) * LANES] = taken[b]


def call(kernel, outs, scratch, *args, scalars=0):
    shape = lambda s: jax.ShapeDtypeStruct(s, jnp.float32)
    specs = [pl.BlockSpec(memory_space=pltpu.SMEM)] * scalars + [pl.BlockSpec(memory_space=pltpu.VMEM)] * (len(args) - scalars)
    out = pl.pallas_call(
        kernel,
        out_shape=[shape(s) for s in outs],
        in_specs=specs,
        out_specs=[pl.BlockSpec(memory_space=pltpu.VMEM)] * len(outs),
        scratch_shapes=[pltpu.VMEM(s, jnp.float32) for s in scratch],
        compiler_params=PARAMS,
        name=kernel.__name__,
    )(*args)
    return out


def swap(values, axis, first, unit=1):
    count, pairs = lax.axis_size(axis), []
    for i in range(count):
        group = i // unit
        other = group ^ 1 if first else ((group - 1) ^ 1) + 1
        if 0 <= other < count // unit:
            pairs.append((i, other * unit + i % unit))
    return lax.ppermute(values, axis, pairs)


def shards(right_side, density):
    blocks = lax.axis_size("gz")
    depth, rows, columns = density.shape
    i, j = lax.axis_index("gx"), lax.axis_index("gz")
    position = jnp.stack([i, j, lax.axis_size("gx"), blocks, i % 2, j % 2, i // 2 % 2]).astype(jnp.int32)
    W, R0, R1 = 2 * LANES, rows + 2 * HALO, rows // 2

    (sent,) = call(pack_kernel, [(blocks, (C + 1) * depth, rows, W)], [], right_side.reshape(C * depth, rows, columns), density)
    taken = lax.all_to_all(sent, "gz", 0, 0)
    own, first, second = call(
        unpack_kernel,
        [(C + 1, rows, NZ, W), (C + 1, HALO, NZ, W), (C + 1, HALO, NZ, W)],
        [(C + 1, 2, NZ * rows, LANES)],
        position,
        taken,
        scalars=1,
    )
    fine, mid = (C, R0, NZ, W), (C, R1 + 4, NZ, LANES)
    g0, d0, f0, v0, g1, d1, f1, v1, packed = call(
        first_down_kernel,
        [fine, fine[1:], fine[1:], fine, mid, (R1 + 6, NZ, LANES), (R1 + 6, NZ, LANES), mid, (C + 1, NZ, LANES)],
        [fine, mid],
        position,
        own,
        swap(first, "gx", True),
        swap(second, "gx", False),
        scalars=1,
    )

    def coarse(packed, v1):
        partner = swap(packed, "gx", True)
        pair = jnp.where(i % 2 == 0, jnp.stack([packed, partner]), jnp.stack([partner, packed]))
        near = [swap(pair, "gx", first, 2) for first in (True, False)]
        far = [swap(near[1], "gx", True, 2), swap(near[0], "gx", False, 2)]
        two, three = (C, 22, NZ, LANES), (C, 11, NZ, LANES)
        out, first, second = call(
            coarse_kernel,
            [(C, R1, NZ, LANES)] + [(C, R1 - 1, NZ, LANES)] * 2,
            [two, two[1:], two[1:], three, three[1:], three[1:], two, two, three, three],
            position,
            pair,
            *near,
            *far,
            v1,
            scalars=1,
        )
        return out, swap(first, "gx", True), swap(second, "gx", False)

    middle = (C, R1 + 6, NZ, LANES)
    reach = HALO + 1
    field, first, second = call(
        first_up_kernel,
        [(C, rows, NZ, LANES), (C, reach, NZ, LANES), (C, reach, NZ, LANES)],
        [middle, middle, middle, fine, fine],
        position,
        *coarse(packed, v1),
        g0,
        f0,
        v0,
        g1,
        f1,
        scalars=1,
    )
    half = (rows + 2 * reach) // 2
    tall, first, second = call(
        side_kernel,
        [(C, 2 * half, NZ, LANES)] + [(C, half, NZ, LANES)] * 2,
        [],
        position,
        field,
        swap(first, "gx", True),
        swap(second, "gx", False),
        scalars=1,
    )
    v0, g1, v1, packed = call(
        second_down_kernel,
        [fine, mid, mid, (C + 1, NZ, LANES)],
        [(C, 2 * half, NZ, W), fine, mid],
        position,
        tall,
        swap(first, "gz", True),
        swap(second, "gz", False),
        g0,
        d0,
        f0,
        d1,
        f1,
        scalars=1,
    )
    (sent,) = call(
        last_up_kernel,
        [(blocks, C * depth, rows, LANES)],
        [middle, middle, middle, fine, fine, (C, NZ * rows, LANES)],
        position,
        *coarse(packed, v1),
        g0,
        f0,
        v0,
        g1,
        f1,
        scalars=1,
    )
    (out,) = call(join_kernel, [(C * depth, rows, columns)], [], lax.all_to_all(sent, "gz", 0, 0))
    return out.reshape(right_side.shape)


def solution(mesh):
    return jax.shard_map(
        shards,
        mesh=mesh,
        in_specs=(P(None, "gz", "gx", None), P("gz", "gx", None)),
        out_specs=P(None, "gz", "gx", None),
        check_vma=False,
    )
```

```python
import jax
import jax.numpy as jnp
from jax import lax
from jax.experimental import pallas as pl
from jax.experimental.pallas import tpu as pltpu
from jax.sharding import PartitionSpec as P

relaxation = 0.8
plane_coupling = 16.0
depth_coupling = 1.0
C = 3
NZ = 24
HALO = 6
LANES = 128
UNROLL = (2, 4, 8, 8)
PARAMS = pltpu.CompilerParams(vmem_limit_bytes=12 << 20)


def coupling_of(level):
    return plane_coupling / 4.0**level


def base_of(level):
    return 4.0 * coupling_of(level) + 2.0 * depth_coupling


class Row:
    def __init__(self, base, shift):
        self.base, self.shift = base, shift

    def __add__(self, n):
        return Row(self.base, self.shift + n)

    def __sub__(self, n):
        return self + -n

    def double(self):
        return Row(2 * self.base, 2 * self.shift)


def index(field, r):
    return r.base + (r.shift - field[1]) if isinstance(r, Row) else r - field[1]


def row(field, c, r):
    return field[0][c, index(field, r)]


def shared(field, r):
    return field[0][index(field, r)]


def neighbours(field, c, r, level):
    mid = row(field, c, r)
    width = mid.shape[1]
    lateral = row(field, c, r - 1) + row(field, c, r + 1) + pltpu.roll(mid, 1, 1) + pltpu.roll(mid, width - 1, 1)
    vertical = pltpu.roll(mid, 1, 0) + pltpu.roll(mid, NZ - 1, 0)
    return mid, coupling_of(level) * lateral + depth_coupling * vertical


def each_row(low, high, body, unroll):
    steps = (high - low) // unroll

    def step(n, carry):
        for k in range(unroll):
            body(Row(unroll * n, low + k))
        return carry

    if steps > 1:
        lax.fori_loop(0, steps, step, 0)
        low += steps * unroll
    for r in range(low, high):
        body(Row(0, r))


def sweep(target, field, source, factor, level, low, high):
    def body(r):
        f = shared(factor, r)
        for c in range(C):
            mid, around = neighbours(field, c, r, level)
            target[0][c, index(target, r)] = (1.0 - relaxation) * mid + f * (row(source, c, r) + around)

    each_row(low, high, body, UNROLL[level])


def lane_index():
    return lax.broadcasted_iota(jnp.int32, (NZ, LANES), 1)


def take(values, index):
    return jnp.take_along_axis(values, index, axis=1, mode="promise_in_bounds")


def pair_sum(values, period):
    lane = lane_index()
    if values.shape[1] == 2 * LANES:
        even = (2 * lane) % LANES
        halves = [take(h + pltpu.roll(h, LANES - 1, 1), even) for h in (values[:, :LANES], values[:, LANES:])]
        return jnp.where(lane < LANES // 2, halves[0], halves[1])
    return take(values + pltpu.roll(values, LANES - 1, 1), (2 * lane) % period)


def spread(values, period):
    lane = lane_index()
    if period == 2 * LANES:
        return jnp.concatenate([take(values, lane // 2), take(values, LANES // 2 + lane // 2)], axis=1)
    return take(values, (lane % period) // 2)


def coarse_source(target, field, source, density, level, period, low, high):
    def body(q):
        for c in range(C):
            total = None
            for r in (q.double(), q.double() + 1):
                mid, around = neighbours(field, c, r, level)
                residual = row(source, c, r) + around - (shared(density, r) + base_of(level)) * mid
                total = residual if total is None else total + residual
            target[0][c, index(target, q)] = 0.25 * pair_sum(total, period)

    each_row(low, high, body, max(1, UNROLL[level] // 2))


def from_zero(target, source, density, factor, level, period, rows, position, low, high, finer=None, reach=0, group=1):
    i, j, count_x, count_y = position[0] // group, position[1], position[2] // group, position[3]
    width = factor[0].shape[-1]
    lane = lax.broadcasted_iota(jnp.int32, (NZ, width), 1) % period
    inside_y = ((lane < 3 * period // 4) | (j > 0)) & ((lane < period // 2) | (lane >= 3 * period // 4) | (j < count_y - 1))

    def body(r):
        if finer is None:
            own = shared(density, r)
        else:
            own = 0.25 * pair_sum(shared(finer, r.double()) + shared(finer, r.double() + 1), 2 * period)
            density[0][index(density, r)] = own
        at = i * rows + r.base
        inside = inside_y & ((at >= -r.shift) & (at < count_x * rows - r.shift))
        f = jnp.where(inside, relaxation / (own + base_of(level)), 0.0)
        factor[0][index(factor, r)] = f
        return f

    def whole(r):
        f = body(r)
        for c in range(C):
            target[0][c, index(target, r)] = f * row(source, c, r)

    for r in [*range(low - reach, low), *range(high, high + reach)]:
        body(Row(0, r))
    each_row(low, high, whole, UNROLL[level])


def first_sweep(target, source, factor, level, low, high):
    def body(r):
        f = shared(factor, r)
        for c in range(C):
            target[0][c, index(target, r)] = f * row(source, c, r)

    each_row(low, high, body, UNROLL[level])


def level_one_down(position, g1, v1, scratch, d1, f1, packed, edge):
    sweep(v1, scratch, g1, f1, 1, -1, 5)
    lane = lane_index()
    for c in range(C + 1):
        pair = []
        for q in (0, 1):
            total = None
            for r in (2 * q, 2 * q + 1):
                if c == C:
                    part = shared(d1, r)
                else:
                    mid, around = neighbours(v1, c, r, 1)
                    part = row(g1, c, r) + around - (shared(d1, r) + base_of(1)) * mid
                total = part if total is None else total + part
            pair.append(0.25 * pair_sum(total, LANES))
        packed[c] = jnp.where(lane < LANES // 2, pair[0], pair[1])
    count = edge.shape[0] // C
    for c in range(C):
        for r in range(count):
            edge[c * count + r] = v1[0][c, (1 - position[4]) + (r - v1[1])]


def rows_to_send(position, own, first, second):
    odd, spare = position[4], own.shape[1] - first.shape[1]
    for c in range(own.shape[0]):
        for r in range(first.shape[1]):
            first[c, r] = own[c, (1 - odd) * spare + r]
            second[c, r] = own[c, odd * spare + r]


def with_halo(position, own, first, second, store):
    odd, rows, halo = position[4], own.shape[1], first.shape[1]
    for c in range(own.shape[0]):
        for piece, at in ((first, (1 - odd) * (halo + rows)), (own, halo), (second, odd * (halo + rows))):
            for r in range(piece.shape[1]):
                store(c, at + r, piece[c, r])


def pack_kernel(source, density, out):
    blocks = out.shape[0]
    for ref, at, n in ((source, 0, source.shape[0]), (density, source.shape[0], density.shape[0])):
        for m in range(n):
            for b in range(blocks):
                out[b, at + m, :, :LANES] = ref[m, :, b * LANES : (b + 1) * LANES]
                zero = jnp.zeros((ref.shape[1], LANES), jnp.float32)
                after = ref[m, :, (b + 1) * LANES : (b + 2) * LANES] if b + 1 < blocks else zero
                before = ref[m, :, (b - 1) * LANES : b * LANES] if b else zero
                lane = lax.broadcasted_iota(jnp.int32, zero.shape, 1)
                out[b, at + m, :, LANES:] = jnp.where(lane < LANES // 2, after, before)


def unpack_kernel(position, taken, own, first, second, scratch):
    blocks, _, rows, _ = taken.shape
    depth = NZ // blocks
    for c in range(C + 1):
        for b in range(blocks):
            for z in range(depth):
                at = (b * depth + z) * rows
                for h in range(2):
                    scratch[c, h, at : at + rows] = taken[b, c * depth + z, :, h * LANES : (h + 1) * LANES]
    for c in range(C + 1):
        for r in range(rows):
            for h in range(2):
                part = scratch[c, h, pl.ds(r, NZ, stride=rows), :]
                lanes = slice(h * LANES, (h + 1) * LANES)
                own[c, r, :, lanes] = part
    rows_to_send(position, own, first, second)


def first_down_kernel(position, own, first, second, g0, d0, f0, v0, g1, d1, f1, v1, packed, edge, field, field1):
    rows = own.shape[1]

    def store(c, at, value):
        if c < C:
            g0[c, at] = value
        else:
            d0[at] = value

    with_halo(position, own, first, second, store)
    g, d, f, a, b = (g0, -HALO), (d0, -HALO), (f0, -HALO), (field, -HALO), (v0, -HALO)
    from_zero(a, g, d, f, 0, 2 * LANES, rows, position, -HALO, rows + HALO)
    sweep(b, a, g, f, 0, -5, rows + 5)
    coarse_source((g1, -2), b, g, d, 0, 2 * LANES, -2, rows // 2 + 2)
    from_zero((field1, -2), (g1, -2), (d1, -3), (f1, -3), 1, LANES, rows // 2, position, -2, rows // 2 + 2, d, 1)
    level_one_down(position, (g1, -2), (v1, -2), (field1, -2), (d1, -3), (f1, -3), packed, edge)


def side_kernel(position, own, first, second, tall, to_first, to_second):
    half = tall.shape[1] // 2
    low = (lane_index() < LANES // 2) == (position[5] == 1)

    def store(c, at, value):
        tall[c, at] = value

    with_halo(position, own, first, second, store)
    for c in range(C):
        for r in range(half):
            one, two = tall[c, r], pltpu.roll(tall[c, r + half], LANES // 2, 1)
            to_first[c, r] = jnp.where(low, one, two)
            to_second[c, r] = jnp.where(low, two, one)


def second_down_kernel(position, tall, first, second, g0, d0, f0, d1, f1, v0, g1, v1, packed, edge, wide, field, field1):
    half = tall.shape[1] // 2
    halo = half - v0.shape[1] // 2 + HALO
    rows = 2 * (half - halo)
    low = (lane_index() < LANES // 2) == (position[5] == 0)
    for c in range(C):
        for r in range(2 * half):
            wide[c, r, :, :LANES] = tall[c, r]
        for r in range(half):
            wide[c, r, :, LANES:] = jnp.where(low, first[c, r], second[c, r])
            wide[c, r + half, :, LANES:] = pltpu.roll(jnp.where(low, second[c, r], first[c, r]), LANES // 2, 1)
    g, d, f, a, b = (g0, -HALO), (d0, -HALO), (f0, -HALO), (field, -HALO), (v0, -HALO)
    sweep(a, (wide, -halo), g, f, 0, -6, rows + 6)
    sweep(b, a, g, f, 0, -5, rows + 5)
    coarse_source((g1, -2), b, g, d, 0, 2 * LANES, -2, rows // 2 + 2)
    first_sweep((field1, -2), (g1, -2), (f1, -3), 1, -2, rows // 2 + 2)
    level_one_down(position, (g1, -2), (v1, -2), (field1, -2), (d1, -3), (f1, -3), packed, edge)


def coarse_kernel(position, mine, other, v1, out, first, second, g2, d2, f2, g3, d3, f3, a, b, a3, b3):
    lane = lane_index()
    odd, step = position[4], 1 - 2 * position[6]
    count, reach = first.shape[1], 8
    units = C + 1

    for ref, core in ((mine, odd), (other, 1 - odd)):
        for n, away in enumerate((0, step, -step, 2 * step, -2 * step)):
            at = 4 * away + (2 * core + reach)
            for c in range(units):
                both = ref[n * units + c]
                twin = pltpu.roll(both, LANES // 2, 1)
                for q, value in ((0, jnp.where(lane < LANES // 2, both, twin)), (1, jnp.where(lane < LANES // 2, twin, both))):
                    if c < C:
                        g2[c, at + q] = value
                    else:
                        d2[at + q] = value
    g, d, f, u, w = (g2, -reach), (d2, -reach), (f2, -reach), (a, -reach), (b, -reach)
    h, e, k, s, t = (g3, -reach // 2), (d3, -reach // 2), (f3, -reach // 2), (a3, -reach // 2), (b3, -reach // 2)
    from_zero(u, g, d, f, 2, LANES // 2, 4, position, -8, 12, group=2)
    sweep(w, u, g, f, 2, -7, 11)
    coarse_source(h, w, g, d, 2, LANES // 2, -3, 5)
    from_zero(s, h, e, k, 3, LANES // 4, 2, position, -3, 5, d, group=2)
    sweep(t, s, h, k, 3, -2, 4)
    sweep(s, t, h, k, 3, -1, 3)

    def correct(q):
        for c in range(C):
            fine = spread(row(s, c, q), LANES // 2)
            for r in (q.double(), q.double() + 1):
                b[c, index(w, r)] = row(w, c, r) + fine

    each_row(-1, 3, correct, 4)
    sweep(u, w, g, f, 2, -1, 5)
    sweep(w, u, g, f, 2, 0, 4)
    for c in range(C):
        for q in (0, 1):
            fine = spread(b[c, 2 * odd + (q + reach)], LANES)
            for r in (2 * q, 2 * q + 1):
                out[c, r] = v1[c, r + 2] + fine
        for r, q in enumerate((0, odd, 1)):
            fine = spread(b[c, 2 * (1 - odd) + (reach + q)], LANES)
            first[c, r] = other[5 * units + c * count + r] + fine
        for r in range(count):
            second[c, r] = out[c, odd * (out.shape[1] - count) + r]


def climb(position, own, first, second, g0, f0, v0, g1, f1, wide, u, w, field, emit):
    rows1, halo = own.shape[1], first.shape[1]

    def store(c, at, value):
        wide[c, at] = value

    with_halo(position, own, first, second, store)
    sweep((u, -3), (wide, -halo), (g1, -2), (f1, -3), 1, -2, rows1 + 2)
    sweep((w, -3), (u, -3), (g1, -2), (f1, -3), 1, -1, rows1 + 1)

    def correct(q):
        for c in range(C):
            fine = spread(row((w, -3), c, q), 2 * LANES)
            for r in (q.double(), q.double() + 1):
                field[c, index((field, -HALO), r)] = row((v0, -HALO), c, r) + fine

    each_row(-1, rows1 + 1, correct, 2)
    rows = 2 * rows1
    sweep((emit, -HALO), (field, -HALO), (g0, -HALO), (f0, -HALO), 0, -1, rows + 1)
    sweep((field, -HALO), (emit, -HALO), (g0, -HALO), (f0, -HALO), 0, 0, rows)


def first_up_kernel(position, own, left, right, g0, f0, v0, g1, f1, out, first, second, wide, u, w, field, other):
    climb(position, own, left, right, g0, f0, v0, g1, f1, wide, u, w, field, other)
    for c in range(C):
        for r in range(out.shape[1]):
            out[c, r] = field[c, r + HALO, :, :LANES]
    rows_to_send(position, out, first, second)


def last_up_kernel(position, own, left, right, g0, f0, v0, g1, f1, out, wide, u, w, field, other, scratch):
    climb(position, own, left, right, g0, f0, v0, g1, f1, wide, u, w, field, other)
    blocks, _, rows, _ = out.shape
    depth = NZ // blocks
    for c in range(C):
        for r in range(rows):
            scratch[c, pl.ds(r, NZ, stride=rows), :] = field[c, r + HALO, :, :LANES]
    for c in range(C):
        for z in range(NZ):
            out[z // depth, c * depth + z % depth] = scratch[c, z * rows : (z + 1) * rows]


def join_kernel(taken, out):
    for b in range(taken.shape[0]):
        out[:, :, b * LANES : (b + 1) * LANES] = taken[b]


def call(kernel, outs, scratch, *args, scalars=0):
    shape = lambda s: jax.ShapeDtypeStruct(s, jnp.float32)
    specs = [pl.BlockSpec(memory_space=pltpu.SMEM)] * scalars + [pl.BlockSpec(memory_space=pltpu.VMEM)] * (len(args) - scalars)
    out = pl.pallas_call(
        kernel,
        out_shape=[shape(s) for s in outs],
        in_specs=specs,
        out_specs=[pl.BlockSpec(memory_space=pltpu.VMEM)] * len(outs),
        scratch_shapes=[pltpu.VMEM(s, jnp.float32) for s in scratch],
        compiler_params=PARAMS,
        name=kernel.__name__,
    )(*args)
    return out


def swap(values, axis, first, unit=1):
    count, pairs = lax.axis_size(axis), []
    for i in range(count):
        group = i // unit
        other = group ^ 1 if first else ((group - 1) ^ 1) + 1
        if 0 <= other < count // unit:
            pairs.append((i, other * unit + i % unit))
    return lax.ppermute(values, axis, pairs)


def shards(right_side, density):
    blocks = lax.axis_size("gz")
    depth, rows, columns = density.shape
    i, j = lax.axis_index("gx"), lax.axis_index("gz")
    position = jnp.stack([i, j, lax.axis_size("gx"), blocks, i % 2, j % 2, i // 2 % 2]).astype(jnp.int32)
    W, R0, R1 = 2 * LANES, rows + 2 * HALO, rows // 2

    (sent,) = call(pack_kernel, [(blocks, (C + 1) * depth, rows, W)], [], right_side.reshape(C * depth, rows, columns), density)
    taken = lax.all_to_all(sent, "gz", 0, 0)
    own, first, second = call(
        unpack_kernel,
        [(C + 1, rows, NZ, W), (C + 1, HALO, NZ, W), (C + 1, HALO, NZ, W)],
        [(C + 1, 2, NZ * rows, LANES)],
        position,
        taken,
        scalars=1,
    )
    fine, mid = (C, R0, NZ, W), (C, R1 + 4, NZ, LANES)
    sends = [(C + 1, NZ, LANES), (C * (R1 - 1), NZ, LANES)]
    g0, d0, f0, v0, g1, d1, f1, *down = call(
        first_down_kernel,
        [fine, fine[1:], fine[1:], fine, mid, (R1 + 6, NZ, LANES), (R1 + 6, NZ, LANES), mid, *sends],
        [fine, mid],
        position,
        own,
        swap(first, "gx", True),
        swap(second, "gx", False),
        scalars=1,
    )

    def coarse(v1, packed, edge):
        near = [swap(packed, "gx", first, 2) for first in (True, False)]
        far = [swap(near[1], "gx", True, 2), swap(near[0], "gx", False, 2)]
        mine = jnp.concatenate([packed, *near, *far, edge])
        two, three = (C, 20, NZ, LANES), (C, 10, NZ, LANES)
        out, first, second = call(
            coarse_kernel,
            [(C, R1, NZ, LANES)] + [(C, R1 - 1, NZ, LANES)] * 2,
            [two, two[1:], two[1:], three, three[1:], three[1:], two, two, three, three],
            position,
            mine,
            swap(mine, "gx", True),
            v1,
            scalars=1,
        )
        return out, first, swap(second, "gx", False)

    middle = (C, R1 + 6, NZ, LANES)
    reach = HALO + 1
    field, first, second = call(
        first_up_kernel,
        [(C, rows, NZ, LANES), (C, reach, NZ, LANES), (C, reach, NZ, LANES)],
        [middle, middle, middle, fine, fine],
        position,
        *coarse(*down),
        g0,
        f0,
        v0,
        g1,
        f1,
        scalars=1,
    )
    half = (rows + 2 * reach) // 2
    tall, first, second = call(
        side_kernel,
        [(C, 2 * half, NZ, LANES)] + [(C, half, NZ, LANES)] * 2,
        [],
        position,
        field,
        swap(first, "gx", True),
        swap(second, "gx", False),
        scalars=1,
    )
    v0, g1, *down = call(
        second_down_kernel,
        [fine, mid, mid, *sends],
        [(C, 2 * half, NZ, W), fine, mid],
        position,
        tall,
        swap(first, "gz", True),
        swap(second, "gz", False),
        g0,
        d0,
        f0,
        d1,
        f1,
        scalars=1,
    )
    (sent,) = call(
        last_up_kernel,
        [(blocks, C * depth, rows, LANES)],
        [middle, middle, middle, fine, fine, (C, NZ * rows, LANES)],
        position,
        *coarse(*down),
        g0,
        f0,
        v0,
        g1,
        f1,
        scalars=1,
    )
    (out,) = call(join_kernel, [(C * depth, rows, columns)], [], lax.all_to_all(sent, "gz", 0, 0))
    return out.reshape(right_side.shape)


def solution(mesh):
    return jax.shard_map(
        shards,
        mesh=mesh,
        in_specs=(P(None, "gz", "gx", None), P("gz", "gx", None)),
        out_specs=P(None, "gz", "gx", None),
        check_vma=False,
    )
```

```python
import jax
import jax.numpy as jnp
from jax import lax
from jax.experimental import pallas as pl
from jax.experimental.pallas import tpu as pltpu
from jax.sharding import PartitionSpec as P

relaxation = 0.8
plane_coupling = 16.0
depth_coupling = 1.0
C = 3
NZ = 24
HALO = 6
LANES = 128
UNROLL = (3, 8, 10, 10)
PARAMS = pltpu.CompilerParams(vmem_limit_bytes=12 << 20)


def coupling_of(level):
    return plane_coupling / 4.0**level


def base_of(level):
    return 4.0 * coupling_of(level) + 2.0 * depth_coupling


class Row:
    def __init__(self, base, shift):
        self.base, self.shift = base, shift

    def __add__(self, n):
        return Row(self.base, self.shift + n)

    def __sub__(self, n):
        return self + -n

    def double(self):
        return Row(2 * self.base, 2 * self.shift)


def index(field, r):
    return r.base + (r.shift - field[1]) if isinstance(r, Row) else r - field[1]


def row(field, c, r):
    return field[0][c, index(field, r)]


def shared(field, r):
    return field[0][index(field, r)]


def neighbours(field, c, r, level):
    mid = row(field, c, r)
    width = mid.shape[1]
    lateral = row(field, c, r - 1) + row(field, c, r + 1) + pltpu.roll(mid, 1, 1) + pltpu.roll(mid, width - 1, 1)
    vertical = pltpu.roll(mid, 1, 0) + pltpu.roll(mid, NZ - 1, 0)
    return mid, coupling_of(level) * lateral + depth_coupling * vertical


def each_row(low, high, body, unroll):
    steps = (high - low) // unroll

    def step(n, carry):
        for k in range(unroll):
            body(Row(unroll * n, low + k))
        return carry

    if steps > 1:
        lax.fori_loop(0, steps, step, 0)
        low += steps * unroll
    for r in range(low, high):
        body(Row(0, r))


def sweep(target, field, source, factor, level, low, high):
    def body(r):
        f = shared(factor, r)
        for c in range(C):
            mid, around = neighbours(field, c, r, level)
            target[0][c, index(target, r)] = (1.0 - relaxation) * mid + f * (row(source, c, r) + around)

    each_row(low, high, body, UNROLL[level])


def lane_index():
    return lax.broadcasted_iota(jnp.int32, (NZ, LANES), 1)


def take(values, index):
    return jnp.take_along_axis(values, index, axis=1, mode="promise_in_bounds")


def pair_sum(values, period):
    lane = lane_index()
    if values.shape[1] == 2 * LANES:
        even = (2 * lane) % LANES
        halves = [take(h + pltpu.roll(h, LANES - 1, 1), even) for h in (values[:, :LANES], values[:, LANES:])]
        return jnp.where(lane < LANES // 2, halves[0], halves[1])
    return take(values + pltpu.roll(values, LANES - 1, 1), (2 * lane) % period)


def spread(values, period):
    lane = lane_index()
    if period == 2 * LANES:
        return jnp.concatenate([take(values, lane // 2), take(values, LANES // 2 + lane // 2)], axis=1)
    return take(values, (lane % period) // 2)


def coarse_source(target, field, source, density, level, period, low, high):
    def body(q):
        for c in range(C):
            total = None
            for r in (q.double(), q.double() + 1):
                mid, around = neighbours(field, c, r, level)
                residual = row(source, c, r) + around - (shared(density, r) + base_of(level)) * mid
                total = residual if total is None else total + residual
            target[0][c, index(target, q)] = 0.25 * pair_sum(total, period)

    each_row(low, high, body, (UNROLL[level] + 1) // 2)


def from_zero(target, source, density, factor, level, period, rows, position, low, high, finer=None, reach=0, group=1):
    i, j, count_x, count_y = position[0] // group, position[1], position[2] // group, position[3]
    width = factor[0].shape[-1]
    lane = lax.broadcasted_iota(jnp.int32, (NZ, width), 1) % period
    inside_y = ((lane < 3 * period // 4) | (j > 0)) & ((lane < period // 2) | (lane >= 3 * period // 4) | (j < count_y - 1))

    def body(r):
        if finer is None:
            own = shared(density, r)
        else:
            own = 0.25 * pair_sum(shared(finer, r.double()) + shared(finer, r.double() + 1), 2 * period)
            density[0][index(density, r)] = own
        at = i * rows + r.base
        inside = inside_y & ((at >= -r.shift) & (at < count_x * rows - r.shift))
        f = jnp.where(inside, relaxation / (own + base_of(level)), 0.0)
        factor[0][index(factor, r)] = f
        return f

    def whole(r):
        f = body(r)
        for c in range(C):
            target[0][c, index(target, r)] = f * row(source, c, r)

    for r in [*range(low - reach, low), *range(high, high + reach)]:
        body(Row(0, r))
    each_row(low, high, whole, UNROLL[level])


def first_sweep(target, source, factor, level, low, high):
    def body(r):
        f = shared(factor, r)
        for c in range(C):
            target[0][c, index(target, r)] = f * row(source, c, r)

    each_row(low, high, body, UNROLL[level])


def level_one_down(position, g1, v1, scratch, d1, f1, packed, edge):
    sweep(v1, scratch, g1, f1, 1, -1, 5)
    lane = lane_index()
    for c in range(C + 1):
        pair = []
        for q in (0, 1):
            total = None
            for r in (2 * q, 2 * q + 1):
                if c == C:
                    part = shared(d1, r)
                else:
                    mid, around = neighbours(v1, c, r, 1)
                    part = row(g1, c, r) + around - (shared(d1, r) + base_of(1)) * mid
                total = part if total is None else total + part
            pair.append(0.25 * pair_sum(total, LANES))
        packed[c] = jnp.where(lane < LANES // 2, pair[0], pair[1])
    count = edge.shape[0] // C
    for c in range(C):
        for r in range(count):
            edge[c * count + r] = v1[0][c, (1 - position[4]) + (r - v1[1])]


def by_parity(position, body):
    for odd in range(2):
        pl.when(position[4] == odd)(lambda odd=odd: body(odd))


def rows_to_send(position, own, first, second):
    spare = own.shape[1] - first.shape[1]

    def body(odd):
        for c in range(own.shape[0]):
            for r in range(first.shape[1]):
                first[c, r] = own[c, (1 - odd) * spare + r]
                second[c, r] = own[c, odd * spare + r]

    by_parity(position, body)


def with_halo(position, own, first, second, store):
    rows, halo = own.shape[1], first.shape[1]

    def body(odd):
        for c in range(own.shape[0]):
            for piece, at in ((first, (1 - odd) * (halo + rows)), (second, odd * (halo + rows))):
                for r in range(halo):
                    store(c, at + r, piece[c, r])

    for c in range(own.shape[0]):
        for r in range(rows):
            store(c, halo + r, own[c, r])
    by_parity(position, body)


def pack_kernel(position, source, density, out):
    blocks = out.shape[0]
    for ref, at, n in ((source, 0, source.shape[0]), (density, source.shape[0], density.shape[0])):
        for m in range(n):
            for b in range(blocks):
                out[b, at + m, :, :LANES] = ref[m, :, b * LANES : (b + 1) * LANES]
                zero = jnp.zeros((ref.shape[1], LANES), jnp.float32)
                after = ref[m, :, (b + 1) * LANES : (b + 2) * LANES] if b + 1 < blocks else zero
                before = ref[m, :, (b - 1) * LANES : b * LANES] if b else zero
                lane = lax.broadcasted_iota(jnp.int32, zero.shape, 1)
                out[b, at + m, :, LANES:] = jnp.where(lane < LANES // 2, after, before)


def unpack_kernel(position, taken, own, first, second, scratch):
    blocks, _, rows, _ = taken.shape
    depth = NZ // blocks
    for c in range(C + 1):
        for b in range(blocks):
            for z in range(depth):
                at = (b * depth + z) * rows
                for h in range(2):
                    scratch[c, h, at : at + rows] = taken[b, c * depth + z, :, h * LANES : (h + 1) * LANES]
    for c in range(C + 1):
        for r in range(rows):
            for h in range(2):
                part = scratch[c, h, pl.ds(r, NZ, stride=rows), :]
                lanes = slice(h * LANES, (h + 1) * LANES)
                own[c, r, :, lanes] = part
    rows_to_send(position, own, first, second)


def first_down_kernel(position, own, second, first, g0, d0, f0, v0, g1, d1, f1, v1, packed, edge, field, field1):
    rows = own.shape[1]

    def store(c, at, value):
        if c < C:
            g0[c, at] = value
        else:
            d0[at] = value

    with_halo(position, own, first, second, store)
    g, d, f, a, b = (g0, -HALO), (d0, -HALO), (f0, -HALO), (field, -HALO), (v0, -HALO)
    from_zero(a, g, d, f, 0, 2 * LANES, rows, position, -HALO, rows + HALO)
    sweep(b, a, g, f, 0, -5, rows + 5)
    coarse_source((g1, -2), b, g, d, 0, 2 * LANES, -2, rows // 2 + 2)
    from_zero((field1, -2), (g1, -2), (d1, -3), (f1, -3), 1, LANES, rows // 2, position, -2, rows // 2 + 2, d, 1)
    level_one_down(position, (g1, -2), (v1, -2), (field1, -2), (d1, -3), (f1, -3), packed, edge)


def side_kernel(position, own, second, first, tall, to_first, to_second):
    half = tall.shape[1] // 2
    low = (lane_index() < LANES // 2) == (position[5] == 1)

    def store(c, at, value):
        tall[c, at] = value

    with_halo(position, own, first, second, store)
    for c in range(C):
        for r in range(half):
            one, two = tall[c, r], pltpu.roll(tall[c, r + half], LANES // 2, 1)
            to_first[c, r] = jnp.where(low, one, two)
            to_second[c, r] = jnp.where(low, two, one)


def second_down_kernel(position, tall, first, second, g0, d0, f0, d1, f1, v0, g1, v1, packed, edge, wide, field, field1):
    half = tall.shape[1] // 2
    halo = half - v0.shape[1] // 2 + HALO
    rows = 2 * (half - halo)
    low = (lane_index() < LANES // 2) == (position[5] == 0)
    for c in range(C):
        for r in range(2 * half):
            wide[c, r, :, :LANES] = tall[c, r]
        for r in range(half):
            wide[c, r, :, LANES:] = jnp.where(low, first[c, r], second[c, r])
            wide[c, r + half, :, LANES:] = pltpu.roll(jnp.where(low, second[c, r], first[c, r]), LANES // 2, 1)
    g, d, f, a, b = (g0, -HALO), (d0, -HALO), (f0, -HALO), (field, -HALO), (v0, -HALO)
    sweep(a, (wide, -halo), g, f, 0, -6, rows + 6)
    sweep(b, a, g, f, 0, -5, rows + 5)
    coarse_source((g1, -2), b, g, d, 0, 2 * LANES, -2, rows // 2 + 2)
    first_sweep((field1, -2), (g1, -2), (f1, -3), 1, -2, rows // 2 + 2)
    level_one_down(position, (g1, -2), (v1, -2), (field1, -2), (d1, -3), (f1, -3), packed, edge)


def coarse_kernel(position, mine, other, v1, out, first, second, g2, d2, f2, g3, d3, f3, a, b, a3, b3):
    lane = lane_index()
    odd, step = position[4], 1 - 2 * position[6]
    count, reach = first.shape[1], 8
    units = C + 1

    for ref, core in ((mine, odd), (other, 1 - odd)):
        for n, away in enumerate((0, step, -step, 2 * step, -2 * step)):
            at = 4 * away + (2 * core + reach)
            for c in range(units):
                both = ref[n * units + c]
                twin = pltpu.roll(both, LANES // 2, 1)
                for q, value in ((0, jnp.where(lane < LANES // 2, both, twin)), (1, jnp.where(lane < LANES // 2, twin, both))):
                    if c < C:
                        g2[c, at + q] = value
                    else:
                        d2[at + q] = value
    g, d, f, u, w = (g2, -reach), (d2, -reach), (f2, -reach), (a, -reach), (b, -reach)
    h, e, k, s, t = (g3, -reach // 2), (d3, -reach // 2), (f3, -reach // 2), (a3, -reach // 2), (b3, -reach // 2)
    from_zero(u, g, d, f, 2, LANES // 2, 4, position, -8, 12, group=2)
    sweep(w, u, g, f, 2, -7, 11)
    coarse_source(h, w, g, d, 2, LANES // 2, -3, 5)
    from_zero(s, h, e, k, 3, LANES // 4, 2, position, -3, 5, d, group=2)
    sweep(t, s, h, k, 3, -2, 4)
    sweep(s, t, h, k, 3, -1, 3)

    def correct(q):
        for c in range(C):
            fine = spread(row(s, c, q), LANES // 2)
            for r in (q.double(), q.double() + 1):
                b[c, index(w, r)] = row(w, c, r) + fine

    each_row(-1, 3, correct, 4)
    sweep(u, w, g, f, 2, -1, 5)
    sweep(w, u, g, f, 2, 0, 4)
    for c in range(C):
        for q in (0, 1):
            fine = spread(b[c, 2 * odd + (q + reach)], LANES)
            for r in (2 * q, 2 * q + 1):
                out[c, r] = v1[c, r + 2] + fine
        for r, q in enumerate((0, odd, 1)):
            fine = spread(b[c, 2 * (1 - odd) + (reach + q)], LANES)
            first[c, r] = other[5 * units + c * count + r] + fine
        for r in range(count):
            second[c, r] = out[c, odd * (out.shape[1] - count) + r]


def climb(position, own, first, second, g0, f0, v0, g1, f1, wide, u, w, field, emit):
    rows1, halo = own.shape[1], first.shape[1]

    def store(c, at, value):
        wide[c, at] = value

    with_halo(position, own, first, second, store)
    sweep((u, -3), (wide, -halo), (g1, -2), (f1, -3), 1, -2, rows1 + 2)
    sweep((w, -3), (u, -3), (g1, -2), (f1, -3), 1, -1, rows1 + 1)

    def correct(q):
        for c in range(C):
            fine = spread(row((w, -3), c, q), 2 * LANES)
            for r in (q.double(), q.double() + 1):
                field[c, index((field, -HALO), r)] = row((v0, -HALO), c, r) + fine

    each_row(-1, rows1 + 1, correct, 2)
    rows = 2 * rows1
    sweep((emit, -HALO), (field, -HALO), (g0, -HALO), (f0, -HALO), 0, -1, rows + 1)
    sweep((field, -HALO), (emit, -HALO), (g0, -HALO), (f0, -HALO), 0, 0, rows)


def first_up_kernel(position, own, left, right, g0, f0, v0, g1, f1, out, first, second, wide, u, w, field, other):
    climb(position, own, left, right, g0, f0, v0, g1, f1, wide, u, w, field, other)
    for c in range(C):
        for r in range(out.shape[1]):
            out[c, r] = field[c, r + HALO, :, :LANES]
    rows_to_send(position, out, first, second)


def last_up_kernel(position, own, left, right, g0, f0, v0, g1, f1, out, wide, u, w, field, other, scratch):
    climb(position, own, left, right, g0, f0, v0, g1, f1, wide, u, w, field, other)
    blocks, _, rows, _ = out.shape
    depth = NZ // blocks
    for c in range(C):
        for r in range(rows):
            scratch[c, pl.ds(r, NZ, stride=rows), :] = field[c, r + HALO, :, :LANES]
    for c in range(C):
        for z in range(NZ):
            out[z // depth, c * depth + z % depth] = scratch[c, z * rows : (z + 1) * rows]


def join_kernel(taken, out):
    for b in range(taken.shape[0]):
        out[:, :, b * LANES : (b + 1) * LANES] = taken[b]


def call(kernel, outs, scratch, *args, scalars=0):
    shape = lambda s: jax.ShapeDtypeStruct(s, jnp.float32)
    specs = [pl.BlockSpec(memory_space=pltpu.SMEM)] * scalars + [pl.BlockSpec(memory_space=pltpu.VMEM)] * (len(args) - scalars)
    out = pl.pallas_call(
        kernel,
        out_shape=[shape(s) for s in outs],
        in_specs=specs,
        out_specs=[pl.BlockSpec(memory_space=pltpu.VMEM)] * len(outs),
        scratch_shapes=[pltpu.VMEM(s, jnp.float32) for s in scratch],
        compiler_params=PARAMS,
        name=kernel.__name__,
    )(*args)
    return out


def swap(values, axis, first, unit=1):
    count, pairs = lax.axis_size(axis), []
    for i in range(count):
        group = i // unit
        other = group ^ 1 if first else ((group - 1) ^ 1) + 1
        if 0 <= other < count // unit:
            pairs.append((i, other * unit + i % unit))
    return lax.ppermute(values, axis, pairs)


def shards(right_side, density):
    blocks = lax.axis_size("gz")
    depth, rows, columns = density.shape
    i, j = lax.axis_index("gx"), lax.axis_index("gz")
    position = jnp.stack([i, j, lax.axis_size("gx"), blocks, i % 2, j % 2, i // 2 % 2]).astype(jnp.int32)
    W, R0, R1 = 2 * LANES, rows + 2 * HALO, rows // 2

    (sent,) = call(pack_kernel, [(blocks, (C + 1) * depth, rows, W)], [], position, right_side.reshape(C * depth, rows, columns), density, scalars=1)
    taken = lax.all_to_all(sent, "gz", 0, 0)
    own, first, second = call(
        unpack_kernel,
        [(C + 1, rows, NZ, W), (C + 1, HALO, NZ, W), (C + 1, HALO, NZ, W)],
        [(C + 1, 2, NZ * rows, LANES)],
        position,
        taken,
        scalars=1,
    )
    fine, mid = (C, R0, NZ, W), (C, R1 + 4, NZ, LANES)
    sends = [(C + 1, NZ, LANES), (C * (R1 - 1), NZ, LANES)]
    g0, d0, f0, v0, g1, d1, f1, *down = call(
        first_down_kernel,
        [fine, fine[1:], fine[1:], fine, mid, (R1 + 6, NZ, LANES), (R1 + 6, NZ, LANES), mid, *sends],
        [fine, mid],
        position,
        own,
        swap(second, "gx", False),
        swap(first, "gx", True),
        scalars=1,
    )

    def coarse(v1, packed, edge):
        near = [swap(packed, "gx", first, 2) for first in (True, False)]
        far = [swap(near[1], "gx", True, 2), swap(near[0], "gx", False, 2)]
        mine = jnp.concatenate([packed, *near, *far, edge])
        two, three = (C, 20, NZ, LANES), (C, 10, NZ, LANES)
        out, first, second = call(
            coarse_kernel,
            [(C, R1, NZ, LANES)] + [(C, R1 - 1, NZ, LANES)] * 2,
            [two, two[1:], two[1:], three, three[1:], three[1:], two, two, three, three],
            position,
            mine,
            swap(mine, "gx", True),
            v1,
            scalars=1,
        )
        return out, first, swap(second, "gx", False)

    middle = (C, R1 + 6, NZ, LANES)
    reach = HALO + 1
    field, first, second = call(
        first_up_kernel,
        [(C, rows, NZ, LANES), (C, reach, NZ, LANES), (C, reach, NZ, LANES)],
        [middle, middle, middle, fine, fine],
        position,
        *coarse(*down),
        g0,
        f0,
        v0,
        g1,
        f1,
        scalars=1,
    )
    half = (rows + 2 * reach) // 2
    tall, first, second = call(
        side_kernel,
        [(C, 2 * half, NZ, LANES)] + [(C, half, NZ, LANES)] * 2,
        [],
        position,
        field,
        swap(second, "gx", False),
        swap(first, "gx", True),
        scalars=1,
    )
    v0, g1, *down = call(
        second_down_kernel,
        [fine, mid, mid, *sends],
        [(C, 2 * half, NZ, W), fine, mid],
        position,
        tall,
        swap(first, "gz", True),
        swap(second, "gz", False),
        g0,
        d0,
        f0,
        d1,
        f1,
        scalars=1,
    )
    (sent,) = call(
        last_up_kernel,
        [(blocks, C * depth, rows, LANES)],
        [middle, middle, middle, fine, fine, (C, NZ * rows, LANES)],
        position,
        *coarse(*down),
        g0,
        f0,
        v0,
        g1,
        f1,
        scalars=1,
    )
    (out,) = call(join_kernel, [(C * depth, rows, columns)], [], lax.all_to_all(sent, "gz", 0, 0))
    return out.reshape(right_side.shape)


def solution(mesh):
    return jax.shard_map(
        shards,
        mesh=mesh,
        in_specs=(P(None, "gz", "gx", None), P("gz", "gx", None)),
        out_specs=P(None, "gz", "gx", None),
        check_vma=False,
    )
```

```python
import jax
import jax.numpy as jnp
from jax import lax
from jax.experimental import pallas as pl
from jax.experimental.pallas import tpu as pltpu
from jax.sharding import PartitionSpec as P

relaxation = 0.8
plane_coupling = 16.0
depth_coupling = 1.0
C = 3
NZ = 24
HALO = 6
LANES = 128
UNROLL = (3, 4, 8, 8)
PARAMS = pltpu.CompilerParams(vmem_limit_bytes=12 << 20)


def coupling_of(level):
    return plane_coupling / 4.0**level


def base_of(level):
    return 4.0 * coupling_of(level) + 2.0 * depth_coupling


class Row:
    def __init__(self, base, shift):
        self.base, self.shift = base, shift

    def __add__(self, n):
        return Row(self.base, self.shift + n)

    def __sub__(self, n):
        return self + -n

    def double(self):
        return Row(2 * self.base, 2 * self.shift)


def index(field, r):
    return r.base + (r.shift - field[1]) if isinstance(r, Row) else r - field[1]


def row(field, c, r):
    return field[0][c, index(field, r)]


def shared(field, r):
    return field[0][index(field, r)]


def neighbours(field, c, r, level):
    mid = row(field, c, r)
    width = mid.shape[1]
    lateral = row(field, c, r - 1) + row(field, c, r + 1) + pltpu.roll(mid, 1, 1) + pltpu.roll(mid, width - 1, 1)
    vertical = pltpu.roll(mid, 1, 0) + pltpu.roll(mid, NZ - 1, 0)
    return mid, coupling_of(level) * lateral + depth_coupling * vertical


def each_row(low, high, body, unroll):
    steps = (high - low) // unroll

    def step(n, carry):
        for k in range(unroll):
            body(Row(unroll * n, low + k))
        return carry

    if steps > 1:
        lax.fori_loop(0, steps, step, 0)
        low += steps * unroll
    for r in range(low, high):
        body(Row(0, r))


def sweep(target, field, source, factor, level, low, high):
    def body(r):
        f = shared(factor, r)
        for c in range(C):
            mid, around = neighbours(field, c, r, level)
            target[0][c, index(target, r)] = (1.0 - relaxation) * mid + f * (row(source, c, r) + around)

    each_row(low, high, body, UNROLL[level])


def lane_index():
    return lax.broadcasted_iota(jnp.int32, (NZ, LANES), 1)


def take(values, index):
    return jnp.take_along_axis(values, index, axis=1, mode="promise_in_bounds")


def pair_sum(values, period):
    lane = lane_index()
    if values.shape[1] == 2 * LANES:
        even = (2 * lane) % LANES
        halves = [take(h + pltpu.roll(h, LANES - 1, 1), even) for h in (values[:, :LANES], values[:, LANES:])]
        return jnp.where(lane < LANES // 2, halves[0], halves[1])
    return take(values + pltpu.roll(values, LANES - 1, 1), (2 * lane) % period)


def spread(values, period):
    lane = lane_index()
    if period == 2 * LANES:
        return jnp.concatenate([take(values, lane // 2), take(values, LANES // 2 + lane // 2)], axis=1)
    return take(values, (lane % period) // 2)


def coarse_source(target, field, source, density, level, period, low, high):
    def body(q):
        for c in range(C):
            total = None
            for r in (q.double(), q.double() + 1):
                mid, around = neighbours(field, c, r, level)
                residual = row(source, c, r) + around - (shared(density, r) + base_of(level)) * mid
                total = residual if total is None else total + residual
            target[0][c, index(target, q)] = 0.25 * pair_sum(total, period)

    each_row(low, high, body, max(1, UNROLL[level] // 2))


def from_zero(target, source, density, factor, level, period, rows, position, low, high, finer=None, reach=0, group=1):
    i, j, count_x, count_y = position[0] // group, position[1], position[2] // group, position[3]
    width = factor[0].shape[-1]
    lane = lax.broadcasted_iota(jnp.int32, (NZ, width), 1) % period
    inside_y = ((lane < 3 * period // 4) | (j > 0)) & ((lane < period // 2) | (lane >= 3 * period // 4) | (j < count_y - 1))

    def body(r):
        if finer is None:
            own = shared(density, r)
        else:
            own = 0.25 * pair_sum(shared(finer, r.double()) + shared(finer, r.double() + 1), 2 * period)
            density[0][index(density, r)] = own
        at = i * rows + r.base
        inside = inside_y & ((at >= -r.shift) & (at < count_x * rows - r.shift))
        f = jnp.where(inside, relaxation / (own + base_of(level)), 0.0)
        factor[0][index(factor, r)] = f
        return f

    def whole(r):
        f = body(r)
        for c in range(C):
            target[0][c, index(target, r)] = f * row(source, c, r)

    for r in [*range(low - reach, low), *range(high, high + reach)]:
        body(Row(0, r))
    each_row(low, high, whole, UNROLL[level])


def first_sweep(target, source, factor, level, low, high):
    def body(r):
        f = shared(factor, r)
        for c in range(C):
            target[0][c, index(target, r)] = f * row(source, c, r)

    each_row(low, high, body, UNROLL[level])


def level_one_down(position, g1, v1, scratch, d1, f1, packed, edge):
    sweep(v1, scratch, g1, f1, 1, -1, 5)
    lane = lane_index()
    for c in range(C + 1):
        pair = []
        for q in (0, 1):
            total = None
            for r in (2 * q, 2 * q + 1):
                if c == C:
                    part = shared(d1, r)
                else:
                    mid, around = neighbours(v1, c, r, 1)
                    part = row(g1, c, r) + around - (shared(d1, r) + base_of(1)) * mid
                total = part if total is None else total + part
            pair.append(0.25 * pair_sum(total, LANES))
        packed[c] = jnp.where(lane < LANES // 2, pair[0], pair[1])
    count = edge.shape[0] // C
    for c in range(C):
        for r in range(count):
            edge[c * count + r] = v1[0][c, (1 - position[4]) + (r - v1[1])]


def own_position():
    i, j = lax.axis_index("gx"), lax.axis_index("gz")
    return i, j, lax.axis_size("gx"), lax.axis_size("gz"), i % 2, j % 2, i // 2 % 2


def by_parity(position, body):
    for odd in range(2):
        pl.when(position[4] == odd)(lambda odd=odd: body(odd))


def rows_to_send(position, own, first, second):
    spare = own.shape[1] - first.shape[1]

    def body(odd):
        for c in range(own.shape[0]):
            for r in range(first.shape[1]):
                first[c, r] = own[c, (1 - odd) * spare + r]
                second[c, r] = own[c, odd * spare + r]

    by_parity(position, body)


def with_halo(position, own, first, second, store):
    rows, halo = own.shape[1], first.shape[1]

    def body(odd):
        for c in range(own.shape[0]):
            for piece, at in ((first, (1 - odd) * (halo + rows)), (second, odd * (halo + rows))):
                for r in range(halo):
                    store(c, at + r, piece[c, r])

    for c in range(own.shape[0]):
        for r in range(rows):
            store(c, halo + r, own[c, r])
    by_parity(position, body)


def pack_kernel(source, density, out):
    blocks = out.shape[0]
    for ref, at, n in ((source, 0, source.shape[0]), (density, source.shape[0], density.shape[0])):
        for m in range(n):
            for b in range(blocks):
                out[b, at + m, :, :LANES] = ref[m, :, b * LANES : (b + 1) * LANES]
                zero = jnp.zeros((ref.shape[1], LANES), jnp.float32)
                after = ref[m, :, (b + 1) * LANES : (b + 2) * LANES] if b + 1 < blocks else zero
                before = ref[m, :, (b - 1) * LANES : b * LANES] if b else zero
                lane = lax.broadcasted_iota(jnp.int32, zero.shape, 1)
                out[b, at + m, :, LANES:] = jnp.where(lane < LANES // 2, after, before)


def unpack_kernel(taken, own, first, second, scratch):
    position = own_position()
    blocks, _, rows, _ = taken.shape
    depth = NZ // blocks
    for c in range(C + 1):
        for b in range(blocks):
            for z in range(depth):
                at = (b * depth + z) * rows
                for h in range(2):
                    scratch[c, h, at : at + rows] = taken[b, c * depth + z, :, h * LANES : (h + 1) * LANES]
    for c in range(C + 1):
        for r in range(rows):
            for h in range(2):
                part = scratch[c, h, pl.ds(r, NZ, stride=rows), :]
                lanes = slice(h * LANES, (h + 1) * LANES)
                own[c, r, :, lanes] = part
    rows_to_send(position, own, first, second)


def first_down_kernel(own, second, first, g0, d0, f0, v0, g1, d1, f1, v1, packed, edge, field, field1):
    position = own_position()
    rows = own.shape[1]

    def store(c, at, value):
        if c < C:
            g0[c, at] = value
        else:
            d0[at] = value

    with_halo(position, own, first, second, store)
    g, d, f, a, b = (g0, -HALO), (d0, -HALO), (f0, -HALO), (field, -HALO), (v0, -HALO)
    from_zero(a, g, d, f, 0, 2 * LANES, rows, position, -HALO, rows + HALO)
    sweep(b, a, g, f, 0, -5, rows + 5)
    coarse_source((g1, -2), b, g, d, 0, 2 * LANES, -2, rows // 2 + 2)
    from_zero((field1, -2), (g1, -2), (d1, -3), (f1, -3), 1, LANES, rows // 2, position, -2, rows // 2 + 2, d, 1)
    level_one_down(position, (g1, -2), (v1, -2), (field1, -2), (d1, -3), (f1, -3), packed, edge)


def side_kernel(own, second, first, tall, to_first, to_second):
    position = own_position()
    half = tall.shape[1] // 2
    low = (lane_index() < LANES // 2) == (position[5] == 1)

    def store(c, at, value):
        tall[c, at] = value

    with_halo(position, own, first, second, store)
    for c in range(C):
        for r in range(half):
            one, two = tall[c, r], pltpu.roll(tall[c, r + half], LANES // 2, 1)
            to_first[c, r] = jnp.where(low, one, two)
            to_second[c, r] = jnp.where(low, two, one)


def second_down_kernel(tall, first, second, g0, d0, f0, d1, f1, v0, g1, v1, packed, edge, wide, field, field1):
    position = own_position()
    half = tall.shape[1] // 2
    halo = half - v0.shape[1] // 2 + HALO
    rows = 2 * (half - halo)
    low = (lane_index() < LANES // 2) == (position[5] == 0)
    for c in range(C):
        for r in range(2 * half):
            wide[c, r, :, :LANES] = tall[c, r]
        for r in range(half):
            wide[c, r, :, LANES:] = jnp.where(low, first[c, r], second[c, r])
            wide[c, r + half, :, LANES:] = pltpu.roll(jnp.where(low, second[c, r], first[c, r]), LANES // 2, 1)
    g, d, f, a, b = (g0, -HALO), (d0, -HALO), (f0, -HALO), (field, -HALO), (v0, -HALO)
    sweep(a, (wide, -halo), g, f, 0, -6, rows + 6)
    sweep(b, a, g, f, 0, -5, rows + 5)
    coarse_source((g1, -2), b, g, d, 0, 2 * LANES, -2, rows // 2 + 2)
    first_sweep((field1, -2), (g1, -2), (f1, -3), 1, -2, rows // 2 + 2)
    level_one_down(position, (g1, -2), (v1, -2), (field1, -2), (d1, -3), (f1, -3), packed, edge)


def coarse_kernel(mine, other, v1, out, first, second, g2, d2, f2, g3, d3, f3, a, b, a3, b3):
    position = own_position()
    lane = lane_index()
    odd, step = position[4], 1 - 2 * position[6]
    count, reach = first.shape[1], 8
    units = C + 1

    for ref, core in ((mine, odd), (other, 1 - odd)):
        for n, away in enumerate((0, step, -step, 2 * step, -2 * step)):
            at = 4 * away + (2 * core + reach)
            for c in range(units):
                both = ref[n * units + c]
                twin = pltpu.roll(both, LANES // 2, 1)
                for q, value in ((0, jnp.where(lane < LANES // 2, both, twin)), (1, jnp.where(lane < LANES // 2, twin, both))):
                    if c < C:
                        g2[c, at + q] = value
                    else:
                        d2[at + q] = value
    g, d, f, u, w = (g2, -reach), (d2, -reach), (f2, -reach), (a, -reach), (b, -reach)
    h, e, k, s, t = (g3, -reach // 2), (d3, -reach // 2), (f3, -reach // 2), (a3, -reach // 2), (b3, -reach // 2)
    from_zero(u, g, d, f, 2, LANES // 2, 4, position, -8, 12, group=2)
    sweep(w, u, g, f, 2, -7, 11)
    coarse_source(h, w, g, d, 2, LANES // 2, -3, 5)
    from_zero(s, h, e, k, 3, LANES // 4, 2, position, -3, 5, d, group=2)
    sweep(t, s, h, k, 3, -2, 4)
    sweep(s, t, h, k, 3, -1, 3)

    def correct(q):
        for c in range(C):
            fine = spread(row(s, c, q), LANES // 2)
            for r in (q.double(), q.double() + 1):
                b[c, index(w, r)] = row(w, c, r) + fine

    each_row(-1, 3, correct, 4)
    sweep(u, w, g, f, 2, -1, 5)
    sweep(w, u, g, f, 2, 0, 4)
    for c in range(C):
        for q in (0, 1):
            fine = spread(b[c, 2 * odd + (q + reach)], LANES)
            for r in (2 * q, 2 * q + 1):
                out[c, r] = v1[c, r + 2] + fine
        for r, q in enumerate((0, odd, 1)):
            fine = spread(b[c, 2 * (1 - odd) + (reach + q)], LANES)
            first[c, r] = other[5 * units + c * count + r] + fine
        for r in range(count):
            second[c, r] = out[c, odd * (out.shape[1] - count) + r]


def climb(position, own, first, second, g0, f0, v0, g1, f1, wide, u, w, field, emit):
    rows1, halo = own.shape[1], first.shape[1]

    def store(c, at, value):
        wide[c, at] = value

    with_halo(position, own, first, second, store)
    sweep((u, -3), (wide, -halo), (g1, -2), (f1, -3), 1, -2, rows1 + 2)
    sweep((w, -3), (u, -3), (g1, -2), (f1, -3), 1, -1, rows1 + 1)

    def correct(q):
        for c in range(C):
            fine = spread(row((w, -3), c, q), 2 * LANES)
            for r in (q.double(), q.double() + 1):
                field[c, index((field, -HALO), r)] = row((v0, -HALO), c, r) + fine

    each_row(-1, rows1 + 1, correct, 2)
    rows = 2 * rows1
    sweep((emit, -HALO), (field, -HALO), (g0, -HALO), (f0, -HALO), 0, -1, rows + 1)
    sweep((field, -HALO), (emit, -HALO), (g0, -HALO), (f0, -HALO), 0, 0, rows)


def first_up_kernel(own, left, right, g0, f0, v0, g1, f1, out, first, second, wide, u, w, field, other):
    position = own_position()
    climb(position, own, left, right, g0, f0, v0, g1, f1, wide, u, w, field, other)
    for c in range(C):
        for r in range(out.shape[1]):
            out[c, r] = field[c, r + HALO, :, :LANES]
    rows_to_send(position, out, first, second)


def last_up_kernel(own, left, right, g0, f0, v0, g1, f1, out, wide, u, w, field, other, scratch):
    position = own_position()
    climb(position, own, left, right, g0, f0, v0, g1, f1, wide, u, w, field, other)
    blocks, _, rows, _ = out.shape
    depth = NZ // blocks
    for c in range(C):
        for r in range(rows):
            scratch[c, pl.ds(r, NZ, stride=rows), :] = field[c, r + HALO, :, :LANES]
    for c in range(C):
        for z in range(NZ):
            out[z // depth, c * depth + z % depth] = scratch[c, z * rows : (z + 1) * rows]


def join_kernel(taken, out):
    for b in range(taken.shape[0]):
        out[:, :, b * LANES : (b + 1) * LANES] = taken[b]


def call(kernel, outs, scratch, *args):
    shape = lambda s: jax.ShapeDtypeStruct(s, jnp.float32)
    out = pl.pallas_call(
        kernel,
        out_shape=[shape(s) for s in outs],
        in_specs=[pl.BlockSpec(memory_space=pltpu.VMEM)] * len(args),
        out_specs=[pl.BlockSpec(memory_space=pltpu.VMEM)] * len(outs),
        scratch_shapes=[pltpu.VMEM(s, jnp.float32) for s in scratch],
        compiler_params=PARAMS,
        name=kernel.__name__,
    )(*args)
    return out


def swap(values, axis, first, unit=1):
    count, pairs = lax.axis_size(axis), []
    for i in range(count):
        group = i // unit
        other = group ^ 1 if first else ((group - 1) ^ 1) + 1
        if 0 <= other < count // unit:
            pairs.append((i, other * unit + i % unit))
    return lax.ppermute(values, axis, pairs)


def shards(right_side, density):
    blocks = lax.axis_size("gz")
    depth, rows, columns = density.shape
    W, R0, R1 = 2 * LANES, rows + 2 * HALO, rows // 2

    (sent,) = call(pack_kernel, [(blocks, (C + 1) * depth, rows, W)], [], right_side.reshape(C * depth, rows, columns), density)
    taken = lax.all_to_all(sent, "gz", 0, 0)
    own, first, second = call(
        unpack_kernel,
        [(C + 1, rows, NZ, W), (C + 1, HALO, NZ, W), (C + 1, HALO, NZ, W)],
        [(C + 1, 2, NZ * rows, LANES)],
        taken,
    )
    fine, mid = (C, R0, NZ, W), (C, R1 + 4, NZ, LANES)
    sends = [(C + 1, NZ, LANES), (C * (R1 - 1), NZ, LANES)]
    g0, d0, f0, v0, g1, d1, f1, *down = call(
        first_down_kernel,
        [fine, fine[1:], fine[1:], fine, mid, (R1 + 6, NZ, LANES), (R1 + 6, NZ, LANES), mid, *sends],
        [fine, mid],
        own,
        swap(second, "gx", False),
        swap(first, "gx", True),
    )

    def coarse(v1, packed, edge):
        near = [swap(packed, "gx", first, 2) for first in (True, False)]
        far = [swap(near[1], "gx", True, 2), swap(near[0], "gx", False, 2)]
        mine = jnp.concatenate([packed, *near, *far, edge])
        two, three = (C, 20, NZ, LANES), (C, 10, NZ, LANES)
        out, first, second = call(
            coarse_kernel,
            [(C, R1, NZ, LANES)] + [(C, R1 - 1, NZ, LANES)] * 2,
            [two, two[1:], two[1:], three, three[1:], three[1:], two, two, three, three],
                mine,
            swap(mine, "gx", True),
            v1,
        )
        return out, first, swap(second, "gx", False)

    middle = (C, R1 + 6, NZ, LANES)
    reach = HALO + 1
    field, first, second = call(
        first_up_kernel,
        [(C, rows, NZ, LANES), (C, reach, NZ, LANES), (C, reach, NZ, LANES)],
        [middle, middle, middle, fine, fine],
        *coarse(*down),
        g0,
        f0,
        v0,
        g1,
        f1,
    )
    half = (rows + 2 * reach) // 2
    tall, first, second = call(
        side_kernel,
        [(C, 2 * half, NZ, LANES)] + [(C, half, NZ, LANES)] * 2,
        [],
        field,
        swap(second, "gx", False),
        swap(first, "gx", True),
    )
    v0, g1, *down = call(
        second_down_kernel,
        [fine, mid, mid, *sends],
        [(C, 2 * half, NZ, W), fine, mid],
        tall,
        swap(first, "gz", True),
        swap(second, "gz", False),
        g0,
        d0,
        f0,
        d1,
        f1,
    )
    (sent,) = call(
        last_up_kernel,
        [(blocks, C * depth, rows, LANES)],
        [middle, middle, middle, fine, fine, (C, NZ * rows, LANES)],
        *coarse(*down),
        g0,
        f0,
        v0,
        g1,
        f1,
    )
    (out,) = call(join_kernel, [(C * depth, rows, columns)], [], lax.all_to_all(sent, "gz", 0, 0))
    return out.reshape(right_side.shape)


def solution(mesh):
    return jax.shard_map(
        shards,
        mesh=mesh,
        in_specs=(P(None, "gz", "gx", None), P("gz", "gx", None)),
        out_specs=P(None, "gz", "gx", None),
        check_vma=False,
    )
```

```python
import jax
import jax.numpy as jnp
from jax import lax
from jax.experimental import pallas as pl
from jax.experimental.pallas import tpu as pltpu
from jax.sharding import PartitionSpec as P

relaxation = 0.8
plane_coupling = 16.0
depth_coupling = 1.0
C = 3
NZ = 24
HALO = 6
LANES = 128
UNROLL = (3, 4, 8, 8)
PARAMS = pltpu.CompilerParams(vmem_limit_bytes=12 << 20)


def coupling_of(level):
    return plane_coupling / 4.0**level


def base_of(level):
    return 4.0 * coupling_of(level) + 2.0 * depth_coupling


class Row:
    def __init__(self, base, shift):
        self.base, self.shift = base, shift

    def __add__(self, n):
        return Row(self.base, self.shift + n)

    def __sub__(self, n):
        return self + -n

    def double(self):
        return Row(2 * self.base, 2 * self.shift)


def index(field, r):
    return r.base + (r.shift - field[1]) if isinstance(r, Row) else r - field[1]


def row(field, c, r):
    return field[0][c, index(field, r)]


def shared(field, r):
    return field[0][index(field, r)]


def neighbours(field, c, r, level):
    mid = row(field, c, r)
    width = mid.shape[1]
    lateral = row(field, c, r - 1) + row(field, c, r + 1) + pltpu.roll(mid, 1, 1) + pltpu.roll(mid, width - 1, 1)
    vertical = pltpu.roll(mid, 1, 0) + pltpu.roll(mid, NZ - 1, 0)
    return mid, coupling_of(level) * lateral + depth_coupling * vertical


def each_row(low, high, body, unroll):
    steps = (high - low) // unroll

    def step(n, carry):
        for k in range(unroll):
            body(Row(unroll * n, low + k))
        return carry

    if steps > 1:
        lax.fori_loop(0, steps, step, 0)
        low += steps * unroll
    for r in range(low, high):
        body(Row(0, r))


def sweep(target, field, source, factor, level, low, high):
    def body(r):
        f = shared(factor, r)
        for c in range(C):
            mid, around = neighbours(field, c, r, level)
            target[0][c, index(target, r)] = (1.0 - relaxation) * mid + f * (row(source, c, r) + around)

    each_row(low, high, body, UNROLL[level])


def lane_index():
    return lax.broadcasted_iota(jnp.int32, (NZ, LANES), 1)


def take(values, index):
    return jnp.take_along_axis(values, index, axis=1, mode="promise_in_bounds")


def pair_sum(values, period):
    lane = lane_index()
    if values.shape[1] == 2 * LANES:
        even = (2 * lane) % LANES
        halves = [take(h + pltpu.roll(h, LANES - 1, 1), even) for h in (values[:, :LANES], values[:, LANES:])]
        return jnp.where(lane < LANES // 2, halves[0], halves[1])
    return take(values + pltpu.roll(values, LANES - 1, 1), (2 * lane) % period)


def spread(values, period):
    lane = lane_index()
    if period == 2 * LANES:
        return jnp.concatenate([take(values, lane // 2), take(values, LANES // 2 + lane // 2)], axis=1)
    return take(values, (lane % period) // 2)


def coarse_source(target, field, source, density, level, period, low, high):
    def body(q):
        for c in range(C):
            total = None
            for r in (q.double(), q.double() + 1):
                mid, around = neighbours(field, c, r, level)
                residual = row(source, c, r) + around - (shared(density, r) + base_of(level)) * mid
                total = residual if total is None else total + residual
            target[0][c, index(target, q)] = 0.25 * pair_sum(total, period)

    each_row(low, high, body, max(1, UNROLL[level] // 2))


def from_zero(target, source, density, factor, level, period, rows, position, low, high, finer=None, reach=0, group=1):
    i, j, count_x, count_y = position[0] // group, position[1], position[2] // group, position[3]
    width = factor[0].shape[-1]
    lane = lax.broadcasted_iota(jnp.int32, (NZ, width), 1) % period
    inside_y = ((lane < 3 * period // 4) | (j > 0)) & ((lane < period // 2) | (lane >= 3 * period // 4) | (j < count_y - 1))

    def body(r):
        if finer is None:
            own = shared(density, r)
        else:
            own = 0.25 * pair_sum(shared(finer, r.double()) + shared(finer, r.double() + 1), 2 * period)
            density[0][index(density, r)] = own
        at = i * rows + r.base
        inside = inside_y & ((at >= -r.shift) & (at < count_x * rows - r.shift))
        f = jnp.where(inside, relaxation / (own + base_of(level)), 0.0)
        factor[0][index(factor, r)] = f
        return f

    def whole(r):
        f = body(r)
        for c in range(C):
            target[0][c, index(target, r)] = f * row(source, c, r)

    for r in [*range(low - reach, low), *range(high, high + reach)]:
        body(Row(0, r))
    each_row(low, high, whole, UNROLL[level])


def first_sweep(target, source, factor, level, low, high):
    def body(r):
        f = shared(factor, r)
        for c in range(C):
            target[0][c, index(target, r)] = f * row(source, c, r)

    each_row(low, high, body, UNROLL[level])


def level_one_down(position, g1, v1, scratch, d1, f1, packed, edge):
    sweep(v1, scratch, g1, f1, 1, -1, 5)
    lane = lane_index()
    for c in range(C + 1):
        pair = []
        for q in (0, 1):
            total = None
            for r in (2 * q, 2 * q + 1):
                if c == C:
                    part = shared(d1, r)
                else:
                    mid, around = neighbours(v1, c, r, 1)
                    part = row(g1, c, r) + around - (shared(d1, r) + base_of(1)) * mid
                total = part if total is None else total + part
            pair.append(0.25 * pair_sum(total, LANES))
        packed[c] = jnp.where(lane < LANES // 2, pair[0], pair[1])
    count = edge.shape[0] // C
    for c in range(C):
        for r in range(count):
            edge[c * count + r] = v1[0][c, (1 - position[4]) + (r - v1[1])]


def own_position():
    i, j = lax.axis_index("gx"), lax.axis_index("gz")
    return i, j, lax.axis_size("gx"), lax.axis_size("gz"), i % 2, j % 2, i // 2 % 2


def by_parity(position, body):
    for odd in range(2):
        pl.when(position[4] == odd)(lambda odd=odd: body(odd))


def rows_to_send(position, own, first, second):
    spare = own.shape[1] - first.shape[1]

    def body(odd):
        for c in range(own.shape[0]):
            for r in range(first.shape[1]):
                first[c, r] = own[c, (1 - odd) * spare + r]
                second[c, r] = own[c, odd * spare + r]

    by_parity(position, body)


def with_halo(position, own, first, second, store):
    rows, halo = own.shape[1], first.shape[1]

    def body(odd):
        for c in range(own.shape[0]):
            for piece, at in ((first, (1 - odd) * (halo + rows)), (second, odd * (halo + rows))):
                for r in range(halo):
                    store(c, at + r, piece[c, r])

    for c in range(own.shape[0]):
        for r in range(rows):
            store(c, halo + r, own[c, r])
    by_parity(position, body)


def squeeze(parts):
    lane = lax.broadcasted_iota(jnp.int32, parts[0].shape, 1)
    last = parts[3]
    spare = [pltpu.roll(last, 48, 1), pltpu.roll(last, 80, 1), jnp.where(lane < 64, pltpu.roll(last, 16, 1), pltpu.roll(last, 112, 1))]
    return [jnp.where((lane < 48) | (lane >= 80), parts[t], spare[t]) for t in range(3)]


def unsqueeze(tiles):
    lane = lax.broadcasted_iota(jnp.int32, tiles[0].shape, 1)
    low = jnp.where(lane < 32, pltpu.roll(tiles[0], 80, 1), pltpu.roll(tiles[2], 112, 1))
    high = jnp.where(lane < 96, pltpu.roll(tiles[2], 16, 1), pltpu.roll(tiles[1], 48, 1))
    return [*tiles, jnp.where(lane < 48, low, jnp.where(lane < 80, 1.0, high))]


def pack_kernel(source, density, out):
    blocks, n = out.shape[0], source.shape[0]
    count = n + density.shape[0]

    def block(m, b):
        ref, at = (source, m) if m < n else (density, m - n)
        return ref[at, :, b * LANES : (b + 1) * LANES]

    zero = jnp.zeros((out.shape[2], LANES), jnp.float32)
    lane = lax.broadcasted_iota(jnp.int32, zero.shape, 1)
    for k in range(count // 4):
        for b in range(blocks):
            halos = []
            for m in range(4 * k, 4 * k + 4):
                out[b, m] = block(m, b)
                after = block(m, b + 1) if b + 1 < blocks else zero
                before = block(m, b - 1) if b else zero
                halos.append(jnp.where(lane < LANES // 2, after, before))
            for t, tile in enumerate(squeeze(halos)):
                out[b, count + 3 * k + t] = tile


def unpack_kernel(taken, own, first, second, scratch):
    position = own_position()
    blocks, _, rows, _ = taken.shape
    depth = NZ // blocks
    count = (C + 1) * depth
    for b in range(blocks):
        for k in range(count // 4):
            halos = unsqueeze([taken[b, count + 3 * k + t] for t in range(3)])
            for m in range(4 * k, 4 * k + 4):
                at = (b * depth + m % depth) * rows
                scratch[m // depth, 0, at : at + rows] = taken[b, m]
                scratch[m // depth, 1, at : at + rows] = halos[m - 4 * k]
    for c in range(C + 1):
        for r in range(rows):
            for h in range(2):
                own[c, r, :, h * LANES : (h + 1) * LANES] = scratch[c, h, pl.ds(r, NZ, stride=rows), :]
    spare = rows - HALO

    def send(odd):
        for target, start in ((first, (1 - odd) * spare), (second, odd * spare)):
            for r in range(HALO):
                for c in range(C + 1):
                    target[c, r] = own[c, start + r, :, :LANES]
                for t, tile in enumerate(squeeze([own[c, start + r, :, LANES:] for c in range(C + 1)])):
                    target[C + 1 + t, r] = tile

    by_parity(position, send)


def first_down_kernel(own, second, first, g0, d0, f0, v0, g1, d1, f1, v1, packed, edge, field, field1):
    position = own_position()
    rows = own.shape[1]

    def store(c, at, value):
        if c < C:
            g0[c, at] = value
        else:
            d0[at] = value

    for c in range(C + 1):
        for r in range(rows):
            store(c, HALO + r, own[c, r])

    def receive(odd):
        for piece, at in ((first, (1 - odd) * (HALO + rows)), (second, odd * (HALO + rows))):
            for r in range(HALO):
                halos = unsqueeze([piece[C + 1 + t, r] for t in range(3)])
                for c in range(C + 1):
                    store(c, at + r, jnp.concatenate([piece[c, r], halos[c]], axis=1))

    by_parity(position, receive)
    g, d, f, a, b = (g0, -HALO), (d0, -HALO), (f0, -HALO), (field, -HALO), (v0, -HALO)
    from_zero(a, g, d, f, 0, 2 * LANES, rows, position, -HALO, rows + HALO)
    sweep(b, a, g, f, 0, -5, rows + 5)
    coarse_source((g1, -2), b, g, d, 0, 2 * LANES, -2, rows // 2 + 2)
    from_zero((field1, -2), (g1, -2), (d1, -3), (f1, -3), 1, LANES, rows // 2, position, -2, rows // 2 + 2, d, 1)
    level_one_down(position, (g1, -2), (v1, -2), (field1, -2), (d1, -3), (f1, -3), packed, edge)


def side_kernel(own, second, first, tall, to_first, to_second):
    position = own_position()
    half = tall.shape[1] // 2
    low = (lane_index() < LANES // 2) == (position[5] == 1)

    def store(c, at, value):
        tall[c, at] = value

    with_halo(position, own, first, second, store)
    for c in range(C):
        for r in range(half):
            one, two = tall[c, r], pltpu.roll(tall[c, r + half], LANES // 2, 1)
            to_first[c, r] = jnp.where(low, one, two)
            to_second[c, r] = jnp.where(low, two, one)


def second_down_kernel(tall, first, second, g0, d0, f0, d1, f1, v0, g1, v1, packed, edge, wide, field, field1):
    position = own_position()
    half = tall.shape[1] // 2
    halo = half - v0.shape[1] // 2 + HALO
    rows = 2 * (half - halo)
    low = (lane_index() < LANES // 2) == (position[5] == 0)
    for c in range(C):
        for r in range(2 * half):
            wide[c, r, :, :LANES] = tall[c, r]
        for r in range(half):
            wide[c, r, :, LANES:] = jnp.where(low, first[c, r], second[c, r])
            wide[c, r + half, :, LANES:] = pltpu.roll(jnp.where(low, second[c, r], first[c, r]), LANES // 2, 1)
    g, d, f, a, b = (g0, -HALO), (d0, -HALO), (f0, -HALO), (field, -HALO), (v0, -HALO)
    sweep(a, (wide, -halo), g, f, 0, -6, rows + 6)
    sweep(b, a, g, f, 0, -5, rows + 5)
    coarse_source((g1, -2), b, g, d, 0, 2 * LANES, -2, rows // 2 + 2)
    first_sweep((field1, -2), (g1, -2), (f1, -3), 1, -2, rows // 2 + 2)
    level_one_down(position, (g1, -2), (v1, -2), (field1, -2), (d1, -3), (f1, -3), packed, edge)


def coarse_kernel(mine, other, v1, out, first, second, g2, d2, f2, g3, d3, f3, a, b, a3, b3):
    position = own_position()
    lane = lane_index()
    odd, step = position[4], 1 - 2 * position[6]
    count, reach = first.shape[1], 8
    units = C + 1

    for ref, core in ((mine, odd), (other, 1 - odd)):
        for n, away in enumerate((0, step, -step, 2 * step, -2 * step)):
            at = 4 * away + (2 * core + reach)
            for c in range(units):
                both = ref[n * units + c]
                twin = pltpu.roll(both, LANES // 2, 1)
                for q, value in ((0, jnp.where(lane < LANES // 2, both, twin)), (1, jnp.where(lane < LANES // 2, twin, both))):
                    if c < C:
                        g2[c, at + q] = value
                    else:
                        d2[at + q] = value
    g, d, f, u, w = (g2, -reach), (d2, -reach), (f2, -reach), (a, -reach), (b, -reach)
    h, e, k, s, t = (g3, -reach // 2), (d3, -reach // 2), (f3, -reach // 2), (a3, -reach // 2), (b3, -reach // 2)
    from_zero(u, g, d, f, 2, LANES // 2, 4, position, -8, 12, group=2)
    sweep(w, u, g, f, 2, -7, 11)
    coarse_source(h, w, g, d, 2, LANES // 2, -3, 5)
    from_zero(s, h, e, k, 3, LANES // 4, 2, position, -3, 5, d, group=2)
    sweep(t, s, h, k, 3, -2, 4)
    sweep(s, t, h, k, 3, -1, 3)

    def correct(q):
        for c in range(C):
            fine = spread(row(s, c, q), LANES // 2)
            for r in (q.double(), q.double() + 1):
                b[c, index(w, r)] = row(w, c, r) + fine

    each_row(-1, 3, correct, 4)
    sweep(u, w, g, f, 2, -1, 5)
    sweep(w, u, g, f, 2, 0, 4)
    for c in range(C):
        for q in (0, 1):
            fine = spread(b[c, 2 * odd + (q + reach)], LANES)
            for r in (2 * q, 2 * q + 1):
                out[c, r] = v1[c, r + 2] + fine
        for r, q in enumerate((0, odd, 1)):
            fine = spread(b[c, 2 * (1 - odd) + (reach + q)], LANES)
            first[c, r] = other[5 * units + c * count + r] + fine
        for r in range(count):
            second[c, r] = out[c, odd * (out.shape[1] - count) + r]


def climb(position, own, first, second, g0, f0, v0, g1, f1, wide, u, w, field, emit):
    rows1, halo = own.shape[1], first.shape[1]

    def store(c, at, value):
        wide[c, at] = value

    with_halo(position, own, first, second, store)
    sweep((u, -3), (wide, -halo), (g1, -2), (f1, -3), 1, -2, rows1 + 2)
    sweep((w, -3), (u, -3), (g1, -2), (f1, -3), 1, -1, rows1 + 1)

    def correct(q):
        for c in range(C):
            fine = spread(row((w, -3), c, q), 2 * LANES)
            for r in (q.double(), q.double() + 1):
                field[c, index((field, -HALO), r)] = row((v0, -HALO), c, r) + fine

    each_row(-1, rows1 + 1, correct, 2)
    rows = 2 * rows1
    sweep((emit, -HALO), (field, -HALO), (g0, -HALO), (f0, -HALO), 0, -1, rows + 1)
    sweep((field, -HALO), (emit, -HALO), (g0, -HALO), (f0, -HALO), 0, 0, rows)


def first_up_kernel(own, left, right, g0, f0, v0, g1, f1, out, first, second, wide, u, w, field, other):
    position = own_position()
    climb(position, own, left, right, g0, f0, v0, g1, f1, wide, u, w, field, other)
    for c in range(C):
        for r in range(out.shape[1]):
            out[c, r] = field[c, r + HALO, :, :LANES]
    rows_to_send(position, out, first, second)


def last_up_kernel(own, left, right, g0, f0, v0, g1, f1, out, wide, u, w, field, other, scratch):
    position = own_position()
    climb(position, own, left, right, g0, f0, v0, g1, f1, wide, u, w, field, other)
    blocks, _, rows, _ = out.shape
    depth = NZ // blocks
    for c in range(C):
        for r in range(rows):
            scratch[c, pl.ds(r, NZ, stride=rows), :] = field[c, r + HALO, :, :LANES]
    for c in range(C):
        for z in range(NZ):
            out[z // depth, c * depth + z % depth] = scratch[c, z * rows : (z + 1) * rows]


def join_kernel(taken, out):
    for b in range(taken.shape[0]):
        out[:, :, b * LANES : (b + 1) * LANES] = taken[b]


def call(kernel, outs, scratch, *args):
    shape = lambda s: jax.ShapeDtypeStruct(s, jnp.float32)
    out = pl.pallas_call(
        kernel,
        out_shape=[shape(s) for s in outs],
        in_specs=[pl.BlockSpec(memory_space=pltpu.VMEM)] * len(args),
        out_specs=[pl.BlockSpec(memory_space=pltpu.VMEM)] * len(outs),
        scratch_shapes=[pltpu.VMEM(s, jnp.float32) for s in scratch],
        compiler_params=PARAMS,
        name=kernel.__name__,
    )(*args)
    return out


def swap(values, axis, first, unit=1):
    count, pairs = lax.axis_size(axis), []
    for i in range(count):
        group = i // unit
        other = group ^ 1 if first else ((group - 1) ^ 1) + 1
        if 0 <= other < count // unit:
            pairs.append((i, other * unit + i % unit))
    return lax.ppermute(values, axis, pairs)


def shards(right_side, density):
    blocks = lax.axis_size("gz")
    depth, rows, columns = density.shape
    W, R0, R1 = 2 * LANES, rows + 2 * HALO, rows // 2

    count = (C + 1) * depth
    (sent,) = call(
        pack_kernel,
        [(blocks, count + 3 * (count // 4), rows, LANES)],
        [],
        right_side.reshape(C * depth, rows, columns),
        density,
    )
    taken = lax.all_to_all(sent, "gz", 0, 0)
    own, first, second = call(
        unpack_kernel,
        [(C + 1, rows, NZ, W)] + [(C + 4, HALO, NZ, LANES)] * 2,
        [(C + 1, 2, NZ * rows, LANES)],
        taken,
    )
    fine, mid = (C, R0, NZ, W), (C, R1 + 4, NZ, LANES)
    sends = [(C + 1, NZ, LANES), (C * (R1 - 1), NZ, LANES)]
    g0, d0, f0, v0, g1, d1, f1, *down = call(
        first_down_kernel,
        [fine, fine[1:], fine[1:], fine, mid, (R1 + 6, NZ, LANES), (R1 + 6, NZ, LANES), mid, *sends],
        [fine, mid],
        own,
        swap(second, "gx", False),
        swap(first, "gx", True),
    )

    def coarse(v1, packed, edge):
        near = [swap(packed, "gx", first, 2) for first in (True, False)]
        far = [swap(near[1], "gx", True, 2), swap(near[0], "gx", False, 2)]
        mine = jnp.concatenate([packed, *near, *far, edge])
        two, three = (C, 20, NZ, LANES), (C, 10, NZ, LANES)
        out, first, second = call(
            coarse_kernel,
            [(C, R1, NZ, LANES)] + [(C, R1 - 1, NZ, LANES)] * 2,
            [two, two[1:], two[1:], three, three[1:], three[1:], two, two, three, three],
                mine,
            swap(mine, "gx", True),
            v1,
        )
        return out, first, swap(second, "gx", False)

    middle = (C, R1 + 6, NZ, LANES)
    reach = HALO + 1
    field, first, second = call(
        first_up_kernel,
        [(C, rows, NZ, LANES), (C, reach, NZ, LANES), (C, reach, NZ, LANES)],
        [middle, middle, middle, fine, fine],
        *coarse(*down),
        g0,
        f0,
        v0,
        g1,
        f1,
    )
    half = (rows + 2 * reach) // 2
    tall, first, second = call(
        side_kernel,
        [(C, 2 * half, NZ, LANES)] + [(C, half, NZ, LANES)] * 2,
        [],
        field,
        swap(second, "gx", False),
        swap(first, "gx", True),
    )
    v0, g1, *down = call(
        second_down_kernel,
        [fine, mid, mid, *sends],
        [(C, 2 * half, NZ, W), fine, mid],
        tall,
        swap(first, "gz", True),
        swap(second, "gz", False),
        g0,
        d0,
        f0,
        d1,
        f1,
    )
    (sent,) = call(
        last_up_kernel,
        [(blocks, C * depth, rows, LANES)],
        [middle, middle, middle, fine, fine, (C, NZ * rows, LANES)],
        *coarse(*down),
        g0,
        f0,
        v0,
        g1,
        f1,
    )
    (out,) = call(join_kernel, [(C * depth, rows, columns)], [], lax.all_to_all(sent, "gz", 0, 0))
    return out.reshape(right_side.shape)


def solution(mesh):
    return jax.shard_map(
        shards,
        mesh=mesh,
        in_specs=(P(None, "gz", "gx", None), P("gz", "gx", None)),
        out_specs=P(None, "gz", "gx", None),
        check_vma=False,
    )
```

```python
import jax
import jax.numpy as jnp
from jax import lax
from jax.experimental import pallas as pl
from jax.experimental.pallas import tpu as pltpu
from jax.sharding import PartitionSpec as P

relaxation = 0.8
plane_coupling = 16.0
depth_coupling = 1.0
C = 3
NZ = 24
HALO = 6
LANES = 128
UNROLL = (18, 8, 18, 8)
SOURCE = (2, 1, 4, 4)
CLIMB = (10, 8)
PARAMS = pltpu.CompilerParams(vmem_limit_bytes=12 << 20)


def coupling_of(level):
    return plane_coupling / 4.0**level


def base_of(level):
    return 4.0 * coupling_of(level) + 2.0 * depth_coupling


class Row:
    def __init__(self, base, shift):
        self.base, self.shift = base, shift

    def __add__(self, n):
        return Row(self.base, self.shift + n)

    def __sub__(self, n):
        return self + -n

    def double(self):
        return Row(2 * self.base, 2 * self.shift)


def index(field, r):
    return r.base + (r.shift - field[1]) if isinstance(r, Row) else r - field[1]


def row(field, c, r):
    return field[0][c, index(field, r)]


def shared(field, r):
    return field[0][index(field, r)]


def neighbours(field, c, r, level):
    mid = row(field, c, r)
    width = mid.shape[1]
    lateral = row(field, c, r - 1) + row(field, c, r + 1) + pltpu.roll(mid, 1, 1) + pltpu.roll(mid, width - 1, 1)
    vertical = pltpu.roll(mid, 1, 0) + pltpu.roll(mid, NZ - 1, 0)
    return mid, coupling_of(level) * lateral + depth_coupling * vertical


def each_row(low, high, body, unroll):
    steps = (high - low) // unroll

    def step(n, carry):
        for k in range(unroll):
            body(Row(unroll * n, low + k))
        return carry

    if steps > 1:
        lax.fori_loop(0, steps, step, 0)
        low += steps * unroll
    for r in range(low, high):
        body(Row(0, r))


def sweep(target, field, source, factor, level, low, high, unroll=None):
    def body(r):
        f = shared(factor, r)
        for c in range(C):
            mid, around = neighbours(field, c, r, level)
            target[0][c, index(target, r)] = (1.0 - relaxation) * mid + f * (row(source, c, r) + around)

    each_row(low, high, body, unroll or UNROLL[level])


def lane_index():
    return lax.broadcasted_iota(jnp.int32, (NZ, LANES), 1)


def take(values, index):
    return jnp.take_along_axis(values, index, axis=1, mode="promise_in_bounds")


def pair_sum(values, period):
    lane = lane_index()
    if values.shape[1] == 2 * LANES:
        even = (2 * lane) % LANES
        halves = [take(h + pltpu.roll(h, LANES - 1, 1), even) for h in (values[:, :LANES], values[:, LANES:])]
        return jnp.where(lane < LANES // 2, halves[0], halves[1])
    return take(values + pltpu.roll(values, LANES - 1, 1), (2 * lane) % period)


def spread(values, period):
    lane = lane_index()
    if period == 2 * LANES:
        return jnp.concatenate([take(values, lane // 2), take(values, LANES // 2 + lane // 2)], axis=1)
    return take(values, (lane % period) // 2)


def coarse_source(target, field, source, density, level, period, low, high):
    def body(q):
        for c in range(C):
            total = None
            for r in (q.double(), q.double() + 1):
                mid, around = neighbours(field, c, r, level)
                residual = row(source, c, r) + around - (shared(density, r) + base_of(level)) * mid
                total = residual if total is None else total + residual
            target[0][c, index(target, q)] = 0.25 * pair_sum(total, period)

    each_row(low, high, body, SOURCE[level])


def from_zero(target, source, density, factor, level, period, rows, position, low, high, finer=None, reach=0, group=1):
    i, j, count_x, count_y = position[0] // group, position[1], position[2] // group, position[3]
    width = factor[0].shape[-1]
    lane = lax.broadcasted_iota(jnp.int32, (NZ, width), 1) % period
    inside_y = ((lane < 3 * period // 4) | (j > 0)) & ((lane < period // 2) | (lane >= 3 * period // 4) | (j < count_y - 1))

    def body(r):
        if finer is None:
            own = shared(density, r)
        else:
            own = 0.25 * pair_sum(shared(finer, r.double()) + shared(finer, r.double() + 1), 2 * period)
            density[0][index(density, r)] = own
        at = i * rows + r.base
        inside = inside_y & ((at >= -r.shift) & (at < count_x * rows - r.shift))
        f = jnp.where(inside, relaxation / (own + base_of(level)), 0.0)
        factor[0][index(factor, r)] = f
        return f

    def whole(r):
        f = body(r)
        for c in range(C):
            target[0][c, index(target, r)] = f * row(source, c, r)

    for r in [*range(low - reach, low), *range(high, high + reach)]:
        body(Row(0, r))
    each_row(low, high, whole, UNROLL[level])


def first_sweep(target, source, factor, level, low, high):
    def body(r):
        f = shared(factor, r)
        for c in range(C):
            target[0][c, index(target, r)] = f * row(source, c, r)

    each_row(low, high, body, UNROLL[level])


def level_one_down(position, g1, v1, scratch, d1, f1, packed, edge):
    sweep(v1, scratch, g1, f1, 1, -1, 5)
    lane = lane_index()
    for c in range(C + 1):
        pair = []
        for q in (0, 1):
            total = None
            for r in (2 * q, 2 * q + 1):
                if c == C:
                    part = shared(d1, r)
                else:
                    mid, around = neighbours(v1, c, r, 1)
                    part = row(g1, c, r) + around - (shared(d1, r) + base_of(1)) * mid
                total = part if total is None else total + part
            pair.append(0.25 * pair_sum(total, LANES))
        packed[c] = jnp.where(lane < LANES // 2, pair[0], pair[1])
    count = edge.shape[0] // C
    for c in range(C):
        for r in range(count):
            edge[c * count + r] = v1[0][c, (1 - position[4]) + (r - v1[1])]


def own_position():
    i, j = lax.axis_index("gx"), lax.axis_index("gz")
    return i, j, lax.axis_size("gx"), lax.axis_size("gz"), i % 2, j % 2, i // 2 % 2


def by_parity(position, body):
    for odd in range(2):
        pl.when(position[4] == odd)(lambda odd=odd: body(odd))


def rows_to_send(position, own, first, second):
    spare = own.shape[1] - first.shape[1]

    def body(odd):
        for c in range(own.shape[0]):
            for r in range(first.shape[1]):
                first[c, r] = own[c, (1 - odd) * spare + r]
                second[c, r] = own[c, odd * spare + r]

    by_parity(position, body)


def with_halo(position, own, first, second, store):
    rows, halo = own.shape[1], first.shape[1]

    def body(odd):
        for c in range(own.shape[0]):
            for piece, at in ((first, (1 - odd) * (halo + rows)), (second, odd * (halo + rows))):
                for r in range(halo):
                    store(c, at + r, piece[c, r])

    for c in range(own.shape[0]):
        for r in range(rows):
            store(c, halo + r, own[c, r])
    by_parity(position, body)


def squeeze(parts):
    lane = lax.broadcasted_iota(jnp.int32, parts[0].shape, 1)
    last = parts[3]
    spare = [pltpu.roll(last, 48, 1), pltpu.roll(last, 80, 1), jnp.where(lane < 64, pltpu.roll(last, 16, 1), pltpu.roll(last, 112, 1))]
    return [jnp.where((lane < 48) | (lane >= 80), parts[t], spare[t]) for t in range(3)]


def unsqueeze(tiles):
    lane = lax.broadcasted_iota(jnp.int32, tiles[0].shape, 1)
    low = jnp.where(lane < 32, pltpu.roll(tiles[0], 80, 1), pltpu.roll(tiles[2], 112, 1))
    high = jnp.where(lane < 96, pltpu.roll(tiles[2], 16, 1), pltpu.roll(tiles[1], 48, 1))
    return [*tiles, jnp.where(lane < 48, low, jnp.where(lane < 80, 1.0, high))]


def pack_kernel(source, density, out):
    blocks, n = out.shape[0], source.shape[0]
    count = n + density.shape[0]

    def block(m, b):
        ref, at = (source, m) if m < n else (density, m - n)
        return ref[at, :, b * LANES : (b + 1) * LANES]

    zero = jnp.zeros((out.shape[2], LANES), jnp.float32)
    lane = lax.broadcasted_iota(jnp.int32, zero.shape, 1)
    for k in range(count // 4):
        for b in range(blocks):
            halos = []
            for m in range(4 * k, 4 * k + 4):
                out[b, m] = block(m, b)
                after = block(m, b + 1) if b + 1 < blocks else zero
                before = block(m, b - 1) if b else zero
                halos.append(jnp.where(lane < LANES // 2, after, before))
            for t, tile in enumerate(squeeze(halos)):
                out[b, count + 3 * k + t] = tile


def unpack_kernel(taken, own, first, second, scratch):
    position = own_position()
    blocks, _, rows, _ = taken.shape
    depth = NZ // blocks
    count = (C + 1) * depth
    for b in range(blocks):
        for k in range(count // 4):
            halos = unsqueeze([taken[b, count + 3 * k + t] for t in range(3)])
            for m in range(4 * k, 4 * k + 4):
                at = (b * depth + m % depth) * rows
                scratch[m // depth, 0, at : at + rows] = taken[b, m]
                scratch[m // depth, 1, at : at + rows] = halos[m - 4 * k]
    for c in range(C + 1):
        for r in range(rows):
            for h in range(2):
                own[c, r, :, h * LANES : (h + 1) * LANES] = scratch[c, h, pl.ds(r, NZ, stride=rows), :]
    spare = rows - HALO

    def send(odd):
        for target, start in ((first, (1 - odd) * spare), (second, odd * spare)):
            for r in range(HALO):
                for c in range(C + 1):
                    target[c, r] = own[c, start + r, :, :LANES]
                for t, tile in enumerate(squeeze([own[c, start + r, :, LANES:] for c in range(C + 1)])):
                    target[C + 1 + t, r] = tile

    by_parity(position, send)


def first_down_kernel(own, second, first, g0, d0, f0, v0, g1, d1, f1, v1, packed, edge, field, field1):
    position = own_position()
    rows = own.shape[1]

    def store(c, at, value):
        if c < C:
            g0[c, at] = value
        else:
            d0[at] = value

    for c in range(C + 1):
        for r in range(rows):
            store(c, HALO + r, own[c, r])

    def receive(odd):
        for piece, at in ((first, (1 - odd) * (HALO + rows)), (second, odd * (HALO + rows))):
            for r in range(HALO):
                halos = unsqueeze([piece[C + 1 + t, r] for t in range(3)])
                for c in range(C + 1):
                    store(c, at + r, jnp.concatenate([piece[c, r], halos[c]], axis=1))

    by_parity(position, receive)
    g, d, f, a, b = (g0, -HALO), (d0, -HALO), (f0, -HALO), (field, -HALO), (v0, -HALO)
    from_zero(a, g, d, f, 0, 2 * LANES, rows, position, -HALO, rows + HALO)
    sweep(b, a, g, f, 0, -5, rows + 5)
    coarse_source((g1, -2), b, g, d, 0, 2 * LANES, -2, rows // 2 + 2)
    from_zero((field1, -2), (g1, -2), (d1, -3), (f1, -3), 1, LANES, rows // 2, position, -2, rows // 2 + 2, d, 1)
    level_one_down(position, (g1, -2), (v1, -2), (field1, -2), (d1, -3), (f1, -3), packed, edge)


def side_kernel(own, second, first, tall, to_first, to_second):
    position = own_position()
    half = tall.shape[1] // 2
    low = (lane_index() < LANES // 2) == (position[5] == 1)

    def store(c, at, value):
        tall[c, at] = value

    with_halo(position, own, first, second, store)
    for c in range(C):
        for r in range(half):
            one, two = tall[c, r], pltpu.roll(tall[c, r + half], LANES // 2, 1)
            to_first[c, r] = jnp.where(low, one, two)
            to_second[c, r] = jnp.where(low, two, one)


def second_down_kernel(tall, first, second, g0, d0, f0, d1, f1, v0, g1, v1, packed, edge, wide, field, field1):
    position = own_position()
    half = tall.shape[1] // 2
    halo = half - v0.shape[1] // 2 + HALO
    rows = 2 * (half - halo)
    low = (lane_index() < LANES // 2) == (position[5] == 0)
    for c in range(C):
        for r in range(2 * half):
            wide[c, r, :, :LANES] = tall[c, r]
        for r in range(half):
            wide[c, r, :, LANES:] = jnp.where(low, first[c, r], second[c, r])
            wide[c, r + half, :, LANES:] = pltpu.roll(jnp.where(low, second[c, r], first[c, r]), LANES // 2, 1)
    g, d, f, a, b = (g0, -HALO), (d0, -HALO), (f0, -HALO), (field, -HALO), (v0, -HALO)
    sweep(a, (wide, -halo), g, f, 0, -6, rows + 6)
    sweep(b, a, g, f, 0, -5, rows + 5)
    coarse_source((g1, -2), b, g, d, 0, 2 * LANES, -2, rows // 2 + 2)
    first_sweep((field1, -2), (g1, -2), (f1, -3), 1, -2, rows // 2 + 2)
    level_one_down(position, (g1, -2), (v1, -2), (field1, -2), (d1, -3), (f1, -3), packed, edge)


def coarse_kernel(mine, other, v1, out, first, second, g2, d2, f2, g3, d3, f3, a, b, a3, b3):
    position = own_position()
    lane = lane_index()
    odd, step = position[4], 1 - 2 * position[6]
    count, reach = first.shape[1], 8
    units = C + 1

    for ref, core in ((mine, odd), (other, 1 - odd)):
        for n, away in enumerate((0, step, -step, 2 * step, -2 * step)):
            at = 4 * away + (2 * core + reach)
            for c in range(units):
                both = ref[n * units + c]
                twin = pltpu.roll(both, LANES // 2, 1)
                for q, value in ((0, jnp.where(lane < LANES // 2, both, twin)), (1, jnp.where(lane < LANES // 2, twin, both))):
                    if c < C:
                        g2[c, at + q] = value
                    else:
                        d2[at + q] = value
    g, d, f, u, w = (g2, -reach), (d2, -reach), (f2, -reach), (a, -reach), (b, -reach)
    h, e, k, s, t = (g3, -reach // 2), (d3, -reach // 2), (f3, -reach // 2), (a3, -reach // 2), (b3, -reach // 2)
    from_zero(u, g, d, f, 2, LANES // 2, 4, position, -8, 12, group=2)
    sweep(w, u, g, f, 2, -7, 11)
    coarse_source(h, w, g, d, 2, LANES // 2, -3, 5)
    from_zero(s, h, e, k, 3, LANES // 4, 2, position, -3, 5, d, group=2)
    sweep(t, s, h, k, 3, -2, 4)
    sweep(s, t, h, k, 3, -1, 3)

    def correct(q):
        for c in range(C):
            fine = spread(row(s, c, q), LANES // 2)
            for r in (q.double(), q.double() + 1):
                b[c, index(w, r)] = row(w, c, r) + fine

    each_row(-1, 3, correct, 4)
    sweep(u, w, g, f, 2, -1, 5)
    sweep(w, u, g, f, 2, 0, 4)
    for c in range(C):
        for q in (0, 1):
            fine = spread(b[c, 2 * odd + (q + reach)], LANES)
            for r in (2 * q, 2 * q + 1):
                out[c, r] = v1[c, r + 2] + fine
        for r, q in enumerate((0, odd, 1)):
            fine = spread(b[c, 2 * (1 - odd) + (reach + q)], LANES)
            first[c, r] = other[5 * units + c * count + r] + fine
        for r in range(count):
            second[c, r] = out[c, odd * (out.shape[1] - count) + r]


def climb(position, own, first, second, g0, f0, v0, g1, f1, wide, u, w, field, emit):
    rows1, halo = own.shape[1], first.shape[1]

    def store(c, at, value):
        wide[c, at] = value

    with_halo(position, own, first, second, store)
    sweep((u, -3), (wide, -halo), (g1, -2), (f1, -3), 1, -2, rows1 + 2, CLIMB[1])
    sweep((w, -3), (u, -3), (g1, -2), (f1, -3), 1, -1, rows1 + 1, CLIMB[1])

    def correct(q):
        for c in range(C):
            fine = spread(row((w, -3), c, q), 2 * LANES)
            for r in (q.double(), q.double() + 1):
                field[c, index((field, -HALO), r)] = row((v0, -HALO), c, r) + fine

    each_row(-1, rows1 + 1, correct, CLIMB[1])
    rows = 2 * rows1
    sweep((emit, -HALO), (field, -HALO), (g0, -HALO), (f0, -HALO), 0, -1, rows + 1, CLIMB[0])
    sweep((field, -HALO), (emit, -HALO), (g0, -HALO), (f0, -HALO), 0, 0, rows, CLIMB[0])


def first_up_kernel(own, left, right, g0, f0, v0, g1, f1, out, first, second, wide, u, w, field, other):
    position = own_position()
    climb(position, own, left, right, g0, f0, v0, g1, f1, wide, u, w, field, other)
    for c in range(C):
        for r in range(out.shape[1]):
            out[c, r] = field[c, r + HALO, :, :LANES]
    rows_to_send(position, out, first, second)


def last_up_kernel(own, left, right, g0, f0, v0, g1, f1, out, wide, u, w, field, other, scratch):
    position = own_position()
    climb(position, own, left, right, g0, f0, v0, g1, f1, wide, u, w, field, other)
    blocks, _, rows, _ = out.shape
    depth = NZ // blocks
    for c in range(C):
        for r in range(rows):
            scratch[c, pl.ds(r, NZ, stride=rows), :] = field[c, r + HALO, :, :LANES]
    for c in range(C):
        for z in range(NZ):
            out[z // depth, c * depth + z % depth] = scratch[c, z * rows : (z + 1) * rows]


def join_kernel(taken, out):
    for b in range(taken.shape[0]):
        out[:, :, b * LANES : (b + 1) * LANES] = taken[b]


def call(kernel, outs, scratch, *args):
    shape = lambda s: jax.ShapeDtypeStruct(s, jnp.float32)
    out = pl.pallas_call(
        kernel,
        out_shape=[shape(s) for s in outs],
        in_specs=[pl.BlockSpec(memory_space=pltpu.VMEM)] * len(args),
        out_specs=[pl.BlockSpec(memory_space=pltpu.VMEM)] * len(outs),
        scratch_shapes=[pltpu.VMEM(s, jnp.float32) for s in scratch],
        compiler_params=PARAMS,
        name=kernel.__name__,
    )(*args)
    return out


def swap(values, axis, first, unit=1):
    count, pairs = lax.axis_size(axis), []
    for i in range(count):
        group = i // unit
        other = group ^ 1 if first else ((group - 1) ^ 1) + 1
        if 0 <= other < count // unit:
            pairs.append((i, other * unit + i % unit))
    return lax.ppermute(values, axis, pairs)


def shards(right_side, density):
    blocks = lax.axis_size("gz")
    depth, rows, columns = density.shape
    W, R0, R1 = 2 * LANES, rows + 2 * HALO, rows // 2

    count = (C + 1) * depth
    (sent,) = call(
        pack_kernel,
        [(blocks, count + 3 * (count // 4), rows, LANES)],
        [],
        right_side.reshape(C * depth, rows, columns),
        density,
    )
    taken = lax.all_to_all(sent, "gz", 0, 0)
    own, first, second = call(
        unpack_kernel,
        [(C + 1, rows, NZ, W)] + [(C + 4, HALO, NZ, LANES)] * 2,
        [(C + 1, 2, NZ * rows, LANES)],
        taken,
    )
    fine, mid = (C, R0, NZ, W), (C, R1 + 4, NZ, LANES)
    sends = [(C + 1, NZ, LANES), (C * (R1 - 1), NZ, LANES)]
    g0, d0, f0, v0, g1, d1, f1, *down = call(
        first_down_kernel,
        [fine, fine[1:], fine[1:], fine, mid, (R1 + 6, NZ, LANES), (R1 + 6, NZ, LANES), mid, *sends],
        [fine, mid],
        own,
        swap(second, "gx", False),
        swap(first, "gx", True),
    )

    def coarse(v1, packed, edge):
        near = [swap(packed, "gx", first, 2) for first in (True, False)]
        far = [swap(near[1], "gx", True, 2), swap(near[0], "gx", False, 2)]
        mine = jnp.concatenate([packed, *near, *far, edge])
        two, three = (C, 20, NZ, LANES), (C, 10, NZ, LANES)
        out, first, second = call(
            coarse_kernel,
            [(C, R1, NZ, LANES)] + [(C, R1 - 1, NZ, LANES)] * 2,
            [two, two[1:], two[1:], three, three[1:], three[1:], two, two, three, three],
                mine,
            swap(mine, "gx", True),
            v1,
        )
        return out, first, swap(second, "gx", False)

    middle = (C, R1 + 6, NZ, LANES)
    reach = HALO + 1
    field, first, second = call(
        first_up_kernel,
        [(C, rows, NZ, LANES), (C, reach, NZ, LANES), (C, reach, NZ, LANES)],
        [middle, middle, middle, fine, fine],
        *coarse(*down),
        g0,
        f0,
        v0,
        g1,
        f1,
    )
    half = (rows + 2 * reach) // 2
    tall, first, second = call(
        side_kernel,
        [(C, 2 * half, NZ, LANES)] + [(C, half, NZ, LANES)] * 2,
        [],
        field,
        swap(second, "gx", False),
        swap(first, "gx", True),
    )
    v0, g1, *down = call(
        second_down_kernel,
        [fine, mid, mid, *sends],
        [(C, 2 * half, NZ, W), fine, mid],
        tall,
        swap(first, "gz", True),
        swap(second, "gz", False),
        g0,
        d0,
        f0,
        d1,
        f1,
    )
    (sent,) = call(
        last_up_kernel,
        [(blocks, C * depth, rows, LANES)],
        [middle, middle, middle, fine, fine, (C, NZ * rows, LANES)],
        *coarse(*down),
        g0,
        f0,
        v0,
        g1,
        f1,
    )
    (out,) = call(join_kernel, [(C * depth, rows, columns)], [], lax.all_to_all(sent, "gz", 0, 0))
    return out.reshape(right_side.shape)


def solution(mesh):
    return jax.shard_map(
        shards,
        mesh=mesh,
        in_specs=(P(None, "gz", "gx", None), P("gz", "gx", None)),
        out_specs=P(None, "gz", "gx", None),
        check_vma=False,
    )
```

```python
import jax
import jax.numpy as jnp
from jax import lax
from jax.experimental import pallas as pl
from jax.experimental.pallas import tpu as pltpu
from jax.sharding import PartitionSpec as P

relaxation = 0.8
plane_coupling = 16.0
depth_coupling = 1.0
C = 3
NZ = 24
HALO = 6
LANES = 128
UNROLL = (18, 8, 18, 8)
SOURCE = (2, 1, 4, 4)
CLIMB = (10, 8)
PARAMS = pltpu.CompilerParams(vmem_limit_bytes=12 << 20)


def coupling_of(level):
    return plane_coupling / 4.0**level


def base_of(level):
    return 4.0 * coupling_of(level) + 2.0 * depth_coupling


class Row:
    def __init__(self, base, shift):
        self.base, self.shift = base, shift

    def __add__(self, n):
        return Row(self.base, self.shift + n)

    def __sub__(self, n):
        return self + -n

    def double(self):
        return Row(2 * self.base, 2 * self.shift)


def index(field, r):
    return r.base + (r.shift - field[1]) if isinstance(r, Row) else r - field[1]


def row(field, c, r):
    return field[0][c, index(field, r)]


def shared(field, r):
    return field[0][index(field, r)]


def neighbours(field, c, r, level):
    mid = row(field, c, r)
    width = mid.shape[1]
    lateral = row(field, c, r - 1) + row(field, c, r + 1) + pltpu.roll(mid, 1, 1) + pltpu.roll(mid, width - 1, 1)
    vertical = pltpu.roll(mid, 1, 0) + pltpu.roll(mid, NZ - 1, 0)
    return mid, coupling_of(level) * lateral + depth_coupling * vertical


def each_row(low, high, body, unroll):
    steps = (high - low) // unroll

    def step(n, carry):
        for k in range(unroll):
            body(Row(unroll * n, low + k))
        return carry

    if steps > 1:
        lax.fori_loop(0, steps, step, 0)
        low += steps * unroll
    for r in range(low, high):
        body(Row(0, r))


def sweep(target, field, source, factor, level, low, high, unroll=None):
    def body(r):
        f = shared(factor, r)
        for c in range(C):
            mid, around = neighbours(field, c, r, level)
            target[0][c, index(target, r)] = (1.0 - relaxation) * mid + f * (row(source, c, r) + around)

    each_row(low, high, body, unroll or UNROLL[level])


def lane_index():
    return lax.broadcasted_iota(jnp.int32, (NZ, LANES), 1)


def take(values, index):
    return jnp.take_along_axis(values, index, axis=1, mode="promise_in_bounds")


def pair_sum(values, period):
    lane = lane_index()
    if values.shape[1] == 2 * LANES:
        even = (2 * lane) % LANES
        halves = [take(h + pltpu.roll(h, LANES - 1, 1), even) for h in (values[:, :LANES], values[:, LANES:])]
        return jnp.where(lane < LANES // 2, halves[0], halves[1])
    return take(values + pltpu.roll(values, LANES - 1, 1), (2 * lane) % period)


def spread(values, period):
    lane = lane_index()
    if period == 2 * LANES:
        return jnp.concatenate([take(values, lane // 2), take(values, LANES // 2 + lane // 2)], axis=1)
    return take(values, (lane % period) // 2)


def coarse_source(target, field, source, density, level, period, low, high):
    def body(q):
        for c in range(C):
            total = None
            for r in (q.double(), q.double() + 1):
                mid, around = neighbours(field, c, r, level)
                residual = row(source, c, r) + around - (shared(density, r) + base_of(level)) * mid
                total = residual if total is None else total + residual
            target[0][c, index(target, q)] = 0.25 * pair_sum(total, period)

    each_row(low, high, body, SOURCE[level])


def from_zero(target, source, density, factor, level, period, rows, position, low, high, finer=None, reach=0, group=1):
    i, j, count_x, count_y = position[0] // group, position[1], position[2] // group, position[3]
    width = factor[0].shape[-1]
    lane = lax.broadcasted_iota(jnp.int32, (NZ, width), 1) % period
    inside_y = ((lane < 3 * period // 4) | (j > 0)) & ((lane < period // 2) | (lane >= 3 * period // 4) | (j < count_y - 1))

    def body(r):
        if finer is None:
            own = shared(density, r)
        else:
            own = 0.25 * pair_sum(shared(finer, r.double()) + shared(finer, r.double() + 1), 2 * period)
            density[0][index(density, r)] = own
        at = i * rows + r.base
        inside = inside_y & ((at >= -r.shift) & (at < count_x * rows - r.shift))
        f = jnp.where(inside, relaxation / (own + base_of(level)), 0.0)
        factor[0][index(factor, r)] = f
        return f

    def whole(r):
        f = body(r)
        for c in range(C):
            target[0][c, index(target, r)] = f * row(source, c, r)

    for r in [*range(low - reach, low), *range(high, high + reach)]:
        body(Row(0, r))
    each_row(low, high, whole, UNROLL[level])


def first_sweep(target, source, factor, level, low, high):
    def body(r):
        f = shared(factor, r)
        for c in range(C):
            target[0][c, index(target, r)] = f * row(source, c, r)

    each_row(low, high, body, UNROLL[level])


def level_one_down(position, g1, v1, scratch, d1, f1, packed, edge):
    sweep(v1, scratch, g1, f1, 1, -1, 5)
    lane = lane_index()
    for c in range(C + 1):
        pair = []
        for q in (0, 1):
            total = None
            for r in (2 * q, 2 * q + 1):
                if c == C:
                    part = shared(d1, r)
                else:
                    mid, around = neighbours(v1, c, r, 1)
                    part = row(g1, c, r) + around - (shared(d1, r) + base_of(1)) * mid
                total = part if total is None else total + part
            pair.append(0.25 * pair_sum(total, LANES))
        packed[c] = jnp.where(lane < LANES // 2, pair[0], pair[1])
    count = edge.shape[0] // C
    for c in range(C):
        for r in range(count):
            edge[c * count + r] = v1[0][c, (1 - position[4]) + (r - v1[1])]


def own_position():
    i, j = lax.axis_index("gx"), lax.axis_index("gz")
    return i, j, lax.axis_size("gx"), lax.axis_size("gz"), i % 2, j % 2, i // 2 % 2


def by_parity(position, body):
    for odd in range(2):
        pl.when(position[4] == odd)(lambda odd=odd: body(odd))


def rows_to_send(position, own, first, second):
    spare = own.shape[1] - first.shape[1]

    def body(odd):
        for c in range(own.shape[0]):
            for r in range(first.shape[1]):
                first[c, r] = own[c, (1 - odd) * spare + r]
                second[c, r] = own[c, odd * spare + r]

    by_parity(position, body)


def with_halo(position, own, first, second, store):
    rows, halo = own.shape[1], first.shape[1]

    def body(odd):
        for c in range(own.shape[0]):
            for piece, at in ((first, (1 - odd) * (halo + rows)), (second, odd * (halo + rows))):
                for r in range(halo):
                    store(c, at + r, piece[c, r])

    for c in range(own.shape[0]):
        for r in range(rows):
            store(c, halo + r, own[c, r])
    by_parity(position, body)


def squeeze(parts):
    lane = lax.broadcasted_iota(jnp.int32, parts[0].shape, 1)
    last = parts[3]
    spare = [pltpu.roll(last, 48, 1), pltpu.roll(last, 80, 1), jnp.where(lane < 64, pltpu.roll(last, 16, 1), pltpu.roll(last, 112, 1))]
    return [jnp.where((lane < 48) | (lane >= 80), parts[t], spare[t]) for t in range(3)]


def unsqueeze(tiles):
    lane = lax.broadcasted_iota(jnp.int32, tiles[0].shape, 1)
    low = jnp.where(lane < 32, pltpu.roll(tiles[0], 80, 1), pltpu.roll(tiles[2], 112, 1))
    high = jnp.where(lane < 96, pltpu.roll(tiles[2], 16, 1), pltpu.roll(tiles[1], 48, 1))
    return [*tiles, jnp.where(lane < 48, low, jnp.where(lane < 80, 1.0, high))]


def pack_kernel(source, density, out):
    blocks, n = out.shape[0], source.shape[0]
    count = n + density.shape[0]

    def block(m, b):
        ref, at = (source, m) if m < n else (density, m - n)
        return ref[at, :, b * LANES : (b + 1) * LANES]

    zero = jnp.zeros((out.shape[2], LANES), jnp.float32)
    lane = lax.broadcasted_iota(jnp.int32, zero.shape, 1)
    for k in range(count // 4):
        for b in range(blocks):
            halos = []
            for m in range(4 * k, 4 * k + 4):
                out[b, m] = block(m, b)
                after = block(m, b + 1) if b + 1 < blocks else zero
                before = block(m, b - 1) if b else zero
                halos.append(jnp.where(lane < LANES // 2, after, before))
            for t, tile in enumerate(squeeze(halos)):
                out[b, count + 3 * k + t] = tile


def unpack_kernel(taken, own, first, second, scratch):
    position = own_position()
    blocks, _, rows, _ = taken.shape
    depth = NZ // blocks
    count = (C + 1) * depth
    for b in range(blocks):
        for k in range(count // 4):
            halos = unsqueeze([taken[b, count + 3 * k + t] for t in range(3)])
            for m in range(4 * k, 4 * k + 4):
                at = (b * depth + m % depth) * rows
                scratch[m // depth, 0, at : at + rows] = taken[b, m]
                scratch[m // depth, 1, at : at + rows] = halos[m - 4 * k]
    for c in range(C + 1):
        for r in range(rows):
            for h in range(2):
                own[c, r, :, h * LANES : (h + 1) * LANES] = scratch[c, h, pl.ds(r, NZ, stride=rows), :]
    spare = rows - HALO

    def send(odd):
        for target, start in ((first, (1 - odd) * spare), (second, odd * spare)):
            for r in range(HALO):
                for c in range(C + 1):
                    target[c, r] = own[c, start + r, :, :LANES]
                for t, tile in enumerate(squeeze([own[c, start + r, :, LANES:] for c in range(C + 1)])):
                    target[C + 1 + t, r] = tile

    by_parity(position, send)


def first_down_kernel(own, second, first, g0, d0, f0, v0, g1, d1, f1, v1, packed, edge, field, field1):
    position = own_position()
    rows = own.shape[1]

    def store(c, at, value):
        if c < C:
            g0[c, at] = value
        else:
            d0[at] = value

    for c in range(C + 1):
        for r in range(rows):
            store(c, HALO + r, own[c, r])

    def receive(odd):
        for piece, at in ((first, (1 - odd) * (HALO + rows)), (second, odd * (HALO + rows))):
            for r in range(HALO):
                halos = unsqueeze([piece[C + 1 + t, r] for t in range(3)])
                for c in range(C + 1):
                    store(c, at + r, jnp.concatenate([piece[c, r], halos[c]], axis=1))

    by_parity(position, receive)
    g, d, f, a, b = (g0, -HALO), (d0, -HALO), (f0, -HALO), (field, -HALO), (v0, -HALO)
    from_zero(a, g, d, f, 0, 2 * LANES, rows, position, -HALO, rows + HALO)
    sweep(b, a, g, f, 0, -5, rows + 5)
    coarse_source((g1, -2), b, g, d, 0, 2 * LANES, -2, rows // 2 + 2)
    from_zero((field1, -2), (g1, -2), (d1, -3), (f1, -3), 1, LANES, rows // 2, position, -2, rows // 2 + 2, d, 1)
    level_one_down(position, (g1, -2), (v1, -2), (field1, -2), (d1, -3), (f1, -3), packed, edge)


def side_kernel(own, second, first, tall, to_first, to_second):
    position = own_position()
    half = tall.shape[1] // 2
    low = (lane_index() < LANES // 2) == (position[5] == 1)

    def store(c, at, value):
        tall[c, at] = value

    with_halo(position, own, first, second, store)
    tiles = ([], [])
    for n in range(C * half):
        one, other = tall[n // half, n % half], tall[n // half, n % half + half]
        two = jnp.where(lane_index() < LANES // 2, pltpu.roll(other, 48, 1), pltpu.roll(other, 80, 1))
        tiles[0].append(jnp.where(low, one, two))
        tiles[1].append(jnp.where(low, two, one))
    for target, some in ((to_first, tiles[0]), (to_second, tiles[1])):
        whole = len(some) // 4 * 4
        packed = [tile for n in range(0, whole, 4) for tile in squeeze(some[n : n + 4])] + some[whole:]
        for n, tile in enumerate(packed):
            target[n] = tile


def second_down_kernel(tall, first, second, g0, d0, f0, d1, f1, v0, g1, v1, packed, edge, wide, field, field1):
    position = own_position()
    half = tall.shape[1] // 2
    halo = half - v0.shape[1] // 2 + HALO
    rows = 2 * (half - halo)
    low = (lane_index() < LANES // 2) == (position[5] == 0)
    for c in range(C):
        for r in range(2 * half):
            wide[c, r, :, :LANES] = tall[c, r]
    whole = C * half // 4
    sides = []
    for ref in (first, second):
        some = [tile for n in range(whole) for tile in unsqueeze([ref[3 * n + t] for t in range(3)])]
        sides.append(some + [ref[n] for n in range(3 * whole, ref.shape[0])])
    for n, (one, two) in enumerate(zip(*sides)):
        c, r = n // half, n % half
        wide[c, r, :, LANES:] = jnp.where(low, one, two)
        other = jnp.where(low, two, one)
        wide[c, r + half, :, LANES:] = jnp.where(lane_index() < LANES // 2, pltpu.roll(other, 48, 1), pltpu.roll(other, 80, 1))
    g, d, f, a, b = (g0, -HALO), (d0, -HALO), (f0, -HALO), (field, -HALO), (v0, -HALO)
    sweep(a, (wide, -halo), g, f, 0, -6, rows + 6)
    sweep(b, a, g, f, 0, -5, rows + 5)
    coarse_source((g1, -2), b, g, d, 0, 2 * LANES, -2, rows // 2 + 2)
    first_sweep((field1, -2), (g1, -2), (f1, -3), 1, -2, rows // 2 + 2)
    level_one_down(position, (g1, -2), (v1, -2), (field1, -2), (d1, -3), (f1, -3), packed, edge)


def coarse_kernel(mine, other, v1, out, first, second, g2, d2, f2, g3, d3, f3, a, b, a3, b3):
    position = own_position()
    lane = lane_index()
    odd, step = position[4], 1 - 2 * position[6]
    count, reach = first.shape[1], 8
    units = C + 1

    for ref, core in ((mine, odd), (other, 1 - odd)):
        for n, away in enumerate((0, step, -step, 2 * step, -2 * step)):
            at = 4 * away + (2 * core + reach)
            for c in range(units):
                both = ref[n * units + c]
                twin = pltpu.roll(both, LANES // 2, 1)
                for q, value in ((0, jnp.where(lane < LANES // 2, both, twin)), (1, jnp.where(lane < LANES // 2, twin, both))):
                    if c < C:
                        g2[c, at + q] = value
                    else:
                        d2[at + q] = value
    g, d, f, u, w = (g2, -reach), (d2, -reach), (f2, -reach), (a, -reach), (b, -reach)
    h, e, k, s, t = (g3, -reach // 2), (d3, -reach // 2), (f3, -reach // 2), (a3, -reach // 2), (b3, -reach // 2)
    from_zero(u, g, d, f, 2, LANES // 2, 4, position, -8, 12, group=2)
    sweep(w, u, g, f, 2, -7, 11)
    coarse_source(h, w, g, d, 2, LANES // 2, -3, 5)
    from_zero(s, h, e, k, 3, LANES // 4, 2, position, -3, 5, d, group=2)
    sweep(t, s, h, k, 3, -2, 4)
    sweep(s, t, h, k, 3, -1, 3)

    def correct(q):
        for c in range(C):
            fine = spread(row(s, c, q), LANES // 2)
            for r in (q.double(), q.double() + 1):
                b[c, index(w, r)] = row(w, c, r) + fine

    each_row(-1, 3, correct, 4)
    sweep(u, w, g, f, 2, -1, 5)
    sweep(w, u, g, f, 2, 0, 4)
    for c in range(C):
        for q in (0, 1):
            fine = spread(b[c, 2 * odd + (q + reach)], LANES)
            for r in (2 * q, 2 * q + 1):
                out[c, r] = v1[c, r + 2] + fine
        for r, q in enumerate((0, odd, 1)):
            fine = spread(b[c, 2 * (1 - odd) + (reach + q)], LANES)
            first[c, r] = other[5 * units + c * count + r] + fine
        for r in range(count):
            second[c, r] = out[c, odd * (out.shape[1] - count) + r]


def climb(position, own, first, second, g0, f0, v0, g1, f1, wide, u, w, field, emit):
    rows1, halo = own.shape[1], first.shape[1]

    def store(c, at, value):
        wide[c, at] = value

    with_halo(position, own, first, second, store)
    sweep((u, -3), (wide, -halo), (g1, -2), (f1, -3), 1, -2, rows1 + 2, CLIMB[1])
    sweep((w, -3), (u, -3), (g1, -2), (f1, -3), 1, -1, rows1 + 1, CLIMB[1])

    def correct(q):
        for c in range(C):
            fine = spread(row((w, -3), c, q), 2 * LANES)
            for r in (q.double(), q.double() + 1):
                field[c, index((field, -HALO), r)] = row((v0, -HALO), c, r) + fine

    each_row(-1, rows1 + 1, correct, CLIMB[1])
    rows = 2 * rows1
    sweep((emit, -HALO), (field, -HALO), (g0, -HALO), (f0, -HALO), 0, -1, rows + 1, CLIMB[0])
    sweep((field, -HALO), (emit, -HALO), (g0, -HALO), (f0, -HALO), 0, 0, rows, CLIMB[0])


def first_up_kernel(own, left, right, g0, f0, v0, g1, f1, out, first, second, wide, u, w, field, other):
    position = own_position()
    climb(position, own, left, right, g0, f0, v0, g1, f1, wide, u, w, field, other)
    for c in range(C):
        for r in range(out.shape[1]):
            out[c, r] = field[c, r + HALO, :, :LANES]
    rows_to_send(position, out, first, second)


def last_up_kernel(own, left, right, g0, f0, v0, g1, f1, out, wide, u, w, field, other, scratch):
    position = own_position()
    climb(position, own, left, right, g0, f0, v0, g1, f1, wide, u, w, field, other)
    blocks, _, rows, _ = out.shape
    depth = NZ // blocks
    for c in range(C):
        for r in range(rows):
            scratch[c, pl.ds(r, NZ, stride=rows), :] = field[c, r + HALO, :, :LANES]
    for c in range(C):
        for z in range(NZ):
            out[z // depth, c * depth + z % depth] = scratch[c, z * rows : (z + 1) * rows]


def join_kernel(taken, out):
    for b in range(taken.shape[0]):
        out[:, :, b * LANES : (b + 1) * LANES] = taken[b]


def call(kernel, outs, scratch, *args):
    shape = lambda s: jax.ShapeDtypeStruct(s, jnp.float32)
    out = pl.pallas_call(
        kernel,
        out_shape=[shape(s) for s in outs],
        in_specs=[pl.BlockSpec(memory_space=pltpu.VMEM)] * len(args),
        out_specs=[pl.BlockSpec(memory_space=pltpu.VMEM)] * len(outs),
        scratch_shapes=[pltpu.VMEM(s, jnp.float32) for s in scratch],
        compiler_params=PARAMS,
        name=kernel.__name__,
    )(*args)
    return out


def swap(values, axis, first, unit=1):
    count, pairs = lax.axis_size(axis), []
    for i in range(count):
        group = i // unit
        other = group ^ 1 if first else ((group - 1) ^ 1) + 1
        if 0 <= other < count // unit:
            pairs.append((i, other * unit + i % unit))
    return lax.ppermute(values, axis, pairs)


def shards(right_side, density):
    blocks = lax.axis_size("gz")
    depth, rows, columns = density.shape
    W, R0, R1 = 2 * LANES, rows + 2 * HALO, rows // 2

    count = (C + 1) * depth
    (sent,) = call(
        pack_kernel,
        [(blocks, count + 3 * (count // 4), rows, LANES)],
        [],
        right_side.reshape(C * depth, rows, columns),
        density,
    )
    taken = lax.all_to_all(sent, "gz", 0, 0)
    own, first, second = call(
        unpack_kernel,
        [(C + 1, rows, NZ, W)] + [(C + 4, HALO, NZ, LANES)] * 2,
        [(C + 1, 2, NZ * rows, LANES)],
        taken,
    )
    fine, mid = (C, R0, NZ, W), (C, R1 + 4, NZ, LANES)
    sends = [(C + 1, NZ, LANES), (C * (R1 - 1), NZ, LANES)]
    g0, d0, f0, v0, g1, d1, f1, *down = call(
        first_down_kernel,
        [fine, fine[1:], fine[1:], fine, mid, (R1 + 6, NZ, LANES), (R1 + 6, NZ, LANES), mid, *sends],
        [fine, mid],
        own,
        swap(second, "gx", False),
        swap(first, "gx", True),
    )

    def coarse(v1, packed, edge):
        near = [swap(packed, "gx", first, 2) for first in (True, False)]
        far = [swap(near[1], "gx", True, 2), swap(near[0], "gx", False, 2)]
        mine = jnp.concatenate([packed, *near, *far, edge])
        two, three = (C, 20, NZ, LANES), (C, 10, NZ, LANES)
        out, first, second = call(
            coarse_kernel,
            [(C, R1, NZ, LANES)] + [(C, R1 - 1, NZ, LANES)] * 2,
            [two, two[1:], two[1:], three, three[1:], three[1:], two, two, three, three],
                mine,
            swap(mine, "gx", True),
            v1,
        )
        return out, first, swap(second, "gx", False)

    middle = (C, R1 + 6, NZ, LANES)
    reach = HALO + 1
    field, first, second = call(
        first_up_kernel,
        [(C, rows, NZ, LANES), (C, reach, NZ, LANES), (C, reach, NZ, LANES)],
        [middle, middle, middle, fine, fine],
        *coarse(*down),
        g0,
        f0,
        v0,
        g1,
        f1,
    )
    half = (rows + 2 * reach) // 2
    tall, first, second = call(
        side_kernel,
        [(C, 2 * half, NZ, LANES)] + [(C * half - C * half // 4, NZ, LANES)] * 2,
        [],
        field,
        swap(second, "gx", False),
        swap(first, "gx", True),
    )
    v0, g1, *down = call(
        second_down_kernel,
        [fine, mid, mid, *sends],
        [(C, 2 * half, NZ, W), fine, mid],
        tall,
        swap(first, "gz", True),
        swap(second, "gz", False),
        g0,
        d0,
        f0,
        d1,
        f1,
    )
    (sent,) = call(
        last_up_kernel,
        [(blocks, C * depth, rows, LANES)],
        [middle, middle, middle, fine, fine, (C, NZ * rows, LANES)],
        *coarse(*down),
        g0,
        f0,
        v0,
        g1,
        f1,
    )
    (out,) = call(join_kernel, [(C * depth, rows, columns)], [], lax.all_to_all(sent, "gz", 0, 0))
    return out.reshape(right_side.shape)


def solution(mesh):
    return jax.shard_map(
        shards,
        mesh=mesh,
        in_specs=(P(None, "gz", "gx", None), P("gz", "gx", None)),
        out_specs=P(None, "gz", "gx", None),
        check_vma=False,
    )
```

```python
import jax
import jax.numpy as jnp
from jax import lax
from jax.experimental import pallas as pl
from jax.experimental.pallas import tpu as pltpu
from jax.sharding import PartitionSpec as P

relaxation = 0.8
plane_coupling = 16.0
depth_coupling = 1.0
C = 3
NZ = 24
HALO = 6
LANES = 128
UNROLL = (18, 8, 18, 8)
SOURCE = (2, 1, 4, 4)
CLIMB = (10, 8)
PARAMS = pltpu.CompilerParams(vmem_limit_bytes=12 << 20)


def coupling_of(level):
    return plane_coupling / 4.0**level


def base_of(level):
    return 4.0 * coupling_of(level) + 2.0 * depth_coupling


class Row:
    def __init__(self, base, shift):
        self.base, self.shift = base, shift

    def __add__(self, n):
        return Row(self.base, self.shift + n)

    def __sub__(self, n):
        return self + -n

    def double(self):
        return Row(2 * self.base, 2 * self.shift)


def index(field, r):
    return r.base + (r.shift - field[1]) if isinstance(r, Row) else r - field[1]


def row(field, c, r):
    return field[0][c, index(field, r)]


def shared(field, r):
    return field[0][index(field, r)]


def neighbours(field, c, r, level):
    mid = row(field, c, r)
    width = mid.shape[1]
    lateral = row(field, c, r - 1) + row(field, c, r + 1) + pltpu.roll(mid, 1, 1) + pltpu.roll(mid, width - 1, 1)
    vertical = pltpu.roll(mid, 1, 0) + pltpu.roll(mid, NZ - 1, 0)
    return mid, coupling_of(level) * lateral + depth_coupling * vertical


def each_row(low, high, body, unroll):
    steps = (high - low) // unroll

    def step(n, carry):
        for k in range(unroll):
            body(Row(unroll * n, low + k))
        return carry

    if steps > 1:
        lax.fori_loop(0, steps, step, 0)
        low += steps * unroll
    for r in range(low, high):
        body(Row(0, r))


def sweep(target, field, source, factor, level, low, high, unroll=None):
    def body(r):
        f = shared(factor, r)
        for c in range(C):
            mid, around = neighbours(field, c, r, level)
            target[0][c, index(target, r)] = (1.0 - relaxation) * mid + f * (row(source, c, r) + around)

    each_row(low, high, body, unroll or UNROLL[level])


def lane_index():
    return lax.broadcasted_iota(jnp.int32, (NZ, LANES), 1)


def take(values, index):
    return jnp.take_along_axis(values, index, axis=1, mode="promise_in_bounds")


def pair_sum(values, period):
    lane = lane_index()
    if values.shape[1] == 2 * LANES:
        even = (2 * lane) % LANES
        halves = [take(h + pltpu.roll(h, LANES - 1, 1), even) for h in (values[:, :LANES], values[:, LANES:])]
        return jnp.where(lane < LANES // 2, halves[0], halves[1])
    return take(values + pltpu.roll(values, LANES - 1, 1), (2 * lane) % period)


def spread(values, period):
    lane = lane_index()
    if period == 2 * LANES:
        return jnp.concatenate([take(values, lane // 2), take(values, LANES // 2 + lane // 2)], axis=1)
    return take(values, (lane % period) // 2)


def coarse_source(target, field, source, density, level, period, low, high):
    def body(q):
        for c in range(C):
            total = None
            for r in (q.double(), q.double() + 1):
                mid, around = neighbours(field, c, r, level)
                residual = row(source, c, r) + around - (shared(density, r) + base_of(level)) * mid
                total = residual if total is None else total + residual
            target[0][c, index(target, q)] = 0.25 * pair_sum(total, period)

    each_row(low, high, body, SOURCE[level])


def from_zero(target, source, density, factor, level, period, rows, position, low, high, finer=None, reach=0, group=1):
    i, j, count_x, count_y = position[0] // group, position[1], position[2] // group, position[3]
    width = factor[0].shape[-1]
    lane = lax.broadcasted_iota(jnp.int32, (NZ, width), 1) % period
    inside_y = ((lane < 3 * period // 4) | (j > 0)) & ((lane < period // 2) | (lane >= 3 * period // 4) | (j < count_y - 1))

    def body(r):
        if finer is None:
            own = shared(density, r)
        else:
            own = 0.25 * pair_sum(shared(finer, r.double()) + shared(finer, r.double() + 1), 2 * period)
            density[0][index(density, r)] = own
        at = i * rows + r.base
        inside = inside_y & ((at >= -r.shift) & (at < count_x * rows - r.shift))
        f = jnp.where(inside, relaxation / (own + base_of(level)), 0.0)
        factor[0][index(factor, r)] = f
        return f

    def whole(r):
        f = body(r)
        for c in range(C):
            target[0][c, index(target, r)] = f * row(source, c, r)

    for r in [*range(low - reach, low), *range(high, high + reach)]:
        body(Row(0, r))
    each_row(low, high, whole, min(UNROLL[level], 5))


def first_sweep(target, source, factor, level, low, high):
    def body(r):
        f = shared(factor, r)
        for c in range(C):
            target[0][c, index(target, r)] = f * row(source, c, r)

    each_row(low, high, body, UNROLL[level])


def level_one_down(position, g1, v1, scratch, d1, f1, packed, edge):
    sweep(v1, scratch, g1, f1, 1, -1, 5)
    lane = lane_index()
    for c in range(C + 1):
        pair = []
        for q in (0, 1):
            total = None
            for r in (2 * q, 2 * q + 1):
                if c == C:
                    part = shared(d1, r)
                else:
                    mid, around = neighbours(v1, c, r, 1)
                    part = row(g1, c, r) + around - (shared(d1, r) + base_of(1)) * mid
                total = part if total is None else total + part
            pair.append(0.25 * pair_sum(total, LANES))
        packed[c] = jnp.where(lane < LANES // 2, pair[0], pair[1])
    count = edge.shape[0] // C
    for c in range(C):
        for r in range(count):
            edge[c * count + r] = v1[0][c, (1 - position[4]) + (r - v1[1])]


def own_position():
    i, j = lax.axis_index("gx"), lax.axis_index("gz")
    return i, j, lax.axis_size("gx"), lax.axis_size("gz"), i % 2, j % 2, i // 2 % 2


def by_parity(position, body):
    for odd in range(2):
        pl.when(position[4] == odd)(lambda odd=odd: body(odd))


def rows_to_send(position, own, first, second):
    spare = own.shape[1] - first.shape[1]

    def body(odd):
        for c in range(own.shape[0]):
            for r in range(first.shape[1]):
                first[c, r] = own[c, (1 - odd) * spare + r]
                second[c, r] = own[c, odd * spare + r]

    by_parity(position, body)


def with_halo(position, own, first, second, store):
    rows, halo = own.shape[1], first.shape[1]

    def body(odd):
        for c in range(own.shape[0]):
            for piece, at in ((first, (1 - odd) * (halo + rows)), (second, odd * (halo + rows))):
                for r in range(halo):
                    store(c, at + r, piece[c, r])

    for c in range(own.shape[0]):
        for r in range(rows):
            store(c, halo + r, own[c, r])
    by_parity(position, body)


def squeeze(parts):
    lane = lax.broadcasted_iota(jnp.int32, parts[0].shape, 1)
    last = parts[3]
    spare = [pltpu.roll(last, 48, 1), pltpu.roll(last, 80, 1), jnp.where(lane < 64, pltpu.roll(last, 16, 1), pltpu.roll(last, 112, 1))]
    return [jnp.where((lane < 48) | (lane >= 80), parts[t], spare[t]) for t in range(3)]


def unsqueeze(tiles):
    lane = lax.broadcasted_iota(jnp.int32, tiles[0].shape, 1)
    low = jnp.where(lane < 32, pltpu.roll(tiles[0], 80, 1), pltpu.roll(tiles[2], 112, 1))
    high = jnp.where(lane < 96, pltpu.roll(tiles[2], 16, 1), pltpu.roll(tiles[1], 48, 1))
    return [*tiles, jnp.where(lane < 48, low, jnp.where(lane < 80, 1.0, high))]


def pack_kernel(source, density, out):
    blocks, n = out.shape[0], source.shape[0]
    count = n + density.shape[0]

    def block(m, b):
        ref, at = (source, m) if m < n else (density, m - n)
        return ref[at, :, b * LANES : (b + 1) * LANES]

    zero = jnp.zeros((out.shape[2], LANES), jnp.float32)
    lane = lax.broadcasted_iota(jnp.int32, zero.shape, 1)
    for k in range(count // 4):
        for b in range(blocks):
            halos = []
            for m in range(4 * k, 4 * k + 4):
                out[b, m] = block(m, b)
                after = block(m, b + 1) if b + 1 < blocks else zero
                before = block(m, b - 1) if b else zero
                halos.append(jnp.where(lane < LANES // 2, after, before))
            for t, tile in enumerate(squeeze(halos)):
                out[b, count + 3 * k + t] = tile


def unpack_kernel(taken, own, first, second, scratch):
    position = own_position()
    blocks, _, rows, _ = taken.shape
    depth = NZ // blocks
    count = (C + 1) * depth
    for b in range(blocks):
        for k in range(count // 4):
            halos = unsqueeze([taken[b, count + 3 * k + t] for t in range(3)])
            for m in range(4 * k, 4 * k + 4):
                at = (b * depth + m % depth) * rows
                scratch[m // depth, 0, at : at + rows] = taken[b, m]
                scratch[m // depth, 1, at : at + rows] = halos[m - 4 * k]
    for c in range(C + 1):
        for r in range(rows):
            for h in range(2):
                own[c, r, :, h * LANES : (h + 1) * LANES] = scratch[c, h, pl.ds(r, NZ, stride=rows), :]
    spare = rows - HALO

    def send(odd):
        for target, start in ((first, (1 - odd) * spare), (second, odd * spare)):
            for r in range(HALO):
                for c in range(C + 1):
                    target[c, r] = own[c, start + r, :, :LANES]
                for t, tile in enumerate(squeeze([own[c, start + r, :, LANES:] for c in range(C + 1)])):
                    target[C + 1 + t, r] = tile

    by_parity(position, send)


def first_down_kernel(own, second, first, g0, d0, f0, v0, g1, d1, f1, v1, packed, edge, field, field1):
    position = own_position()
    rows = own.shape[1]

    def store(c, at, value):
        if c < C:
            g0[c, at] = value
        else:
            d0[at] = value

    for c in range(C + 1):
        for r in range(rows):
            store(c, HALO + r, own[c, r])

    def receive(odd):
        for piece, at in ((first, (1 - odd) * (HALO + rows)), (second, odd * (HALO + rows))):
            for r in range(HALO):
                halos = unsqueeze([piece[C + 1 + t, r] for t in range(3)])
                for c in range(C + 1):
                    store(c, at + r, jnp.concatenate([piece[c, r], halos[c]], axis=1))

    by_parity(position, receive)
    g, d, f, a, b = (g0, -HALO), (d0, -HALO), (f0, -HALO), (field, -HALO), (v0, -HALO)
    from_zero(a, g, d, f, 0, 2 * LANES, rows, position, -HALO, rows + HALO)
    sweep(b, a, g, f, 0, -5, rows + 5)
    coarse_source((g1, -2), b, g, d, 0, 2 * LANES, -2, rows // 2 + 2)
    from_zero((field1, -2), (g1, -2), (d1, -3), (f1, -3), 1, LANES, rows // 2, position, -2, rows // 2 + 2, d, 1)
    level_one_down(position, (g1, -2), (v1, -2), (field1, -2), (d1, -3), (f1, -3), packed, edge)


def side_kernel(own, second, first, tall, to_first, to_second):
    position = own_position()
    half = tall.shape[1] // 2
    low = (lane_index() < LANES // 2) == (position[5] == 1)

    def store(c, at, value):
        tall[c, at] = value

    with_halo(position, own, first, second, store)
    tiles = ([], [])
    for n in range(C * half):
        one, other = tall[n // half, n % half], tall[n // half, n % half + half]
        two = jnp.where(lane_index() < LANES // 2, pltpu.roll(other, 48, 1), pltpu.roll(other, 80, 1))
        tiles[0].append(jnp.where(low, one, two))
        tiles[1].append(jnp.where(low, two, one))
    for target, some in ((to_first, tiles[0]), (to_second, tiles[1])):
        whole = len(some) // 4 * 4
        packed = [tile for n in range(0, whole, 4) for tile in squeeze(some[n : n + 4])] + some[whole:]
        for n, tile in enumerate(packed):
            target[n] = tile


def second_down_kernel(tall, first, second, g0, d0, f0, d1, f1, v0, g1, v1, packed, edge, wide, field, field1):
    position = own_position()
    half = tall.shape[1] // 2
    halo = half - v0.shape[1] // 2 + HALO
    rows = 2 * (half - halo)
    low = (lane_index() < LANES // 2) == (position[5] == 0)
    for c in range(C):
        for r in range(2 * half):
            wide[c, r, :, :LANES] = tall[c, r]
    whole = C * half // 4
    sides = []
    for ref in (first, second):
        some = [tile for n in range(whole) for tile in unsqueeze([ref[3 * n + t] for t in range(3)])]
        sides.append(some + [ref[n] for n in range(3 * whole, ref.shape[0])])
    for n, (one, two) in enumerate(zip(*sides)):
        c, r = n // half, n % half
        wide[c, r, :, LANES:] = jnp.where(low, one, two)
        other = jnp.where(low, two, one)
        wide[c, r + half, :, LANES:] = jnp.where(lane_index() < LANES // 2, pltpu.roll(other, 48, 1), pltpu.roll(other, 80, 1))
    g, d, f, a, b = (g0, -HALO), (d0, -HALO), (f0, -HALO), (field, -HALO), (v0, -HALO)
    sweep(a, (wide, -halo), g, f, 0, -6, rows + 6)
    sweep(b, a, g, f, 0, -5, rows + 5)
    coarse_source((g1, -2), b, g, d, 0, 2 * LANES, -2, rows // 2 + 2)
    first_sweep((field1, -2), (g1, -2), (f1, -3), 1, -2, rows // 2 + 2)
    level_one_down(position, (g1, -2), (v1, -2), (field1, -2), (d1, -3), (f1, -3), packed, edge)


def coarse_kernel(mine, other, v1, out, first, second, g2, d2, f2, g3, d3, f3, a, b, a3, b3):
    position = own_position()
    lane = lane_index()
    odd, step = position[4], 1 - 2 * position[6]
    count, reach = first.shape[1], 8
    units = C + 1

    for ref, core in ((mine, odd), (other, 1 - odd)):
        for n, away in enumerate((0, step, -step, 2 * step, -2 * step)):
            at = 4 * away + (2 * core + reach)
            for c in range(units):
                both = ref[n * units + c]
                twin = pltpu.roll(both, LANES // 2, 1)
                for q, value in ((0, jnp.where(lane < LANES // 2, both, twin)), (1, jnp.where(lane < LANES // 2, twin, both))):
                    if c < C:
                        g2[c, at + q] = value
                    else:
                        d2[at + q] = value
    g, d, f, u, w = (g2, -reach), (d2, -reach), (f2, -reach), (a, -reach), (b, -reach)
    h, e, k, s, t = (g3, -reach // 2), (d3, -reach // 2), (f3, -reach // 2), (a3, -reach // 2), (b3, -reach // 2)
    from_zero(u, g, d, f, 2, LANES // 2, 4, position, -8, 12, group=2)
    sweep(w, u, g, f, 2, -7, 11)
    coarse_source(h, w, g, d, 2, LANES // 2, -3, 5)
    from_zero(s, h, e, k, 3, LANES // 4, 2, position, -3, 5, d, group=2)
    sweep(t, s, h, k, 3, -2, 4)
    sweep(s, t, h, k, 3, -1, 3)

    def correct(q):
        for c in range(C):
            fine = spread(row(s, c, q), LANES // 2)
            for r in (q.double(), q.double() + 1):
                b[c, index(w, r)] = row(w, c, r) + fine

    each_row(-1, 3, correct, 4)
    sweep(u, w, g, f, 2, -1, 5)
    sweep(w, u, g, f, 2, 0, 4)
    for c in range(C):
        for q in (0, 1):
            fine = spread(b[c, 2 * odd + (q + reach)], LANES)
            for r in (2 * q, 2 * q + 1):
                out[c, r] = v1[c, r + 2] + fine
        for r, q in enumerate((0, odd, 1)):
            fine = spread(b[c, 2 * (1 - odd) + (reach + q)], LANES)
            first[c, r] = other[5 * units + c * count + r] + fine
        for r in range(count):
            second[c, r] = out[c, odd * (out.shape[1] - count) + r]


def climb(position, own, first, second, g0, f0, v0, g1, f1, wide, u, w, field, emit):
    rows1, halo = own.shape[1], first.shape[1]

    def store(c, at, value):
        wide[c, at] = value

    with_halo(position, own, first, second, store)
    sweep((u, -3), (wide, -halo), (g1, -2), (f1, -3), 1, -2, rows1 + 2, CLIMB[1])
    sweep((w, -3), (u, -3), (g1, -2), (f1, -3), 1, -1, rows1 + 1, CLIMB[1])

    def correct(q):
        for c in range(C):
            fine = spread(row((w, -3), c, q), 2 * LANES)
            for r in (q.double(), q.double() + 1):
                field[c, index((field, -HALO), r)] = row((v0, -HALO), c, r) + fine

    each_row(-1, rows1 + 1, correct, CLIMB[1])
    rows = 2 * rows1
    sweep((emit, -HALO), (field, -HALO), (g0, -HALO), (f0, -HALO), 0, -1, rows + 1, CLIMB[0])
    sweep((field, -HALO), (emit, -HALO), (g0, -HALO), (f0, -HALO), 0, 0, rows, CLIMB[0])


def first_up_kernel(own, left, right, g0, f0, v0, g1, f1, out, first, second, wide, u, w, field, other):
    position = own_position()
    climb(position, own, left, right, g0, f0, v0, g1, f1, wide, u, w, field, other)
    for c in range(C):
        for r in range(out.shape[1]):
            out[c, r] = field[c, r + HALO, :, :LANES]
    rows_to_send(position, out, first, second)


def last_up_kernel(own, left, right, g0, f0, v0, g1, f1, out, wide, u, w, field, other, scratch):
    position = own_position()
    climb(position, own, left, right, g0, f0, v0, g1, f1, wide, u, w, field, other)
    blocks, _, rows, _ = out.shape
    depth = NZ // blocks
    for c in range(C):
        for r in range(rows):
            scratch[c, pl.ds(r, NZ, stride=rows), :] = field[c, r + HALO, :, :LANES]
    for c in range(C):
        for z in range(NZ):
            out[z // depth, c * depth + z % depth] = scratch[c, z * rows : (z + 1) * rows]


def join_kernel(taken, out):
    for b in range(taken.shape[0]):
        out[:, :, b * LANES : (b + 1) * LANES] = taken[b]


def call(kernel, outs, scratch, *args):
    shape = lambda s: jax.ShapeDtypeStruct(s, jnp.float32)
    out = pl.pallas_call(
        kernel,
        out_shape=[shape(s) for s in outs],
        in_specs=[pl.BlockSpec(memory_space=pltpu.VMEM)] * len(args),
        out_specs=[pl.BlockSpec(memory_space=pltpu.VMEM)] * len(outs),
        scratch_shapes=[pltpu.VMEM(s, jnp.float32) for s in scratch],
        compiler_params=PARAMS,
        name=kernel.__name__,
    )(*args)
    return out


def swap(values, axis, first, unit=1):
    count, pairs = lax.axis_size(axis), []
    for i in range(count):
        group = i // unit
        other = group ^ 1 if first else ((group - 1) ^ 1) + 1
        if 0 <= other < count // unit:
            pairs.append((i, other * unit + i % unit))
    return lax.ppermute(values, axis, pairs)


def shards(right_side, density):
    blocks = lax.axis_size("gz")
    depth, rows, columns = density.shape
    W, R0, R1 = 2 * LANES, rows + 2 * HALO, rows // 2

    count = (C + 1) * depth
    (sent,) = call(
        pack_kernel,
        [(blocks, count + 3 * (count // 4), rows, LANES)],
        [],
        right_side.reshape(C * depth, rows, columns),
        density,
    )
    taken = lax.all_to_all(sent, "gz", 0, 0)
    own, first, second = call(
        unpack_kernel,
        [(C + 1, rows, NZ, W)] + [(C + 4, HALO, NZ, LANES)] * 2,
        [(C + 1, 2, NZ * rows, LANES)],
        taken,
    )
    fine, mid = (C, R0, NZ, W), (C, R1 + 4, NZ, LANES)
    sends = [(C + 1, NZ, LANES), (C * (R1 - 1), NZ, LANES)]
    g0, d0, f0, v0, g1, d1, f1, *down = call(
        first_down_kernel,
        [fine, fine[1:], fine[1:], fine, mid, (R1 + 6, NZ, LANES), (R1 + 6, NZ, LANES), mid, *sends],
        [fine, mid],
        own,
        swap(second, "gx", False),
        swap(first, "gx", True),
    )

    def coarse(v1, packed, edge):
        near = [swap(packed, "gx", first, 2) for first in (True, False)]
        far = [swap(near[1], "gx", True, 2), swap(near[0], "gx", False, 2)]
        mine = jnp.concatenate([packed, *near, *far, edge])
        two, three = (C, 20, NZ, LANES), (C, 10, NZ, LANES)
        out, first, second = call(
            coarse_kernel,
            [(C, R1, NZ, LANES)] + [(C, R1 - 1, NZ, LANES)] * 2,
            [two, two[1:], two[1:], three, three[1:], three[1:], two, two, three, three],
                mine,
            swap(mine, "gx", True),
            v1,
        )
        return out, first, swap(second, "gx", False)

    middle = (C, R1 + 6, NZ, LANES)
    reach = HALO + 1
    field, first, second = call(
        first_up_kernel,
        [(C, rows, NZ, LANES), (C, reach, NZ, LANES), (C, reach, NZ, LANES)],
        [middle, middle, middle, fine, fine],
        *coarse(*down),
        g0,
        f0,
        v0,
        g1,
        f1,
    )
    half = (rows + 2 * reach) // 2
    tall, first, second = call(
        side_kernel,
        [(C, 2 * half, NZ, LANES)] + [(C * half - C * half // 4, NZ, LANES)] * 2,
        [],
        field,
        swap(second, "gx", False),
        swap(first, "gx", True),
    )
    v0, g1, *down = call(
        second_down_kernel,
        [fine, mid, mid, *sends],
        [(C, 2 * half, NZ, W), fine, mid],
        tall,
        swap(first, "gz", True),
        swap(second, "gz", False),
        g0,
        d0,
        f0,
        d1,
        f1,
    )
    (sent,) = call(
        last_up_kernel,
        [(blocks, C * depth, rows, LANES)],
        [middle, middle, middle, fine, fine, (C, NZ * rows, LANES)],
        *coarse(*down),
        g0,
        f0,
        v0,
        g1,
        f1,
    )
    (out,) = call(join_kernel, [(C * depth, rows, columns)], [], lax.all_to_all(sent, "gz", 0, 0))
    return out.reshape(right_side.shape)


def solution(mesh):
    return jax.shard_map(
        shards,
        mesh=mesh,
        in_specs=(P(None, "gz", "gx", None), P("gz", "gx", None)),
        out_specs=P(None, "gz", "gx", None),
        check_vma=False,
    )
```
